32 devices in a mesh: dom: 8 (over z, y), near: 4 (over x, core).
Axes of the slice: x: 2, y: 2, z: 4, core: 2. Of those that a mesh axis runs over, the one named last changes fastest.
Arguments:
- solution: float32 [56, 9, 4096], P(None, None, ('dom', 'near')), may hold values from -6 to 6
- star_matrices: float32 [3, 9, 9, 4096], P(None, None, None, ('dom', 'near')), may hold values from -2.5 to 2.5
- flux_plus: float32 [4, 9, 9, 4096], P(None, None, None, ('dom', 'near')), may hold values from -1.2 to 1.2
- flux_minus: float32 [4, 9, 9, 4096], P(None, None, None, ('dom', 'near')), may hold values from -1.2 to 1.2
- stiffness: float32 [3, 56, 56], replicated, may hold values from -0.75 to 0.75
- face_lift: float32 [4, 56, 21], replicated, may hold values from -0.625 to 0.625
- face_project: float32 [4, 21, 56], replicated, may hold values from -0.75 to 0.75
- cluster: int32 [4096], P(('dom', 'near')), may hold values from 0 to 1, as said below
- neighbour_part: int32 [4, 4096], P(None, ('dom', 'near')), may hold values from 0 to 4, as said below
- neighbour_slot: int32 [4, 4096], P(None, ('dom', 'near')), may hold values from 0 to 127, as said below
- neighbour_face: int32 [4, 4096], P(None, ('dom', 'near')), may hold values from 0 to 3
- orientation: int32 [4, 4096], P(None, ('dom', 'near')), may hold values from 0 to 2
- halo_send: int32 [4, 512], P(None, ('dom', 'near')), may hold values from 0 to 127, as said below
Outputs:
- updated: float32 [56, 9, 4096], P(None, None, ('dom', 'near'))
The draws below stay inside these ranges and needn't reach their ends.
Inputs may be any that keep to these rules, and one draw needn't show every extreme that they name: 0 marks an element that takes two half steps, 1 one that takes one step of length one. A partition holds at most 64 elements of cluster 0, and some partition exactly that many. `neighbour_part`: 0: the neighbour lies in the element's own partition; 1 to 4: it comes from the partition at near -1, near +1, dom -1, dom +1 (cyclic). In each partition each pair of a part p of 1 to 4 and a slot below 16 is named by exactly one face. `neighbour_slot`: an element of the own partition where the part is 0, a slot below 16 otherwise. `halo_send`: row r of a partition lists the elements it sends to the partition at near +1, near -1, dom +1, dom -1 for r = 0, 1, 2, 3; the 16 entries of a row are distinct.
All inputs are finite; a program needn't handle non-finite values.
Results may differ from the reference program's by a relative error of at most 0.0003.
Values sent between devices are 32-bit elements; how exact they have to be, the bound alone decides.
No kernel may reach another device: no remote copies, remote signals or barrier semaphores. Data moves between devices by JAX's collectives and lax.ppermute only.
A program may use at most 128 MiB of HBM per device.

```python
import math
import jax
import jax.numpy as jnp
import numpy as np
from jax import lax

MODES = 56
FIELDS = 9
FACE_MODES = 21
ORDER = 6
E_DEV = 128
HALO = 16
SMALL_MAX = 64
NE = 4096
N_DOM = 8
N_NEAR = 4


def draw_cluster(key, part):
    partitions = NE // E_DEV
    count_key, top_key, order_key = jax.random.split(key, 3)
    counts = jax.random.randint(count_key, (partitions,), 1, SMALL_MAX + 1)
    busiest = jax.random.randint(top_key, (), 0, partitions)
    counts = jnp.where(jnp.arange(partitions) == busiest, SMALL_MAX, counts)
    orders = jax.vmap(lambda subkey: jax.random.permutation(subkey, E_DEV))(jax.random.split(order_key, partitions))
    return jnp.where(orders < counts[:, None], 0, 1).astype(jnp.int32).reshape(NE)


def neighbour_tables(key):
    partitions = NE // E_DEV
    face_count = 4 * E_DEV
    order_key, slot_key = jax.random.split(key)
    orders = jax.vmap(lambda subkey: jax.random.permutation(subkey, face_count))(jax.random.split(order_key, partitions))
    ranks = jax.vmap(lambda permuted: jnp.zeros(face_count, jnp.int32).at[permuted].set(jnp.arange(face_count, dtype=jnp.int32)))(orders)
    halo_faces = ranks < 4 * HALO
    local_slots = jax.random.randint(slot_key, (partitions, face_count), 0, E_DEV)
    parts = jnp.where(halo_faces, 1 + ranks // HALO, 0)
    slots = jnp.where(halo_faces, ranks % HALO, local_slots)
    parts = jnp.transpose(parts.reshape(partitions, 4, E_DEV), (1, 0, 2)).reshape(4, NE)
    slots = jnp.transpose(slots.reshape(partitions, 4, E_DEV), (1, 0, 2)).reshape(4, NE)
    return (parts.astype(jnp.int32), slots.astype(jnp.int32))


def draw_neighbour_part(key, part):
    return neighbour_tables(jax.random.fold_in(key, 11))[0]


def draw_neighbour_slot(key, part):
    return neighbour_tables(jax.random.fold_in(key, 11))[1]


def draw_halo_send(key, part):
    partitions = NE // E_DEV
    subkeys = jax.random.split(jax.random.fold_in(key, 23), partitions * 4)
    lists = jax.vmap(lambda subkey: jax.random.permutation(subkey, E_DEV)[:HALO])(subkeys).reshape(partitions, 4, HALO)
    return jnp.transpose(lists, (1, 0, 2)).reshape(4, partitions * HALO).astype(jnp.int32)


def with_ends(result, key, low, high):
    longest = result.shape.index(max(result.shape))
    spots = []
    for shift in (0, 1):
        where = [jax.random.randint(jax.random.fold_in(key, axis), (), 0, length) for axis, length in enumerate(result.shape)]
        where[longest] = (where[longest] + shift) % result.shape[longest]
        spots.append(tuple(where))
    return result.at[spots[0]].set(low).at[spots[1]].set(high)


def block_levels(own_key, shape, cuts, low, top_value):
    def one(position, shards_of):
        heights = jax.random.uniform(jax.random.fold_in(jax.random.fold_in(own_key, 6), position), (shards_of,), jnp.float32, low / len(cuts), top_value / len(cuts))
        return jnp.repeat(jnp.exp(heights), shape[position] // shards_of).reshape((-1,) + (1,) * (len(shape) - position - 1))

    gain = one(*cuts[0])
    for cut in cuts[1:]:
        gain = gain * one(*cut)
    return gain


def noise(key, extent, width, limit, pieces=(), kind=jnp.bfloat16):
    entries = jax.random.normal(key, extent, jnp.float32) * width
    if len(pieces) > 0:
        entries = block_levels(key, extent, pieces, -0.22, 0.18) * entries
    return jnp.clip(entries, min=-limit, max=limit).astype(kind)


def setup_inputs(seed: int = 0) -> dict:
    keys = jax.random.split(jax.random.key(seed), 14)
    solution = noise(keys[0], (MODES, FIELDS, NE), 1.0, 6.0, ((2, 32),), jnp.float32)
    star_matrices = noise(keys[1], (3, FIELDS, FIELDS, NE), 0.45, 2.5, ((3, 32),), jnp.float32)
    flux_plus = noise(keys[2], (4, FIELDS, FIELDS, NE), 0.2, 1.2, ((3, 32),), jnp.float32)
    flux_minus = noise(keys[3], (4, FIELDS, FIELDS, NE), 0.2, 1.2, ((3, 32),), jnp.float32)
    stiffness = noise(keys[4], (3, MODES, MODES), MODES ** -0.5, 0.75, (), jnp.float32)
    face_lift = noise(keys[5], (4, MODES, FACE_MODES), (4 * FACE_MODES) ** -0.5, 0.625, (), jnp.float32)
    face_project = noise(keys[6], (4, FACE_MODES, MODES), MODES ** -0.5, 0.75, (), jnp.float32)
    cluster = draw_cluster(jax.random.fold_in(keys[13], 71), 0)
    neighbour_part = draw_neighbour_part(jax.random.fold_in(keys[13], 71), 0)
    neighbour_slot = draw_neighbour_slot(jax.random.fold_in(keys[13], 71), 0)
    neighbour_face = with_ends(jax.random.randint(keys[10], (4, NE), 0, 4), jax.random.fold_in(keys[10], 1), 0, 3).astype(jnp.int32)
    orientation = with_ends(jax.random.randint(keys[11], (4, NE), 0, 3), jax.random.fold_in(keys[11], 1), 0, 2).astype(jnp.int32)
    halo_send = draw_halo_send(jax.random.fold_in(keys[13], 71), 0)
    return dict(solution=solution, star_matrices=star_matrices, flux_plus=flux_plus, flux_minus=flux_minus, stiffness=stiffness, face_lift=face_lift, face_project=face_project, cluster=cluster, neighbour_part=neighbour_part, neighbour_slot=neighbour_slot, neighbour_face=neighbour_face, orientation=orientation, halo_send=halo_send)


precise = lax.Precision.HIGHEST


def rotations():
    degree = ORDER - 1
    node_list = [(a, b) for a in range(degree + 1) for b in range(degree + 1 - a)]
    lookup = {point_ab: number for number, point_ab in enumerate(node_list)}
    tables = []
    for rotation in range(3):
        table_row = []
        for point_ab in node_list:
            triple = (point_ab[0], point_ab[1], degree - point_ab[0] - point_ab[1])
            rolled = triple[rotation:] + triple[:rotation]
            table_row.append(lookup[(rolled[0], rolled[1])])
        tables.append(table_row)
    return np.array(tables, dtype=np.int32)


def integral_weights(begin_time, end_time):
    return [(end_time ** (exponent + 1) - begin_time ** (exponent + 1)) / math.factorial(exponent + 1) for exponent in range(ORDER)]


def star_apply(field, star_matrices):
    return jnp.einsum("mfe,dfge->dmge", field, star_matrices, precision=precise)


def taylor_stack(initial, star_matrices, stiffness):
    elements = initial.shape[2]
    forward = jnp.transpose(stiffness, (1, 0, 2)).reshape(MODES, 3 * MODES)
    layers = [initial]
    for exponent in range(ORDER - 1):
        starred = star_apply(layers[-1], star_matrices).reshape(3 * MODES, FIELDS * elements)
        layers.append(jnp.dot(forward, starred, precision=precise).reshape(MODES, FIELDS, elements))
    return layers


def time_integral(layers, begin_time, end_time):
    weights = integral_weights(begin_time, end_time)
    summed = weights[0] * layers[0]
    for exponent in range(1, ORDER):
        summed = summed + weights[exponent] * layers[exponent]
    return summed


def volume_term(integral, star_matrices, stiffness):
    elements = integral.shape[2]
    backward = jnp.transpose(stiffness, (2, 0, 1)).reshape(MODES, 3 * MODES)
    starred = star_apply(integral, star_matrices).reshape(3 * MODES, FIELDS * elements)
    return jnp.dot(backward, starred, precision=precise).reshape(MODES, FIELDS, elements)


def element_update(base_state, integral, gathered, star_matrices, stiffness, flux_plus, flux_minus, face_lift, face_project):
    elements = integral.shape[2]
    projected = jnp.dot(face_project.reshape(4 * FACE_MODES, MODES), integral.reshape(MODES, FIELDS * elements), precision=precise).reshape(4, FACE_MODES, FIELDS, elements)
    inside = jnp.einsum("ipfe,ifge->ipge", projected, flux_plus, precision=precise)
    outside = jnp.einsum("ipfe,ifge->ipge", gathered, flux_minus, precision=precise)
    lifting = jnp.transpose(face_lift, (1, 0, 2)).reshape(MODES, 4 * FACE_MODES)
    lifted = jnp.dot(lifting, (inside + outside).reshape(4 * FACE_MODES, FIELDS * elements), precision=precise).reshape(MODES, FIELDS, elements)
    return base_state + volume_term(integral, star_matrices, stiffness) - lifted


def reference(solution, star_matrices, flux_plus, flux_minus, stiffness, face_lift, face_project, cluster, neighbour_part, neighbour_slot, neighbour_face, orientation, halo_send):
    blocks = NE // E_DEV
    block_ids = jnp.arange(blocks, dtype=jnp.int32)
    combined = face_project[:, rotations(), :].reshape(12, FACE_MODES, MODES)

    def cut(array, block):
        return lax.dynamic_slice_in_dim(array, block * E_DEV, E_DEV, array.ndim - 1)

    def spread(stacked):
        return jnp.transpose(stacked, (1, 2, 0, 3)).reshape(MODES, FIELDS, NE)

    def global_sources(block):
        parts = cut(neighbour_part, block)
        slots = cut(neighbour_slot, block)
        row_pos = block // N_NEAR
        col_pos = block % N_NEAR
        senders = jnp.stack([row_pos * N_NEAR + (col_pos - 1) % N_NEAR, row_pos * N_NEAR + (col_pos + 1) % N_NEAR, ((row_pos - 1) % N_DOM) * N_NEAR + col_pos, ((row_pos + 1) % N_DOM) * N_NEAR + col_pos]).astype(jnp.int32)
        direction = jnp.clip(parts - 1, 0, 3)
        sender = senders[direction]
        sent = halo_send[direction, sender * HALO + jnp.minimum(slots, HALO - 1)]
        return jnp.where(parts == 0, block * E_DEV + slots, sender * E_DEV + sent).astype(jnp.int32)

    def gathered_faces(buffer, block):
        source_ids = global_sources(block)
        source_data = jnp.take(buffer, source_ids, axis=2)
        choose = cut(neighbour_face, block) * 3 + cut(orientation, block)
        selected = jnp.take(combined, choose, axis=0)
        return jnp.einsum("iepm,mfie->ipfe", selected, source_data, precision=precise)

    def matrices(block):
        return (cut(star_matrices, block), stiffness, cut(flux_plus, block), cut(flux_minus, block), face_lift, face_project)

    def section_one(block):
        layers = taylor_stack(cut(solution, block), cut(star_matrices, block), stiffness)
        return (time_integral(layers, 0.0, 0.5), time_integral(layers, 0.5, 1.0), time_integral(layers, 0.0, 1.0))

    first_half, second_half, whole_step = [spread(stacked) for stacked in lax.map(section_one, block_ids)]

    def section_two(block):
        base_state = cut(solution, block)
        is_small = (cut(cluster, block) == 0)[None, None, :]
        moved = element_update(base_state, cut(first_half, block), gathered_faces(first_half, block), *matrices(block))
        middle = jnp.where(is_small, moved, base_state)
        layers = taylor_stack(middle, cut(star_matrices, block), stiffness)
        later = jnp.where(is_small, time_integral(layers, 0.0, 0.5), cut(second_half, block))
        return (middle, later)

    middle_state, later_half = [spread(stacked) for stacked in lax.map(section_two, block_ids)]
    summed = first_half + later_half

    def section_three(block):
        is_small = (cut(cluster, block) == 0)[None, None, :]
        small_new = element_update(cut(middle_state, block), cut(later_half, block), gathered_faces(later_half, block), *matrices(block))
        large_new = element_update(cut(solution, block), cut(whole_step, block), gathered_faces(summed, block), *matrices(block))
        return jnp.where(is_small, small_new, large_new)

    return spread(lax.map(section_three, block_ids))
```

```python
import functools
import math

import jax
import jax.numpy as jnp
import numpy as np
from jax import lax
from jax.experimental import pallas as pl
from jax.experimental.pallas import tpu as pltpu
from jax.sharding import PartitionSpec as P

MODES = 56
FIELDS = 9
NODES = 21
ORDER = 6
MPAD = 64
NPAD = 24
LANES = 128
FACES = 4 * NPAD
BF = jnp.bfloat16
F32 = jnp.float32


def rotations():
    degree = ORDER - 1
    nodes = [(a, b) for a in range(degree + 1) for b in range(degree + 1 - a)]
    lookup = {point: number for number, point in enumerate(nodes)}
    tables = []
    for rotation in range(3):
        row = []
        for a, b in nodes:
            triple = (a, b, degree - a - b)
            rolled = triple[rotation:] + triple[:rotation]
            row.append(lookup[rolled[0], rolled[1]])
        tables.append(row)
    return np.array(tables, dtype=np.int32)


def integral_weights(begin, end):
    return [(end ** (k + 1) - begin ** (k + 1)) / math.factorial(k + 1) for k in range(ORDER)]


def two_parts(x):
    high = x.astype(BF)
    low = (x - high.astype(F32)).astype(BF)
    return high, low


def outer_parts(x):
    high = lax.reduce_precision(x, 8, 7)
    return high, x - high


def field_lanes(f):
    return slice(f * LANES, (f + 1) * LANES)


def field_rows(f):
    return slice(f * MODES, (f + 1) * MODES)


def put_operand(xs_ref, f, x):
    x = jnp.concatenate([x, jnp.zeros((MPAD - MODES, LANES), F32)], axis=0)
    high, low = two_parts(x)
    lanes = field_lanes(f)
    xs_ref[0:MPAD, lanes] = high
    xs_ref[MPAD : 2 * MPAD, lanes] = low
    xs_ref[2 * MPAD : 3 * MPAD, lanes] = high


def big_dot(lhs, rhs):
    return jnp.dot(lhs, rhs, preferred_element_type=F32)


def wide_dot(lhs, xs_ref, y_ref):
    rows = lhs.shape[0]
    for f in range(0, FIELDS, 2):
        lanes = slice(f * LANES, min(f + 2, FIELDS) * LANES)
        y_ref[0:rows, lanes] = big_dot(lhs, xs_ref[:, lanes])


def star_sum(y_ref, star_ref, emit):
    for first in range(0, FIELDS, 3):
        sums = [None] * 3
        for d in range(3):
            for f in range(FIELDS):
                y = y_ref[d * MODES : (d + 1) * MODES, field_lanes(f)]
                for k in range(3):
                    scale = star_ref[d, f, first + k : first + k + 1, :]
                    term = y * scale
                    sums[k] = term if sums[k] is None else sums[k] + term
        for k in range(3):
            emit(first + k, sums[k])


def taylor(start_of, star_ref, forward, xs_ref, y_ref, integrals):
    for f in range(FIELDS):
        value = start_of(f)
        put_operand(xs_ref, f, value)
        for ref, weights in integrals:
            ref[field_rows(f), :] = weights[0] * value
    for k in range(1, ORDER):
        wide_dot(forward, xs_ref, y_ref)

        def emit(g, value, k=k):
            if k < ORDER - 1:
                put_operand(xs_ref, g, value)
            for ref, weights in integrals:
                ref[field_rows(g), :] = ref[field_rows(g), :] + weights[k] * value

        star_sum(y_ref, star_ref, emit)


def send_rims(xs_ref, halo_ref, sends):
    width = halo_ref.shape[1]
    element = lax.broadcasted_iota(jnp.int32, (LANES, width), 0)
    picks = []
    for r in range(4):
        pick = jnp.where(element == halo_ref[r : r + 1, :], 1.0, 0.0).astype(F32)
        picks.append(jnp.transpose(pick))
    pick = jnp.concatenate(picks, axis=0).astype(BF)
    for q in range((FIELDS + 1) // 2):
        if 2 * q + 1 < FIELDS:
            fields = (2 * q, 2 * q + 1)
        else:
            fields = (2 * q, 2 * q)
        total = None
        for piece in range(2):
            rows = slice(piece * MPAD, (piece + 1) * MPAD)
            both = jnp.concatenate([xs_ref[rows, field_lanes(f)] for f in fields], axis=0)
            part = lax.dot_general(
                pick, both, (((1,), (1,)), ((), ())), preferred_element_type=F32
            )
            total = part if total is None else total + part
        for r in range(4):
            sends[r][:, field_lanes(q)] = total[r * width : (r + 1) * width, :]


def local_pick(part, slot, face):
    target = jnp.where(part == 0, face * LANES + slot, -1)
    target = jnp.concatenate([target[i : i + 1, :] for i in range(4)], axis=1)
    row = lax.broadcasted_iota(jnp.int32, (4 * LANES, 4 * LANES), 0)
    return jnp.where(row == target, 1.0, 0.0).astype(BF)


def remote_pick(part, slot, width):
    target = jnp.where(part > 0, (part - 1) * width + slot, -1)
    target = jnp.concatenate([target[i : i + 1, :] for i in range(4)], axis=1)
    row = lax.broadcasted_iota(jnp.int32, (4 * width, 4 * LANES), 0)
    return jnp.where(row == target, 1.0, 0.0).astype(BF)


def pick_faces(y_ref, base_row, table_ref, pick):
    for f in range(FIELDS):
        for j in range(4):
            table_ref[f * NPAD : (f + 1) * NPAD, j * LANES : (j + 1) * LANES] = y_ref[
                base_row + j * NPAD : base_row + (j + 1) * NPAD, field_lanes(f)
            ]
    high, low = two_parts(table_ref[...])
    return big_dot(high, pick) + big_dot(low, pick)


def flux_sum(values_of, flux_ref, emit):
    for first in range(0, FIELDS, 3):
        sums = [[None] * 4 for _ in range(3)]
        for i in range(4):
            for f in range(FIELDS):
                value = values_of(i, f)
                for k in range(3):
                    term = value * flux_ref[i, f, first + k : first + k + 1, :]
                    old = sums[k][i]
                    sums[k][i] = term if old is None else old + term
        for k in range(3):
            emit(first + k, jnp.concatenate(sums[k], axis=0))


def turn_masks(turn):
    masks = []
    for h in range(3):
        rows = [
            jnp.broadcast_to(jnp.where(turn[i : i + 1, :] == h, 1.0, 0.0), (NPAD, LANES))
            for i in range(4)
        ]
        masks.append(jnp.concatenate(rows, axis=0).astype(BF))
    return masks


def stack_own(z_ref, g, value):
    high, low = two_parts(value)
    lanes = field_lanes(g)
    z_ref[0:FACES, lanes] = high
    z_ref[FACES : 2 * FACES, lanes] = low
    z_ref[2 * FACES : 3 * FACES, lanes] = high


def stack_turned(z_ref, base, g, value, masks):
    high, low = two_parts(value)
    lanes = field_lanes(g)
    for h in range(3):
        start = base + h * 3 * FACES
        turned = high * masks[h]
        z_ref[start : start + FACES, lanes] = turned
        z_ref[start + FACES : start + 2 * FACES, lanes] = low * masks[h]
        z_ref[start + 2 * FACES : start + 3 * FACES, lanes] = turned


def received_faces(received, pair_matrix, marks_ref, pick):
    rims = jnp.concatenate([ref[...] for ref in received], axis=0)
    high, low = two_parts(rims)
    parts = []
    for q in range((FIELDS + 1) // 2):
        lanes = field_lanes(q)
        rhs = jnp.concatenate([high[:, lanes], low[:, lanes], high[:, lanes]], axis=1)
        out = lax.dot_general(
            pair_matrix, rhs, (((1,), (1,)), ((), ())), preferred_element_type=F32
        )
        for side in range(2):
            if 2 * q + side < FIELDS:
                total = None
                for j in range(4):
                    start = side * FACES + j * NPAD
                    term = out[start : start + NPAD, :] * marks_ref[j : j + 1, :]
                    total = term if total is None else total + term
                parts.append(total)
    high, low = two_parts(jnp.concatenate(parts, axis=0))
    return big_dot(high, pick) + big_dot(low, pick)


def first_kernel(
    u_hbm, star_ref, forward_ref, halo_ref,
    u_ref, first_ref, second_ref, s0, s1, s2, s3, xs_ref, y_ref, sems,
):
    copies = []
    for f in range(FIELDS):
        copy = pltpu.make_async_copy(u_hbm.at[:, f, :], u_ref.at[field_rows(f), :], sems.at[f])
        copy.start()
        copies.append(copy)
    for copy in copies:
        copy.wait()
    taylor(
        lambda f: u_ref[field_rows(f), :], star_ref, forward_ref[...], xs_ref, y_ref,
        [(first_ref, integral_weights(0.0, 0.5)), (second_ref, integral_weights(0.5, 1.0))],
    )
    for f in range(FIELDS):
        put_operand(xs_ref, f, first_ref[field_rows(f), :])
    send_rims(xs_ref, halo_ref, (s0, s1, s2, s3))


def middle_local_kernel(
    u_ref, first_ref, star_ref, plus_ref, minus_ref, update_ref, lift_ref,
    part_ref, slot_ref, face_ref, turn_ref,
    base_ref, g_ref, marks_ref, xs_ref, y_ref, table_ref, z_ref,
):
    width = marks_ref.shape[1] // 4
    part, slot, face = part_ref[...], slot_ref[...], face_ref[...]
    for f in range(FIELDS):
        put_operand(xs_ref, f, first_ref[field_rows(f), :])
    wide_dot(update_ref[...], xs_ref, y_ref)
    g_ref[...] = pick_faces(y_ref, 3 * MODES, table_ref, local_pick(part, slot, face))
    far = remote_pick(part, slot, width)
    rows = [jnp.where(face == j, 1.0, 0.0) for j in range(4)]
    kinds = jnp.concatenate(
        [jnp.concatenate([row[i : i + 1, :] for i in range(4)], axis=1) for row in rows], axis=0
    )
    kinds = jnp.concatenate([kinds, jnp.zeros_like(kinds)], axis=0).astype(BF)
    marks_ref[...] = lax.dot_general(
        kinds, far, (((1,), (1,)), ((), ())), preferred_element_type=F32
    )
    finish_local(
        lambda f: u_ref[field_rows(f), :], star_ref, plus_ref, minus_ref, lift_ref,
        turn_ref[...], y_ref, g_ref, z_ref, base_ref,
    )


def finish_local(base_of, star_ref, plus_ref, minus_ref, lift_ref, turn, y_ref, g_ref, z_ref, base_ref):
    masks = turn_masks(turn)
    top = 3 * MODES
    flux_sum(
        lambda i, f: y_ref[top + i * NPAD : top + (i + 1) * NPAD, field_lanes(f)],
        plus_ref,
        lambda g, value: stack_own(z_ref, g, value),
    )
    flux_sum(
        lambda i, f: g_ref[f * NPAD : (f + 1) * NPAD, i * LANES : (i + 1) * LANES],
        minus_ref,
        lambda g, value: stack_turned(z_ref, 3 * FACES, g, value, masks),
    )

    def emit(g, value):
        base_ref[field_rows(g), :] = base_of(g) + value

    star_sum(y_ref, star_ref, emit)
    subtract_lift(lift_ref[...], z_ref, base_ref, base_ref)


def subtract_lift(lift, z_ref, base_ref, out_ref):
    for f in range(0, FIELDS, 2):
        fields = range(f, min(f + 2, FIELDS))
        lanes = slice(f * LANES, (fields[-1] + 1) * LANES)
        lifted = big_dot(lift, z_ref[:, lanes])
        for n, g in enumerate(fields):
            out_ref[field_rows(g), :] = base_ref[field_rows(g), :] - lifted[:, field_lanes(n)]


def middle_remote_kernel(
    r0, r1, r2, r3, u_ref, base_ref, g_ref, second_ref, star_ref, minus_ref,
    forward_ref, lift_ref, pair_ref, marks_ref, part_ref, slot_ref, turn_ref, cluster_ref, halo_ref,
    middle_ref, later_ref, gsum_ref, s0, s1, s2, s3, xs_ref, y_ref, z_ref, far_ref,
):
    pick = remote_pick(part_ref[...], slot_ref[...], r0.shape[0])
    far_ref[...] = received_faces((r0, r1, r2, r3), pair_ref[...], marks_ref, pick)
    gsum_ref[...] = g_ref[...] + far_ref[...]
    masks = turn_masks(turn_ref[...])
    flux_sum(
        lambda i, f: far_ref[f * NPAD : (f + 1) * NPAD, i * LANES : (i + 1) * LANES],
        minus_ref,
        lambda g, value: stack_turned(z_ref, 0, g, value, masks),
    )
    subtract_lift(lift_ref[:, 3 * FACES :], z_ref, base_ref, middle_ref)
    small = cluster_ref[...] == 0
    for f in range(FIELDS):
        middle_ref[field_rows(f), :] = jnp.where(
            small, middle_ref[field_rows(f), :], u_ref[field_rows(f), :]
        )
    taylor(
        lambda f: middle_ref[field_rows(f), :], star_ref, forward_ref[...], xs_ref, y_ref,
        [(later_ref, integral_weights(0.0, 0.5))],
    )
    for f in range(FIELDS):
        later = jnp.where(small, later_ref[field_rows(f), :], second_ref[field_rows(f), :])
        later_ref[field_rows(f), :] = later
        put_operand(xs_ref, f, later)
    send_rims(xs_ref, halo_ref, (s0, s1, s2, s3))


def last_local_kernel(
    u_ref, middle_ref, first_ref, second_ref, later_ref, gsum_ref, star_ref, plus_ref, minus_ref,
    update_ref, lift_ref, part_ref, slot_ref, face_ref, turn_ref, cluster_ref,
    base_ref, xs_ref, y_ref, table_ref, z_ref, g_ref,
):
    small = cluster_ref[...] == 0
    for f in range(FIELDS):
        put_operand(xs_ref, f, later_ref[field_rows(f), :])
    wide_dot(update_ref[3 * MODES :, :], xs_ref, y_ref)
    near = pick_faces(y_ref, 0, table_ref, local_pick(part_ref[...], slot_ref[...], face_ref[...]))
    large4 = jnp.concatenate([jnp.where(small, 0.0, 1.0)] * 4, axis=1)
    g_ref[...] = near + gsum_ref[...] * large4
    for f in range(FIELDS):
        rows = field_rows(f)
        put_operand(
            xs_ref, f, jnp.where(small, later_ref[rows, :], first_ref[rows, :] + second_ref[rows, :])
        )
    wide_dot(update_ref[...], xs_ref, y_ref)
    finish_local(
        lambda f: middle_ref[field_rows(f), :],
        star_ref, plus_ref, minus_ref, lift_ref, turn_ref[...], y_ref, g_ref, z_ref, base_ref,
    )


def last_remote_kernel(
    r0, r1, r2, r3, base_ref, minus_ref, lift_ref, pair_ref, marks_ref, part_ref, slot_ref, turn_ref,
    out_hbm, z_ref, far_ref, done_ref, sems,
):
    pick = remote_pick(part_ref[...], slot_ref[...], r0.shape[0])
    far_ref[...] = received_faces((r0, r1, r2, r3), pair_ref[...], marks_ref, pick)
    masks = turn_masks(turn_ref[...])
    flux_sum(
        lambda i, f: far_ref[f * NPAD : (f + 1) * NPAD, i * LANES : (i + 1) * LANES],
        minus_ref,
        lambda g, value: stack_turned(z_ref, 0, g, value, masks),
    )
    subtract_lift(lift_ref[:, 3 * FACES :], z_ref, base_ref, done_ref)
    copies = []
    for f in range(FIELDS):
        copy = pltpu.make_async_copy(done_ref.at[field_rows(f), :], out_hbm.at[:, f, :], sems.at[f])
        copy.start()
        copies.append(copy)
    for copy in copies:
        copy.wait()


def padded_to(x, shape):
    return jnp.pad(x, [(0, want - have) for have, want in zip(x.shape, shape)])


def triple(x):
    high, low = outer_parts(x)
    return jnp.concatenate([high, high, low], axis=-1).astype(BF)


def constants(stiffness, face_lift, face_project):
    forward = padded_to(stiffness, (3, MODES, MPAD)).reshape(3 * MODES, MPAD)
    backward = padded_to(jnp.transpose(stiffness, (0, 2, 1)), (3, MODES, MPAD))
    project = padded_to(face_project, (4, NPAD, MPAD)).reshape(FACES, MPAD)
    update = jnp.concatenate([backward.reshape(3 * MODES, MPAD), project], axis=0)
    zero = jnp.zeros_like(project)
    pair = jnp.concatenate(
        [jnp.concatenate([project, zero], axis=1), jnp.concatenate([zero, project], axis=1)], axis=0
    )
    lifts = []
    tables = rotations()
    for h in (0, 0, 1, 2):
        turned = face_lift[:, :, np.argsort(tables[h])]
        turned = padded_to(turned, (4, MODES, NPAD))
        lifts.append(triple(jnp.transpose(turned, (1, 0, 2)).reshape(MODES, FACES)))
    return triple(forward), triple(update), jnp.concatenate(lifts, axis=1), triple(pair)


VM = pl.BlockSpec(memory_space=pltpu.VMEM)
HB = pl.BlockSpec(memory_space=pl.ANY)
STATE = (FIELDS * MODES, LANES)
GATHERED = (FIELDS * NPAD, 4 * LANES)


def call(kernel, in_specs, outs, out_specs, scratch, name):
    return pl.pallas_call(
        kernel,
        out_shape=[jax.ShapeDtypeStruct(shape, F32) for shape in outs],
        in_specs=in_specs,
        out_specs=out_specs,
        scratch_shapes=scratch,
        compiler_params=pltpu.CompilerParams(vmem_limit_bytes=24 << 20),
        cost_estimate=pl.CostEstimate(flops=10**9, bytes_accessed=10**6, transcendentals=0),
        name=name,
    )


def scratch_xs():
    return pltpu.VMEM((3 * MPAD, FIELDS * LANES), BF)


def scratch_y(rows):
    return pltpu.VMEM((rows, FIELDS * LANES), F32)


def scratch_z(rows):
    return pltpu.VMEM((rows, FIELDS * LANES), BF)


def shift(x, axis, step):
    count = lax.axis_size(axis)
    return lax.ppermute(x, axis, [(i, (i + step) % count) for i in range(count)])


def trade(sends):
    return (
        shift(sends[0], "near", 1),
        shift(sends[1], "near", -1),
        shift(sends[2], "dom", 1),
        shift(sends[3], "dom", -1),
    )


def on_device(
    u, star, plus, minus, stiffness, face_lift, face_project,
    cluster, part, slot, face, turn, halo,
):
    width = halo.shape[1]
    cluster = cluster.reshape(1, LANES)
    forward, update, lift, pair = constants(stiffness, face_lift, face_project)
    rim = (width, 5 * LANES)
    ufm, first, second, *sends = call(
        first_kernel, [HB, VM, VM, VM], [STATE] * 3 + [rim] * 4, [VM] * 7,
        [scratch_xs(), scratch_y(3 * MODES), pltpu.SemaphoreType.DMA((FIELDS,))], "first",
    )(u, star, forward, halo)
    received = trade(sends)
    rows = 3 * MODES + FACES
    base, g, marks = call(
        middle_local_kernel, [VM] * 11, [STATE, GATHERED, (8, 4 * width)], [VM] * 3,
        [scratch_xs(), scratch_y(rows), pltpu.VMEM(GATHERED, F32), scratch_z(12 * FACES)],
        "middle_local",
    )(ufm, first, star, plus, minus, update, lift, part, slot, face, turn)
    middle, later, gsum, *sends = call(
        middle_remote_kernel, [VM] * 19, [STATE, STATE, GATHERED] + [rim] * 4, [VM] * 7,
        [scratch_xs(), scratch_y(3 * MODES), scratch_z(9 * FACES), pltpu.VMEM(GATHERED, F32)],
        "middle_remote",
    )(
        *received, ufm, base, g, second, star, minus, forward, lift, pair, marks,
        part, slot, turn, cluster, halo,
    )
    received = trade(sends)
    (base,) = call(
        last_local_kernel, [VM] * 16, [STATE], [VM],
        [
            scratch_xs(), scratch_y(rows), pltpu.VMEM(GATHERED, F32), scratch_z(12 * FACES),
            pltpu.VMEM(GATHERED, F32),
        ],
        "last_local",
    )(
        ufm, middle, first, second, later, gsum, star, plus, minus, update, lift,
        part, slot, face, turn, cluster,
    )
    (out,) = call(
        last_remote_kernel, [VM] * 12, [u.shape], [HB],
        [
            scratch_z(9 * FACES), pltpu.VMEM(GATHERED, F32), pltpu.VMEM(STATE, F32),
            pltpu.SemaphoreType.DMA((FIELDS,)),
        ],
        "last_remote",
    )(*received, base, minus, lift, pair, marks, part, slot, turn)
    return out


def solution(mesh):
    both = ("dom", "near")
    in_specs = (
        P(None, None, both), P(None, None, None, both), P(None, None, None, both),
        P(None, None, None, both), P(), P(), P(), P(both),
        P(None, both), P(None, both), P(None, both), P(None, both), P(None, both),
    )
    return jax.shard_map(
        on_device, mesh=mesh, in_specs=in_specs, out_specs=P(None, None, both), check_vma=False
    )
```

```python
import functools
import math

import jax
import jax.numpy as jnp
import numpy as np
from jax import lax
from jax.experimental import pallas as pl
from jax.experimental.pallas import tpu as pltpu
from jax.sharding import PartitionSpec as P

MODES = 56
FIELDS = 9
NODES = 21
ORDER = 6
MPAD = 64
NPAD = 24
LANES = 128
FACES = 4 * NPAD
BF = jnp.bfloat16
F32 = jnp.float32


def rotations():
    degree = ORDER - 1
    nodes = [(a, b) for a in range(degree + 1) for b in range(degree + 1 - a)]
    lookup = {point: number for number, point in enumerate(nodes)}
    tables = []
    for rotation in range(3):
        row = []
        for a, b in nodes:
            triple = (a, b, degree - a - b)
            rolled = triple[rotation:] + triple[:rotation]
            row.append(lookup[rolled[0], rolled[1]])
        tables.append(row)
    return np.array(tables, dtype=np.int32)


def integral_weights(begin, end):
    return [(end ** (k + 1) - begin ** (k + 1)) / math.factorial(k + 1) for k in range(ORDER)]


def two_parts(x):
    high = x.astype(BF)
    low = (x - high.astype(F32)).astype(BF)
    return high, low


def float_parts(x):
    high = x.astype(BF).astype(F32)
    return high, x - high


def field_lanes(f):
    return slice(f * LANES, (f + 1) * LANES)


def field_rows(f):
    return slice(f * MODES, (f + 1) * MODES)


def put_operand(xs_ref, f, x):
    x = jnp.concatenate([x, jnp.zeros((MPAD - MODES, LANES), F32)], axis=0)
    high, low = two_parts(x)
    lanes = field_lanes(f)
    xs_ref[0:MPAD, lanes] = high
    xs_ref[MPAD : 2 * MPAD, lanes] = low
    xs_ref[2 * MPAD : 3 * MPAD, lanes] = high


def big_dot(lhs, rhs):
    return jnp.dot(lhs, rhs, preferred_element_type=F32)


def wide_dot(lhs, xs_ref, y_ref):
    rows = lhs.shape[0]
    for f in range(0, FIELDS, 2):
        lanes = slice(f * LANES, min(f + 2, FIELDS) * LANES)
        y_ref[0:rows, lanes] = big_dot(lhs, xs_ref[:, lanes])


def star_sum(y_ref, star_ref, emit):
    for first in range(0, FIELDS, 3):
        sums = [None] * 3
        for d in range(3):
            for f in range(FIELDS):
                y = y_ref[d * MODES : (d + 1) * MODES, field_lanes(f)]
                for k in range(3):
                    scale = star_ref[f, first + k, d : d + 1, :]
                    term = y * scale
                    sums[k] = term if sums[k] is None else sums[k] + term
        for k in range(3):
            emit(first + k, sums[k])


def taylor(start_of, star_ref, forward, xs_ref, y_ref, integrals):
    for f in range(FIELDS):
        value = start_of(f)
        put_operand(xs_ref, f, value)
        for ref, weights in integrals:
            ref[field_rows(f), :] = weights[0] * value
    for k in range(1, ORDER):
        wide_dot(forward, xs_ref, y_ref)

        def emit(g, value, k=k):
            if k < ORDER - 1:
                put_operand(xs_ref, g, value)
            for ref, weights in integrals:
                ref[field_rows(g), :] = ref[field_rows(g), :] + weights[k] * value

        star_sum(y_ref, star_ref, emit)


def evens():
    return [lax.rem(lax.axis_index(axis), 2) == 0 for axis in ("near", "dom")]


def send_rims(xs_ref, halo_ref, sends):
    width = halo_ref.shape[1]
    element = lax.broadcasted_iota(jnp.int32, (LANES, width), 0)
    picks = []
    for axis, even in enumerate(evens()):
        up, down = halo_ref[2 * axis : 2 * axis + 1, :], halo_ref[2 * axis + 1 : 2 * axis + 2, :]
        for row in (jnp.where(even, up, down), jnp.where(even, down, up)):
            pick = jnp.where(element == row, 1.0, 0.0).astype(F32)
            picks.append(jnp.transpose(pick))
    pick = jnp.concatenate(picks, axis=0).astype(BF)
    for q in range((FIELDS + 1) // 2):
        fields = (2 * q, min(2 * q + 1, FIELDS - 1))
        total = None
        for piece in range(2):
            rows = slice(piece * MPAD, (piece + 1) * MPAD)
            both = jnp.concatenate([xs_ref[rows, field_lanes(f)] for f in fields], axis=0)
            part = lax.dot_general(
                pick, both, (((1,), (1,)), ((), ())), preferred_element_type=F32
            )
            total = part if total is None else total + part
        for r in range(4):
            sends[r][:, field_lanes(q)] = total[r * width : (r + 1) * width, :]


def local_pick(part, slot, face):
    target = jnp.where(part == 0, face * LANES + slot, -1)
    target = jnp.concatenate([target[i : i + 1, :] for i in range(4)], axis=1)
    row = lax.broadcasted_iota(jnp.int32, (4 * LANES, 4 * LANES), 0)
    return jnp.where(row == target, 1.0, 0.0).astype(BF)


def remote_pick(part, slot, width):
    near_even, dom_even = evens()
    near_block = jnp.where(near_even, 2 - part, part - 1)
    dom_block = jnp.where(dom_even, 6 - part, part - 1)
    block = jnp.where(part > 2, dom_block, near_block)
    target = jnp.where(part > 0, block * width + slot, -1)
    target = jnp.concatenate([target[i : i + 1, :] for i in range(4)], axis=1)
    row = lax.broadcasted_iota(jnp.int32, (4 * width, 4 * LANES), 0)
    return jnp.where(row == target, 1.0, 0.0).astype(BF)


def pick_faces(y_ref, base_row, table_ref, pick):
    for f in range(FIELDS):
        for j in range(4):
            table_ref[f * NPAD : (f + 1) * NPAD, j * LANES : (j + 1) * LANES] = y_ref[
                base_row + j * NPAD : base_row + (j + 1) * NPAD, field_lanes(f)
            ]
    high, low = two_parts(table_ref[...])
    return big_dot(high, pick) + big_dot(low, pick)


def flux_sum(values_of, flux_ref, emit):
    for first in range(0, FIELDS, 3):
        sums = [[None] * 4 for _ in range(3)]
        for i in range(4):
            for f in range(FIELDS):
                value = values_of(i, f)
                for k in range(3):
                    term = value * flux_ref[f, first + k, i : i + 1, :]
                    old = sums[k][i]
                    sums[k][i] = term if old is None else old + term
        for k in range(3):
            emit(first + k, jnp.concatenate(sums[k], axis=0))


def turn_masks(turn):
    masks = []
    for h in range(3):
        rows = [
            jnp.broadcast_to(jnp.where(turn[i : i + 1, :] == h, 1.0, 0.0), (NPAD, LANES))
            for i in range(4)
        ]
        masks.append(jnp.concatenate(rows, axis=0).astype(BF))
    return masks


def stack_own(z_ref, g, value):
    lanes = field_lanes(g)
    for piece, part in enumerate(two_parts(value)):
        z_ref[piece, 3 * FACES : 4 * FACES, lanes] = part


def stack_turned(z_ref, g, value, masks):
    lanes = field_lanes(g)
    for piece, part in enumerate(two_parts(value)):
        for h in range(3):
            z_ref[piece, h * FACES : (h + 1) * FACES, lanes] = part * masks[h]


def subtract_lift(lift_ref, rows, z_ref, base_ref, out_ref):
    both = lift_ref[:, 0:rows]
    for f in range(0, FIELDS, 2):
        fields = range(f, min(f + 2, FIELDS))
        lanes = slice(f * LANES, (fields[-1] + 1) * LANES)
        high = big_dot(both, z_ref[0, 0:rows, lanes])
        lifted = high[0:MODES] + high[MODES:] + big_dot(both[0:MODES], z_ref[1, 0:rows, lanes])
        for n, g in enumerate(fields):
            out_ref[field_rows(g), :] = base_ref[field_rows(g), :] - lifted[:, field_lanes(n)]


def received_faces(received, pair_matrix, marks_ref, pick):
    rims = jnp.concatenate([ref[...] for ref in received], axis=0)
    high, low = two_parts(rims)
    parts = []
    for q in range((FIELDS + 1) // 2):
        lanes = field_lanes(q)
        rhs = jnp.concatenate([high[:, lanes], low[:, lanes], high[:, lanes]], axis=1)
        out = lax.dot_general(
            pair_matrix, rhs, (((1,), (1,)), ((), ())), preferred_element_type=F32
        )
        for side in range(2):
            if 2 * q + side < FIELDS:
                total = None
                for j in range(4):
                    start = side * FACES + j * NPAD
                    term = out[start : start + NPAD, :] * marks_ref[j : j + 1, :]
                    total = term if total is None else total + term
                parts.append(total)
    high, low = two_parts(jnp.concatenate(parts, axis=0))
    return big_dot(high, pick) + big_dot(low, pick)


def wide(x):
    return jnp.concatenate([x, jnp.zeros((x.shape[0], LANES - x.shape[1]), F32)], axis=1)


def tall(x, rows):
    return jnp.concatenate([x, jnp.zeros((rows - x.shape[0], x.shape[1]), F32)], axis=0)


def tripled(x):
    high, low = float_parts(x)
    first = high + pltpu.roll(high, MPAD, 1)
    return jnp.concatenate([first, low], axis=1).astype(BF)[:, 0 : 3 * MPAD]


def forward_matrix(stiff_ref):
    return tripled(jnp.concatenate([wide(stiff_ref[d]) for d in range(3)], axis=0))


def prepare(stiff_ref, lift_ref, project_ref, update_ref, lifts_ref, pair_ref, rows_ref):
    backward = [
        jnp.transpose(tall(wide(stiff_ref[d]), LANES))[0:MODES, :] for d in range(3)
    ]
    project = jnp.concatenate(
        [wide(tall(project_ref[:, j, :], NPAD)) for j in range(4)], axis=0
    )
    update_ref[...] = tripled(jnp.concatenate(backward + [project], axis=0))
    high, low = float_parts(project)
    moved = [pltpu.roll(part, MPAD, 1) for part in (high, low)]
    highs = jnp.concatenate([high, moved[0]], axis=0).astype(BF)
    lows = jnp.concatenate([low, moved[1]], axis=0).astype(BF)
    pair_ref[...] = jnp.concatenate([highs, highs, lows], axis=1)
    rows_ref[...] = jnp.zeros(rows_ref.shape, F32)
    tables = rotations()
    for block, h in enumerate((0, 1, 2, 0)):
        for i in range(4):
            for p in range(NODES):
                row = block * FACES + i * NPAD + int(tables[h][p])
                rows_ref[row : row + 1, 0:MODES] = lift_ref[p, i : i + 1, :]
    columns = []
    for t in range(4 * FACES // LANES):
        columns.append(jnp.transpose(rows_ref[t * LANES : (t + 1) * LANES, :])[0:MODES, :])
    high, low = float_parts(jnp.concatenate(columns, axis=1))
    lifts_ref[...] = jnp.concatenate([high, low], axis=0).astype(BF)


def first_kernel(
    u_ref, star_ref, stiff_ref, halo_ref,
    first_ref, second_ref, forward_ref, s0, s1, s2, s3, xs_ref, y_ref,
):
    forward_ref[...] = forward_matrix(stiff_ref)
    taylor(
        lambda f: u_ref[field_rows(f), :], star_ref, forward_ref[...], xs_ref, y_ref,
        [(first_ref, integral_weights(0.0, 0.5)), (second_ref, integral_weights(0.5, 1.0))],
    )
    for f in range(FIELDS):
        put_operand(xs_ref, f, first_ref[field_rows(f), :])
    send_rims(xs_ref, halo_ref, (s0, s1, s2, s3))


def middle_local_kernel(
    u_ref, first_ref, star_ref, plus_ref, minus_ref, stiff_ref, face_lift_ref, project_ref,
    part_ref, slot_ref, face_ref, turn_ref,
    base_ref, g_ref, marks_ref, update_ref, lift_ref, pair_ref,
    xs_ref, y_ref, table_ref, z_ref, rows_ref,
):
    width = marks_ref.shape[1] // 4
    prepare(stiff_ref, face_lift_ref, project_ref, update_ref, lift_ref, pair_ref, rows_ref)
    part, slot, face = part_ref[...], slot_ref[...], face_ref[...]
    for f in range(FIELDS):
        put_operand(xs_ref, f, first_ref[field_rows(f), :])
    wide_dot(update_ref[...], xs_ref, y_ref)
    g_ref[...] = pick_faces(y_ref, 3 * MODES, table_ref, local_pick(part, slot, face))
    far = remote_pick(part, slot, width)
    rows = [jnp.where(face == j, 1.0, 0.0) for j in range(4)]
    kinds = jnp.concatenate(
        [jnp.concatenate([row[i : i + 1, :] for i in range(4)], axis=1) for row in rows], axis=0
    )
    kinds = jnp.concatenate([kinds, jnp.zeros_like(kinds)], axis=0).astype(BF)
    marks_ref[...] = lax.dot_general(
        kinds, far, (((1,), (1,)), ((), ())), preferred_element_type=F32
    )
    finish_local(
        lambda f: u_ref[field_rows(f), :], star_ref, plus_ref, minus_ref, lift_ref,
        turn_ref[...], y_ref, g_ref, z_ref, base_ref,
    )


def finish_local(base_of, star_ref, plus_ref, minus_ref, lift_ref, turn, y_ref, g_ref, z_ref, base_ref):
    masks = turn_masks(turn)
    top = 3 * MODES
    flux_sum(
        lambda i, f: y_ref[top + i * NPAD : top + (i + 1) * NPAD, field_lanes(f)],
        plus_ref,
        lambda g, value: stack_own(z_ref, g, value),
    )
    flux_sum(
        lambda i, f: g_ref[f * NPAD : (f + 1) * NPAD, i * LANES : (i + 1) * LANES],
        minus_ref,
        lambda g, value: stack_turned(z_ref, g, value, masks),
    )

    def emit(g, value):
        base_ref[field_rows(g), :] = base_of(g) + value

    star_sum(y_ref, star_ref, emit)
    subtract_lift(lift_ref, 4 * FACES, z_ref, base_ref, base_ref)


def middle_remote_kernel(
    r0, r1, r2, r3, u_ref, base_ref, g_ref, second_ref, star_ref, minus_ref,
    forward_ref, lift_ref, pair_ref, marks_ref, part_ref, slot_ref, turn_ref, cluster_ref, halo_ref,
    middle_ref, later_ref, gsum_ref, s0, s1, s2, s3, xs_ref, y_ref, z_ref, far_ref,
):
    pick = remote_pick(part_ref[...], slot_ref[...], r0.shape[0])
    far_ref[...] = received_faces((r0, r1, r2, r3), pair_ref[...], marks_ref, pick)
    gsum_ref[...] = g_ref[...] + far_ref[...]
    masks = turn_masks(turn_ref[...])
    flux_sum(
        lambda i, f: far_ref[f * NPAD : (f + 1) * NPAD, i * LANES : (i + 1) * LANES],
        minus_ref,
        lambda g, value: stack_turned(z_ref, g, value, masks),
    )
    subtract_lift(lift_ref, 3 * FACES, z_ref, base_ref, middle_ref)
    small = cluster_ref[...] == 0
    for f in range(FIELDS):
        middle_ref[field_rows(f), :] = jnp.where(
            small, middle_ref[field_rows(f), :], u_ref[field_rows(f), :]
        )
    taylor(
        lambda f: middle_ref[field_rows(f), :], star_ref, forward_ref[...], xs_ref, y_ref,
        [(later_ref, integral_weights(0.0, 0.5))],
    )
    for f in range(FIELDS):
        later = jnp.where(small, later_ref[field_rows(f), :], second_ref[field_rows(f), :])
        later_ref[field_rows(f), :] = later
        put_operand(xs_ref, f, later)
    send_rims(xs_ref, halo_ref, (s0, s1, s2, s3))


def last_local_kernel(
    u_ref, middle_ref, first_ref, second_ref, later_ref, gsum_ref, star_ref, plus_ref, minus_ref,
    update_ref, lift_ref, part_ref, slot_ref, face_ref, turn_ref, cluster_ref,
    base_ref, xs_ref, y_ref, table_ref, z_ref, g_ref,
):
    small = cluster_ref[...] == 0
    for f in range(FIELDS):
        put_operand(xs_ref, f, later_ref[field_rows(f), :])
    wide_dot(update_ref[3 * MODES :, :], xs_ref, y_ref)
    near = pick_faces(y_ref, 0, table_ref, local_pick(part_ref[...], slot_ref[...], face_ref[...]))
    large4 = jnp.concatenate([jnp.where(small, 0.0, 1.0)] * 4, axis=1)
    g_ref[...] = near + gsum_ref[...] * large4
    for f in range(FIELDS):
        rows = field_rows(f)
        put_operand(
            xs_ref, f, jnp.where(small, later_ref[rows, :], first_ref[rows, :] + second_ref[rows, :])
        )
    wide_dot(update_ref[...], xs_ref, y_ref)
    finish_local(
        lambda f: middle_ref[field_rows(f), :],
        star_ref, plus_ref, minus_ref, lift_ref, turn_ref[...], y_ref, g_ref, z_ref, base_ref,
    )


def last_remote_kernel(
    r0, r1, r2, r3, base_ref, minus_ref, lift_ref, pair_ref, marks_ref, part_ref, slot_ref, turn_ref,
    out_ref, z_ref, far_ref,
):
    pick = remote_pick(part_ref[...], slot_ref[...], r0.shape[0])
    far_ref[...] = received_faces((r0, r1, r2, r3), pair_ref[...], marks_ref, pick)
    masks = turn_masks(turn_ref[...])
    flux_sum(
        lambda i, f: far_ref[f * NPAD : (f + 1) * NPAD, i * LANES : (i + 1) * LANES],
        minus_ref,
        lambda g, value: stack_turned(z_ref, g, value, masks),
    )
    subtract_lift(lift_ref, 3 * FACES, z_ref, base_ref, out_ref)


VM = pl.BlockSpec(memory_space=pltpu.VMEM)
STATE = (FIELDS * MODES, LANES)
GATHERED = (FIELDS * NPAD, 4 * LANES)


def call(kernel, inputs, outs, scratch, name):
    out_shape = [jax.ShapeDtypeStruct(shape, kind) for shape, kind in outs]
    return pl.pallas_call(
        kernel,
        out_shape=out_shape,
        in_specs=[VM] * len(inputs),
        out_specs=[VM] * len(out_shape),
        scratch_shapes=scratch,
        compiler_params=pltpu.CompilerParams(vmem_limit_bytes=24 << 20),
        cost_estimate=pl.CostEstimate(flops=10**9, bytes_accessed=10**6, transcendentals=0),
        name=name,
    )(*inputs)


def scratch_xs():
    return pltpu.VMEM((3 * MPAD, FIELDS * LANES), BF)


def scratch_y(rows):
    return pltpu.VMEM((rows, FIELDS * LANES), F32)


def scratch_z(rows):
    return pltpu.VMEM((2, rows, FIELDS * LANES), BF)


def swap(x, axis, kind):
    count = lax.axis_size(axis)
    pairs = []
    for a in range(kind, count, 2):
        b = (a + 1) % count
        pairs += [(a, b), (b, a)]
    return lax.ppermute(x, axis, pairs)


def trade(sends):
    dom_odd = swap(sends[3], "dom", 1)
    dom_even = swap(sends[2], "dom", 0)
    near_odd = swap(sends[1], "near", 1)
    near_even = swap(sends[0], "near", 0)
    return near_even, near_odd, dom_even, dom_odd


def on_device(
    u, star, plus, minus, stiffness, face_lift, face_project,
    cluster, part, slot, face, turn, halo,
):
    width = halo.shape[1]
    u = jnp.transpose(u, (1, 0, 2)).reshape(STATE)
    star, plus, minus = [jnp.transpose(x, (1, 2, 0, 3)) for x in (star, plus, minus)]
    face_lift = jnp.transpose(face_lift, (2, 0, 1))
    face_project = jnp.transpose(face_project, (1, 0, 2))
    cluster = cluster.reshape(1, LANES)
    state, gathered = (STATE, F32), (GATHERED, F32)
    rims = [((width, 5 * LANES), F32)] * 4
    update_rows = 3 * MODES + FACES
    first, second, forward, *sends = call(
        first_kernel, (u, star, stiffness, halo),
        [state, state, ((3 * MODES, 3 * MPAD), BF)] + rims,
        [scratch_xs(), scratch_y(3 * MODES)], "first",
    )
    received = trade(sends)
    base, g, marks, update, lift, pair = call(
        middle_local_kernel,
        (u, first, star, plus, minus, stiffness, face_lift, face_project, part, slot, face, turn),
        [
            state, gathered, ((8, 4 * width), F32), ((update_rows, 3 * MPAD), BF),
            ((2 * MODES, 4 * FACES), BF), ((2 * FACES, 3 * LANES), BF),
        ],
        [
            scratch_xs(), scratch_y(update_rows), pltpu.VMEM(GATHERED, F32), scratch_z(4 * FACES),
            pltpu.VMEM((4 * FACES, LANES), F32),
        ],
        "middle_local",
    )
    middle, later, gsum, *sends = call(
        middle_remote_kernel,
        (
            *received, u, base, g, second, star, minus, forward, lift, pair, marks,
            part, slot, turn, cluster, halo,
        ),
        [state, state, gathered] + rims,
        [scratch_xs(), scratch_y(3 * MODES), scratch_z(3 * FACES), pltpu.VMEM(GATHERED, F32)],
        "middle_remote",
    )
    received = trade(sends)
    (base,) = call(
        last_local_kernel,
        (
            u, middle, first, second, later, gsum, star, plus, minus, update, lift,
            part, slot, face, turn, cluster,
        ),
        [state],
        [
            scratch_xs(), scratch_y(update_rows), pltpu.VMEM(GATHERED, F32), scratch_z(4 * FACES),
            pltpu.VMEM(GATHERED, F32),
        ],
        "last_local",
    )
    (out,) = call(
        last_remote_kernel,
        (*received, base, minus, lift, pair, marks, part, slot, turn),
        [state],
        [scratch_z(3 * FACES), pltpu.VMEM(GATHERED, F32)],
        "last_remote",
    )
    return jnp.transpose(out.reshape(FIELDS, MODES, LANES), (1, 0, 2))


def solution(mesh):
    both = ("dom", "near")
    in_specs = (
        P(None, None, both), P(None, None, None, both), P(None, None, None, both),
        P(None, None, None, both), P(), P(), P(), P(both),
        P(None, both), P(None, both), P(None, both), P(None, both), P(None, both),
    )
    return jax.shard_map(
        on_device, mesh=mesh, in_specs=in_specs, out_specs=P(None, None, both), check_vma=False
    )
```

```python
import functools
import math

import jax
import jax.numpy as jnp
import numpy as np
from jax import lax
from jax.experimental import pallas as pl
from jax.experimental.pallas import tpu as pltpu
from jax.sharding import PartitionSpec as P

MODES = 56
FIELDS = 9
NODES = 21
ORDER = 6
MPAD = 64
NPAD = 24
LANES = 128
FACES = 4 * NPAD
BF = jnp.bfloat16
F32 = jnp.float32


def rotations():
    degree = ORDER - 1
    nodes = [(a, b) for a in range(degree + 1) for b in range(degree + 1 - a)]
    lookup = {point: number for number, point in enumerate(nodes)}
    tables = []
    for rotation in range(3):
        row = []
        for a, b in nodes:
            triple = (a, b, degree - a - b)
            rolled = triple[rotation:] + triple[:rotation]
            row.append(lookup[rolled[0], rolled[1]])
        tables.append(row)
    return np.array(tables, dtype=np.int32)


def integral_weights(begin, end):
    return [(end ** (k + 1) - begin ** (k + 1)) / math.factorial(k + 1) for k in range(ORDER)]


def two_parts(x):
    high = x.astype(BF)
    low = (x - high.astype(F32)).astype(BF)
    return high, low


def float_parts(x):
    high = x.astype(BF).astype(F32)
    return high, x - high


def field_lanes(f):
    return slice(f * LANES, (f + 1) * LANES)


def field_rows(f):
    return slice(f * MODES, (f + 1) * MODES)


def put_operand(xs_ref, f, x):
    x = jnp.concatenate([x, jnp.zeros((MPAD - MODES, LANES), F32)], axis=0)
    high, low = two_parts(x)
    lanes = field_lanes(f)
    xs_ref[0:MPAD, lanes] = high
    xs_ref[MPAD : 2 * MPAD, lanes] = low
    xs_ref[2 * MPAD : 3 * MPAD, lanes] = high


def big_dot(lhs, rhs):
    return jnp.dot(lhs, rhs, preferred_element_type=F32)


def wide_dot(lhs, xs_ref, y_ref):
    rows = lhs.shape[0]
    for f in range(0, FIELDS, 2):
        lanes = slice(f * LANES, min(f + 2, FIELDS) * LANES)
        y_ref[0:rows, lanes] = big_dot(lhs, xs_ref[:, lanes])


def star_sum(y_ref, star_ref, emit):
    for first in range(0, FIELDS, 3):
        sums = [None] * 3
        for d in range(3):
            for f in range(FIELDS):
                y = y_ref[d * MODES : (d + 1) * MODES, field_lanes(f)]
                for k in range(3):
                    scale = star_ref[f, first + k, d : d + 1, :]
                    term = y * scale
                    sums[k] = term if sums[k] is None else sums[k] + term
        for k in range(3):
            emit(first + k, sums[k])


def taylor(start_of, star_ref, forward, xs_ref, y_ref, integrals):
    for f in range(FIELDS):
        value = start_of(f)
        put_operand(xs_ref, f, value)
        for ref, weights in integrals:
            ref[field_rows(f), :] = weights[0] * value
    for k in range(1, ORDER):
        wide_dot(forward, xs_ref, y_ref)

        def emit(g, value, k=k):
            if k < ORDER - 1:
                put_operand(xs_ref, g, value)
            for ref, weights in integrals:
                ref[field_rows(g), :] = ref[field_rows(g), :] + weights[k] * value

        star_sum(y_ref, star_ref, emit)


def evens():
    return [lax.rem(lax.axis_index(axis), 2) == 0 for axis in ("near", "dom")]


def send_rims(xs_ref, halo_ref, sends):
    width = halo_ref.shape[1]
    element = lax.broadcasted_iota(jnp.int32, (LANES, width), 0)
    near_even, dom_even = evens()
    picks = []
    for even, first in ((dom_even, 2), (near_even, 0)):
        up, down = halo_ref[first : first + 1, :], halo_ref[first + 1 : first + 2, :]
        for row in (jnp.where(even, down, up), jnp.where(even, up, down)):
            pick = jnp.where(element == row, 1.0, 0.0).astype(F32)
            picks.append(jnp.transpose(pick))
    pick = jnp.concatenate(picks, axis=0).astype(BF)
    for q in range((FIELDS + 1) // 2):
        fields = (2 * q, min(2 * q + 1, FIELDS - 1))
        total = None
        for piece in range(2):
            rows = slice(piece * MPAD, (piece + 1) * MPAD)
            both = jnp.concatenate([xs_ref[rows, field_lanes(f)] for f in fields], axis=0)
            part = lax.dot_general(
                pick, both, (((1,), (1,)), ((), ())), preferred_element_type=F32
            )
            total = part if total is None else total + part
        for r in range(4):
            sends[r][:, field_lanes(q)] = total[r * width : (r + 1) * width, :]


def local_pick(part, slot, face):
    target = jnp.where(part == 0, face * LANES + slot, -1)
    target = jnp.concatenate([target[i : i + 1, :] for i in range(4)], axis=1)
    row = lax.broadcasted_iota(jnp.int32, (4 * LANES, 4 * LANES), 0)
    return jnp.where(row == target, 1.0, 0.0).astype(BF)


def remote_pick(part, slot, width):
    near_even, dom_even = evens()
    near_block = jnp.where(near_even, part + 1, 4 - part)
    dom_block = jnp.where(dom_even, part - 3, 4 - part)
    block = jnp.where(part > 2, dom_block, near_block)
    target = jnp.where(part > 0, block * width + slot, -1)
    target = jnp.concatenate([target[i : i + 1, :] for i in range(4)], axis=1)
    row = lax.broadcasted_iota(jnp.int32, (4 * width, 4 * LANES), 0)
    return jnp.where(row == target, 1.0, 0.0).astype(BF)


def pick_faces(y_ref, base_row, table_ref, pick):
    for f in range(FIELDS):
        for j in range(4):
            table_ref[f * NPAD : (f + 1) * NPAD, j * LANES : (j + 1) * LANES] = y_ref[
                base_row + j * NPAD : base_row + (j + 1) * NPAD, field_lanes(f)
            ]
    high, low = two_parts(table_ref[...])
    return big_dot(high, pick) + big_dot(low, pick)


def flux_sum(values_of, flux_ref, emit):
    for first in range(0, FIELDS, 3):
        sums = [[None] * 4 for _ in range(3)]
        for i in range(4):
            for f in range(FIELDS):
                value = values_of(i, f)
                for k in range(3):
                    term = value * flux_ref[f, first + k, i : i + 1, :]
                    old = sums[k][i]
                    sums[k][i] = term if old is None else old + term
        for k in range(3):
            emit(first + k, jnp.concatenate(sums[k], axis=0))


def turn_masks(turn):
    masks = []
    for h in range(3):
        rows = [
            jnp.broadcast_to(jnp.where(turn[i : i + 1, :] == h, 1.0, 0.0), (NPAD, LANES))
            for i in range(4)
        ]
        masks.append(jnp.concatenate(rows, axis=0).astype(BF))
    return masks


def stack_own(z_ref, g, value):
    lanes = field_lanes(g)
    for piece, part in enumerate(two_parts(value)):
        z_ref[piece, 3 * FACES : 4 * FACES, lanes] = part


def stack_turned(z_ref, g, value, masks):
    lanes = field_lanes(g)
    for piece, part in enumerate(two_parts(value)):
        for h in range(3):
            z_ref[piece, h * FACES : (h + 1) * FACES, lanes] = part * masks[h]


def subtract_lift(lift_ref, rows, z_ref, base_ref, out_ref):
    both = lift_ref[:, 0:rows]
    for f in range(0, FIELDS, 2):
        fields = range(f, min(f + 2, FIELDS))
        lanes = slice(f * LANES, (fields[-1] + 1) * LANES)
        high = big_dot(both, z_ref[0, 0:rows, lanes])
        lifted = high[0:MODES] + high[MODES:] + big_dot(both[0:MODES], z_ref[1, 0:rows, lanes])
        for n, g in enumerate(fields):
            out_ref[field_rows(g), :] = base_ref[field_rows(g), :] - lifted[:, field_lanes(n)]


def received_faces(received, pair_matrix, marks_ref, pick):
    rims = jnp.concatenate([ref[...] for ref in received], axis=0)
    high, low = two_parts(rims)
    parts = []
    for q in range((FIELDS + 1) // 2):
        lanes = field_lanes(q)
        rhs = jnp.concatenate([high[:, lanes], low[:, lanes], high[:, lanes]], axis=1)
        out = lax.dot_general(
            pair_matrix, rhs, (((1,), (1,)), ((), ())), preferred_element_type=F32
        )
        for side in range(2):
            if 2 * q + side < FIELDS:
                total = None
                for j in range(4):
                    start = side * FACES + j * NPAD
                    term = out[start : start + NPAD, :] * marks_ref[j : j + 1, :]
                    total = term if total is None else total + term
                parts.append(total)
    high, low = two_parts(jnp.concatenate(parts, axis=0))
    return big_dot(high, pick) + big_dot(low, pick)


def wide(x):
    return jnp.concatenate([x, jnp.zeros((x.shape[0], LANES - x.shape[1]), F32)], axis=1)


def tall(x, rows):
    return jnp.concatenate([x, jnp.zeros((rows - x.shape[0], x.shape[1]), F32)], axis=0)


def tripled(x):
    high, low = float_parts(x)
    first = high + pltpu.roll(high, MPAD, 1)
    return jnp.concatenate([first, low], axis=1).astype(BF)[:, 0 : 3 * MPAD]


def forward_matrix(stiff_ref):
    return tripled(jnp.concatenate([wide(stiff_ref[d]) for d in range(3)], axis=0))


def prepare(stiff_ref, lift_ref, project_ref, update_ref, lifts_ref, pair_ref, rows_ref):
    backward = [
        jnp.transpose(tall(wide(stiff_ref[d]), LANES))[0:MODES, :] for d in range(3)
    ]
    project = jnp.concatenate(
        [wide(tall(project_ref[:, j, :], NPAD)) for j in range(4)], axis=0
    )
    update_ref[...] = tripled(jnp.concatenate(backward + [project], axis=0))
    high, low = float_parts(project)
    moved = [pltpu.roll(part, MPAD, 1) for part in (high, low)]
    highs = jnp.concatenate([high, moved[0]], axis=0).astype(BF)
    lows = jnp.concatenate([low, moved[1]], axis=0).astype(BF)
    pair_ref[...] = jnp.concatenate([highs, highs, lows], axis=1)
    rows_ref[...] = jnp.zeros(rows_ref.shape, F32)
    tables = rotations()
    for block, h in enumerate((0, 1, 2, 0)):
        for i in range(4):
            for p in range(NODES):
                row = block * FACES + i * NPAD + int(tables[h][p])
                rows_ref[row : row + 1, 0:MODES] = lift_ref[p, i : i + 1, :]
    columns = []
    for t in range(4 * FACES // LANES):
        columns.append(jnp.transpose(rows_ref[t * LANES : (t + 1) * LANES, :])[0:MODES, :])
    high, low = float_parts(jnp.concatenate(columns, axis=1))
    lifts_ref[...] = jnp.concatenate([high, low], axis=0).astype(BF)


INPUTS = 13


def first_kernel(*refs):
    sources, rest = refs[:INPUTS], refs[INPUTS:]
    held, rest = rest[:INPUTS], rest[INPUTS:]
    first_ref, second_ref, forward_ref, s0, s1, s2, s3, xs_ref, y_ref, sems = rest
    copies = [
        pltpu.make_async_copy(source, target, sems.at[n])
        for n, (source, target) in enumerate(zip(sources, held))
    ]
    for copy in copies:
        copy.start()
    u_ref, star_ref, stiff_ref, halo_ref = held[:4]
    for copy in copies[:3]:
        copy.wait()
    forward_ref[...] = forward_matrix(stiff_ref)
    taylor(
        lambda f: u_ref[field_rows(f), :], star_ref, forward_ref[...], xs_ref, y_ref,
        [(first_ref, integral_weights(0.0, 0.5)), (second_ref, integral_weights(0.5, 1.0))],
    )
    for copy in copies[3:]:
        copy.wait()
    for f in range(FIELDS):
        put_operand(xs_ref, f, first_ref[field_rows(f), :])
    send_rims(xs_ref, halo_ref, (s0, s1, s2, s3))


def middle_local_kernel(
    u_ref, first_ref, star_ref, plus_ref, minus_ref, stiff_ref, face_lift_ref, project_ref,
    part_ref, slot_ref, face_ref, turn_ref,
    base_ref, g_ref, marks_ref, update_ref, lift_ref, pair_ref,
    xs_ref, y_ref, table_ref, z_ref, rows_ref,
):
    width = marks_ref.shape[1] // 4
    prepare(stiff_ref, face_lift_ref, project_ref, update_ref, lift_ref, pair_ref, rows_ref)
    part, slot, face = part_ref[...], slot_ref[...], face_ref[...]
    for f in range(FIELDS):
        put_operand(xs_ref, f, first_ref[field_rows(f), :])
    wide_dot(update_ref[...], xs_ref, y_ref)
    g_ref[...] = pick_faces(y_ref, 3 * MODES, table_ref, local_pick(part, slot, face))
    far = remote_pick(part, slot, width)
    rows = [jnp.where(face == j, 1.0, 0.0) for j in range(4)]
    kinds = jnp.concatenate(
        [jnp.concatenate([row[i : i + 1, :] for i in range(4)], axis=1) for row in rows], axis=0
    )
    kinds = jnp.concatenate([kinds, jnp.zeros_like(kinds)], axis=0).astype(BF)
    marks_ref[...] = lax.dot_general(
        kinds, far, (((1,), (1,)), ((), ())), preferred_element_type=F32
    )
    finish_local(
        lambda f: u_ref[field_rows(f), :], star_ref, plus_ref, minus_ref, lift_ref,
        turn_ref[...], y_ref, g_ref, z_ref, base_ref,
    )


def finish_local(base_of, star_ref, plus_ref, minus_ref, lift_ref, turn, y_ref, g_ref, z_ref, base_ref):
    masks = turn_masks(turn)
    top = 3 * MODES
    flux_sum(
        lambda i, f: y_ref[top + i * NPAD : top + (i + 1) * NPAD, field_lanes(f)],
        plus_ref,
        lambda g, value: stack_own(z_ref, g, value),
    )
    flux_sum(
        lambda i, f: g_ref[f * NPAD : (f + 1) * NPAD, i * LANES : (i + 1) * LANES],
        minus_ref,
        lambda g, value: stack_turned(z_ref, g, value, masks),
    )

    def emit(g, value):
        base_ref[field_rows(g), :] = base_of(g) + value

    star_sum(y_ref, star_ref, emit)
    subtract_lift(lift_ref, 4 * FACES, z_ref, base_ref, base_ref)


def middle_remote_kernel(
    r0, r1, r2, r3, u_ref, base_ref, g_ref, second_ref, star_ref, minus_ref,
    forward_ref, lift_ref, pair_ref, marks_ref, part_ref, slot_ref, turn_ref, cluster_ref, halo_ref,
    middle_ref, later_ref, gsum_ref, s0, s1, s2, s3, xs_ref, y_ref, z_ref, far_ref,
):
    pick = remote_pick(part_ref[...], slot_ref[...], r0.shape[0])
    far_ref[...] = received_faces((r0, r1, r2, r3), pair_ref[...], marks_ref, pick)
    gsum_ref[...] = g_ref[...] + far_ref[...]
    masks = turn_masks(turn_ref[...])
    flux_sum(
        lambda i, f: far_ref[f * NPAD : (f + 1) * NPAD, i * LANES : (i + 1) * LANES],
        minus_ref,
        lambda g, value: stack_turned(z_ref, g, value, masks),
    )
    subtract_lift(lift_ref, 3 * FACES, z_ref, base_ref, middle_ref)
    small = cluster_ref[...] == 0
    for f in range(FIELDS):
        middle_ref[field_rows(f), :] = jnp.where(
            small, middle_ref[field_rows(f), :], u_ref[field_rows(f), :]
        )
    taylor(
        lambda f: middle_ref[field_rows(f), :], star_ref, forward_ref[...], xs_ref, y_ref,
        [(later_ref, integral_weights(0.0, 0.5))],
    )
    for f in range(FIELDS):
        later = jnp.where(small, later_ref[field_rows(f), :], second_ref[field_rows(f), :])
        later_ref[field_rows(f), :] = later
        put_operand(xs_ref, f, later)
    send_rims(xs_ref, halo_ref, (s0, s1, s2, s3))


def last_local_kernel(
    u_ref, middle_ref, first_ref, second_ref, later_ref, gsum_ref, star_ref, plus_ref, minus_ref,
    update_ref, lift_ref, part_ref, slot_ref, face_ref, turn_ref, cluster_ref,
    base_ref, xs_ref, y_ref, table_ref, z_ref, g_ref,
):
    small = cluster_ref[...] == 0
    for f in range(FIELDS):
        put_operand(xs_ref, f, later_ref[field_rows(f), :])
    wide_dot(update_ref[3 * MODES :, :], xs_ref, y_ref)
    near = pick_faces(y_ref, 0, table_ref, local_pick(part_ref[...], slot_ref[...], face_ref[...]))
    large4 = jnp.concatenate([jnp.where(small, 0.0, 1.0)] * 4, axis=1)
    g_ref[...] = near + gsum_ref[...] * large4
    for f in range(FIELDS):
        rows = field_rows(f)
        put_operand(
            xs_ref, f, jnp.where(small, later_ref[rows, :], first_ref[rows, :] + second_ref[rows, :])
        )
    wide_dot(update_ref[...], xs_ref, y_ref)
    finish_local(
        lambda f: middle_ref[field_rows(f), :],
        star_ref, plus_ref, minus_ref, lift_ref, turn_ref[...], y_ref, g_ref, z_ref, base_ref,
    )


def last_remote_kernel(
    r0, r1, r2, r3, base_ref, minus_ref, lift_ref, pair_ref, marks_ref, part_ref, slot_ref, turn_ref,
    out_ref, z_ref, far_ref,
):
    pick = remote_pick(part_ref[...], slot_ref[...], r0.shape[0])
    far_ref[...] = received_faces((r0, r1, r2, r3), pair_ref[...], marks_ref, pick)
    masks = turn_masks(turn_ref[...])
    flux_sum(
        lambda i, f: far_ref[f * NPAD : (f + 1) * NPAD, i * LANES : (i + 1) * LANES],
        minus_ref,
        lambda g, value: stack_turned(z_ref, g, value, masks),
    )
    subtract_lift(lift_ref, 3 * FACES, z_ref, base_ref, out_ref)


VM = pl.BlockSpec(memory_space=pltpu.VMEM)
STATE = (FIELDS * MODES, LANES)
GATHERED = (FIELDS * NPAD, 4 * LANES)


def call(kernel, inputs, outs, scratch, name, space=pltpu.VMEM):
    out_shape = [jax.ShapeDtypeStruct(shape, kind) for shape, kind in outs]
    return pl.pallas_call(
        kernel,
        out_shape=out_shape,
        in_specs=[pl.BlockSpec(memory_space=space)] * len(inputs),
        out_specs=[VM] * len(out_shape),
        scratch_shapes=scratch,
        compiler_params=pltpu.CompilerParams(vmem_limit_bytes=24 << 20),
        cost_estimate=pl.CostEstimate(flops=10**9, bytes_accessed=10**6, transcendentals=0),
        name=name,
    )(*inputs)


def scratch_xs():
    return pltpu.VMEM((3 * MPAD, FIELDS * LANES), BF)


def scratch_y(rows):
    return pltpu.VMEM((rows, FIELDS * LANES), F32)


def scratch_z(rows):
    return pltpu.VMEM((2, rows, FIELDS * LANES), BF)


def swap(x, axis, kind):
    count = lax.axis_size(axis)
    pairs = []
    for a in range(kind, count, 2):
        b = (a + 1) % count
        pairs += [(a, b), (b, a)]
    return lax.ppermute(x, axis, pairs)


def trade(sends):
    return [
        swap(send, axis, kind)
        for send, (axis, kind) in zip(sends, (("dom", 1), ("dom", 0), ("near", 1), ("near", 0)))
    ]


def on_device(
    u, star, plus, minus, stiffness, face_lift, face_project,
    cluster, part, slot, face, turn, halo,
):
    width = halo.shape[1]
    u = jnp.transpose(u, (1, 0, 2)).reshape(STATE)
    star, plus, minus = [jnp.transpose(x, (1, 2, 0, 3)) for x in (star, plus, minus)]
    face_lift = jnp.transpose(face_lift, (2, 0, 1))
    face_project = jnp.transpose(face_project, (1, 0, 2))
    state, gathered = (STATE, F32), (GATHERED, F32)
    rims = [((width, 5 * LANES), F32)] * 4
    update_rows = 3 * MODES + FACES
    inputs = (
        u, star, stiffness, halo, plus, minus, face_lift, face_project,
        part, slot, face, turn, cluster.reshape(1, LANES),
    )
    inputs = [pltpu.with_memory_space_constraint(x, pltpu.HBM) for x in inputs]
    *held, first, second, forward, s0, s1, s2, s3 = call(
        first_kernel, inputs,
        [(x.shape, x.dtype) for x in inputs]
        + [state, state, ((3 * MODES, 3 * MPAD), BF)] + rims,
        [scratch_xs(), scratch_y(3 * MODES), pltpu.SemaphoreType.DMA((INPUTS,))], "first",
        pltpu.HBM,
    )
    u, star, stiffness, halo, plus, minus, face_lift, face_project = held[:8]
    part, slot, face, turn, cluster = held[8:]
    sends = s0, s1, s2, s3
    received = trade(sends)
    base, g, marks, update, lift, pair = call(
        middle_local_kernel,
        (u, first, star, plus, minus, stiffness, face_lift, face_project, part, slot, face, turn),
        [
            state, gathered, ((8, 4 * width), F32), ((update_rows, 3 * MPAD), BF),
            ((2 * MODES, 4 * FACES), BF), ((2 * FACES, 3 * LANES), BF),
        ],
        [
            scratch_xs(), scratch_y(update_rows), pltpu.VMEM(GATHERED, F32), scratch_z(4 * FACES),
            pltpu.VMEM((4 * FACES, LANES), F32),
        ],
        "middle_local",
    )
    middle, later, gsum, *sends = call(
        middle_remote_kernel,
        (
            *received, u, base, g, second, star, minus, forward, lift, pair, marks,
            part, slot, turn, cluster, halo,
        ),
        [state, state, gathered] + rims,
        [scratch_xs(), scratch_y(3 * MODES), scratch_z(3 * FACES), pltpu.VMEM(GATHERED, F32)],
        "middle_remote",
    )
    received = trade(sends)
    (base,) = call(
        last_local_kernel,
        (
            u, middle, first, second, later, gsum, star, plus, minus, update, lift,
            part, slot, face, turn, cluster,
        ),
        [state],
        [
            scratch_xs(), scratch_y(update_rows), pltpu.VMEM(GATHERED, F32), scratch_z(4 * FACES),
            pltpu.VMEM(GATHERED, F32),
        ],
        "last_local",
    )
    (out,) = call(
        last_remote_kernel,
        (*received, base, minus, lift, pair, marks, part, slot, turn),
        [state],
        [scratch_z(3 * FACES), pltpu.VMEM(GATHERED, F32)],
        "last_remote",
    )
    return jnp.transpose(out.reshape(FIELDS, MODES, LANES), (1, 0, 2))


def solution(mesh):
    both = ("dom", "near")
    in_specs = (
        P(None, None, both), P(None, None, None, both), P(None, None, None, both),
        P(None, None, None, both), P(), P(), P(), P(both),
        P(None, both), P(None, both), P(None, both), P(None, both), P(None, both),
    )
    return jax.shard_map(
        on_device, mesh=mesh, in_specs=in_specs, out_specs=P(None, None, both), check_vma=False
    )
```

```python
import functools
import math

import jax
import jax.numpy as jnp
import numpy as np
from jax import lax
from jax.experimental import pallas as pl
from jax.experimental.pallas import tpu as pltpu
from jax.sharding import PartitionSpec as P

MODES = 56
FIELDS = 9
NODES = 21
ORDER = 6
MPAD = 64
NPAD = 24
LANES = 128
FACES = 4 * NPAD
BF = jnp.bfloat16
F32 = jnp.float32


def rotations():
    degree = ORDER - 1
    nodes = [(a, b) for a in range(degree + 1) for b in range(degree + 1 - a)]
    lookup = {point: number for number, point in enumerate(nodes)}
    tables = []
    for rotation in range(3):
        row = []
        for a, b in nodes:
            triple = (a, b, degree - a - b)
            rolled = triple[rotation:] + triple[:rotation]
            row.append(lookup[rolled[0], rolled[1]])
        tables.append(row)
    return np.array(tables, dtype=np.int32)


def integral_weights(begin, end):
    return [(end ** (k + 1) - begin ** (k + 1)) / math.factorial(k + 1) for k in range(ORDER)]


def two_parts(x):
    high = x.astype(BF)
    low = (x - high.astype(F32)).astype(BF)
    return high, low


def float_parts(x):
    high = x.astype(BF).astype(F32)
    return high, x - high


def field_lanes(f):
    return slice(f * LANES, (f + 1) * LANES)


def field_rows(f):
    return slice(f * MODES, (f + 1) * MODES)


def put_operand(xs_ref, f, x):
    x = jnp.concatenate([x, jnp.zeros((MPAD - MODES, LANES), F32)], axis=0)
    high, low = two_parts(x)
    lanes = field_lanes(f)
    xs_ref[0:MPAD, lanes] = high
    xs_ref[MPAD : 2 * MPAD, lanes] = low
    xs_ref[2 * MPAD : 3 * MPAD, lanes] = high


def big_dot(lhs, rhs):
    return jnp.dot(lhs, rhs, preferred_element_type=F32)


def wide_dot(lhs, xs_ref, y_ref):
    rows = lhs.shape[0]
    for f in range(0, FIELDS, 2):
        lanes = slice(f * LANES, min(f + 2, FIELDS) * LANES)
        y_ref[0:rows, lanes] = big_dot(lhs, xs_ref[:, lanes])


def star_sum(y_ref, star_ref, emit):
    for first in range(0, FIELDS, 3):
        sums = [None] * 3
        for d in range(3):
            for f in range(FIELDS):
                y = y_ref[d * MODES : (d + 1) * MODES, field_lanes(f)]
                for k in range(3):
                    scale = star_ref[f, first + k, d : d + 1, :]
                    term = y * scale
                    sums[k] = term if sums[k] is None else sums[k] + term
        for k in range(3):
            emit(first + k, sums[k])


GROUP = 3


class Steps:
    def __init__(self, halo_ref):
        self.value = halo_ref[0, 0]
        self.bound = 4096

    def __call__(self, body):
        self.bound += 1
        pl.when(self.value < self.bound)(body)


def star_group(y_ref, star_ref, first, emit, order):
    sums = [None] * GROUP
    for f in order:
        for d in range(3):
            y = y_ref[d * MODES : (d + 1) * MODES, field_lanes(f)]
            for k in range(GROUP):
                term = y * star_ref[f, first + k, d : d + 1, :]
                sums[k] = term if sums[k] is None else sums[k] + term
    for k in range(GROUP):
        emit(first + k, sums[k])


def taylor(block, start_of, star_ref, forward_ref, xs_ref, y_ref, integrals):
    def start():
        for f in range(FIELDS):
            value = start_of(f)
            put_operand(xs_ref, f, value)
            for ref, weights in integrals:
                ref[field_rows(f), :] = weights[0] * value

    def step(k, n):

        def emit(g, value):
            if k < ORDER - 1:
                put_operand(xs_ref, g, value)
            for ref, weights in integrals:
                ref[field_rows(g), :] = ref[field_rows(g), :] + weights[k] * value

        if n == 0:
            wide_dot(forward_ref[...], xs_ref, y_ref)
        star_group(y_ref, star_ref, n * GROUP, emit, range(FIELDS))

    block(start)
    for k in range(1, ORDER):
        block(functools.partial(step, k, 0))

        def rest(k=k):
            step(k, 1)
            step(k, 2)

        block(rest)


PAIRS = (FIELDS + 1) // 2
DROWS = 16


def nt_dot(lhs, rhs):
    return lax.dot_general(lhs, rhs, (((1,), (1,)), ((), ())), preferred_element_type=F32)


def pair_lanes(j):
    return slice(2 * j * LANES, min(2 * j + 2, FIELDS) * LANES)


def pack_matrix(cluster):
    small = jnp.where(cluster == 0, 1.0, 0.0)
    before = lax.broadcasted_iota(jnp.int32, (LANES, LANES), 0)
    after = lax.broadcasted_iota(jnp.int32, (LANES, LANES), 1)
    upper = jnp.where(before < after, 1.0, 0.0).astype(BF)
    place = big_dot(jnp.broadcast_to(small, (8, LANES)).astype(BF), upper)[0:1, :]
    place = jnp.where(cluster == 0, place, -1.0).astype(jnp.int32)
    row = lax.broadcasted_iota(jnp.int32, (MPAD, LANES), 0)
    pick = jnp.where(row == place, 1.0, 0.0)
    none = jnp.zeros_like(pick)
    return jnp.concatenate(
        [jnp.concatenate([pick, none], axis=1), jnp.concatenate([none, pick], axis=1)], axis=0
    ).astype(BF)


def pack_star(star_ref, pack_ref, packed_ref):
    pad = jnp.zeros((DROWS - FIELDS, LANES), F32)
    rows = []
    for f in range(FIELDS):
        parts = []
        for d in range(3):
            parts += [star_ref[f, :, d, :], pad]
        rows.append(jnp.concatenate(parts, axis=0))
    for j in range(PAIRS):
        both = jnp.concatenate(rows[2 * j : 2 * j + 2], axis=1)
        pick = pack_ref[:, 0 : both.shape[1]]
        high, low = two_parts(both)
        packed_ref[j] = nt_dot(high, pick) + nt_dot(low, pick)


def packed_taylor(xs_ref, pack_ref, star_ref, forward, xp_ref, y_ref, sum_ref, weights):
    for j in range(PAIRS):
        lanes = pair_lanes(j)
        pick = pack_ref[:, 0 : lanes.stop - lanes.start]
        value = nt_dot(xs_ref[0:MPAD, lanes], pick) + nt_dot(xs_ref[MPAD : 2 * MPAD, lanes], pick)
        value = value[0:MODES]
        put_operand(xp_ref, j, value)
        sum_ref[field_rows(j), :] = weights[0] * value
    low_half = lax.broadcasted_iota(jnp.int32, (MODES, LANES), 1) < MPAD
    for k in range(1, ORDER):
        for j in range(0, PAIRS, 2):
            lanes = slice(j * LANES, min(j + 2, PAIRS) * LANES)
            y_ref[:, lanes] = big_dot(forward, xp_ref[:, lanes])
        for j in range(PAIRS):
            sums = []
            for g in range(2 * j, min(2 * j + 2, FIELDS)):
                total = None
                for i in range(PAIRS):
                    for d in range(3):
                        y = y_ref[d * MODES : (d + 1) * MODES, field_lanes(i)]
                        term = y * star_ref[i, d * DROWS + g : d * DROWS + g + 1, :]
                        total = term if total is None else total + term
                sums.append(total)
            if len(sums) == 1:
                sums.append(jnp.zeros_like(sums[0]))
            same = jnp.where(low_half, sums[0], sums[1])
            other = jnp.where(low_half, sums[1], sums[0])
            value = same + pltpu.roll(other, MPAD, 1)
            if k < ORDER - 1:
                put_operand(xp_ref, j, value)
            sum_ref[field_rows(j), :] = sum_ref[field_rows(j), :] + weights[k] * value


def unpack(sum_ref, pack_ref, emit):
    for j in range(PAIRS):
        high, low = two_parts(sum_ref[field_rows(j), :])
        pick = pack_ref[:, 0 : min(2, FIELDS - 2 * j) * LANES]
        value = big_dot(high, pick) + big_dot(low, pick)
        for n in range(min(2, FIELDS - 2 * j)):
            emit(2 * j + n, value[:, field_lanes(n)])


def evens():
    return [lax.rem(lax.axis_index(axis), 2) == 0 for axis in ("near", "dom")]


def send_rims(xs_ref, halo_ref, sends):
    width = halo_ref.shape[1]
    element = lax.broadcasted_iota(jnp.int32, (LANES, width), 0)
    near_even, dom_even = evens()
    picks = []
    for even, first in ((dom_even, 2), (near_even, 0)):
        up, down = halo_ref[first : first + 1, :], halo_ref[first + 1 : first + 2, :]
        for row in (jnp.where(even, down, up), jnp.where(even, up, down)):
            pick = jnp.where(element == row, 1.0, 0.0).astype(F32)
            picks.append(jnp.transpose(pick))
    pick = jnp.concatenate(picks, axis=0).astype(BF)
    for q in range((FIELDS + 1) // 2):
        fields = (2 * q, min(2 * q + 1, FIELDS - 1))
        total = None
        for piece in range(2):
            rows = slice(piece * MPAD, (piece + 1) * MPAD)
            both = jnp.concatenate([xs_ref[rows, field_lanes(f)] for f in fields], axis=0)
            part = lax.dot_general(
                pick, both, (((1,), (1,)), ((), ())), preferred_element_type=F32
            )
            total = part if total is None else total + part
        for r in range(4):
            sends[r][:, field_lanes(q)] = total[r * width : (r + 1) * width, :]


def local_pick(part, slot, face):
    target = jnp.where(part == 0, face * LANES + slot, -1)
    target = jnp.concatenate([target[i : i + 1, :] for i in range(4)], axis=1)
    row = lax.broadcasted_iota(jnp.int32, (4 * LANES, 4 * LANES), 0)
    return jnp.where(row == target, 1.0, 0.0).astype(BF)


def remote_pick(part, slot, width):
    near_even, dom_even = evens()
    near_block = jnp.where(near_even, part + 1, 4 - part)
    dom_block = jnp.where(dom_even, part - 3, 4 - part)
    block = jnp.where(part > 2, dom_block, near_block)
    target = jnp.where(part > 0, block * width + slot, -1)
    target = jnp.concatenate([target[i : i + 1, :] for i in range(4)], axis=1)
    row = lax.broadcasted_iota(jnp.int32, (4 * width, 4 * LANES), 0)
    return jnp.where(row == target, 1.0, 0.0).astype(BF)


def pick_faces(y_ref, base_row, table_ref, pick):
    for f in range(FIELDS):
        for j in range(4):
            table_ref[f * NPAD : (f + 1) * NPAD, j * LANES : (j + 1) * LANES] = y_ref[
                base_row + j * NPAD : base_row + (j + 1) * NPAD, field_lanes(f)
            ]
    high, low = two_parts(table_ref[...])
    return big_dot(high, pick) + big_dot(low, pick)


def flux_sum(values_of, flux_ref, emit):
    for first in range(0, FIELDS, 3):
        sums = [[None] * 4 for _ in range(3)]
        for i in range(4):
            for f in range(FIELDS):
                value = values_of(i, f)
                for k in range(3):
                    term = value * flux_ref[f, first + k, i : i + 1, :]
                    old = sums[k][i]
                    sums[k][i] = term if old is None else old + term
        for k in range(3):
            emit(first + k, jnp.concatenate(sums[k], axis=0))


def turn_masks(turn):
    masks = []
    for h in range(3):
        rows = [
            jnp.broadcast_to(jnp.where(turn[i : i + 1, :] == h, 1.0, 0.0), (NPAD, LANES))
            for i in range(4)
        ]
        masks.append(jnp.concatenate(rows, axis=0).astype(BF))
    return masks


def stack_own(z_ref, g, value):
    lanes = field_lanes(g)
    for piece, part in enumerate(two_parts(value)):
        z_ref[piece, 3 * FACES : 4 * FACES, lanes] = part


def stack_turned(z_ref, g, value, masks):
    lanes = field_lanes(g)
    for piece, part in enumerate(two_parts(value)):
        for h in range(3):
            z_ref[piece, h * FACES : (h + 1) * FACES, lanes] = part * masks[h]


def subtract_lift(lift_ref, rows, z_ref, base_ref, out_ref):
    both = lift_ref[:, 0:rows]
    for f in range(0, FIELDS, 2):
        fields = range(f, min(f + 2, FIELDS))
        lanes = slice(f * LANES, (fields[-1] + 1) * LANES)
        high = big_dot(both, z_ref[0, 0:rows, lanes])
        lifted = high[0:MODES] + high[MODES:] + big_dot(both[0:MODES], z_ref[1, 0:rows, lanes])
        for n, g in enumerate(fields):
            out_ref[field_rows(g), :] = base_ref[field_rows(g), :] - lifted[:, field_lanes(n)]


def received_faces(received, pair_matrix, marks_ref, pick):
    rims = jnp.concatenate([ref[...] for ref in received], axis=0)
    high, low = two_parts(rims)
    parts = []
    for q in range((FIELDS + 1) // 2):
        lanes = field_lanes(q)
        rhs = jnp.concatenate([high[:, lanes], low[:, lanes], high[:, lanes]], axis=1)
        out = lax.dot_general(
            pair_matrix, rhs, (((1,), (1,)), ((), ())), preferred_element_type=F32
        )
        for side in range(2):
            if 2 * q + side < FIELDS:
                total = None
                for j in range(4):
                    start = side * FACES + j * NPAD
                    term = out[start : start + NPAD, :] * marks_ref[j : j + 1, :]
                    total = term if total is None else total + term
                parts.append(total)
    high, low = two_parts(jnp.concatenate(parts, axis=0))
    return big_dot(high, pick) + big_dot(low, pick)


def wide(x):
    return jnp.concatenate([x, jnp.zeros((x.shape[0], LANES - x.shape[1]), F32)], axis=1)


def tall(x, rows):
    return jnp.concatenate([x, jnp.zeros((rows - x.shape[0], x.shape[1]), F32)], axis=0)


def tripled(x):
    high, low = float_parts(x)
    first = high + pltpu.roll(high, MPAD, 1)
    return jnp.concatenate([first, low], axis=1).astype(BF)[:, 0 : 3 * MPAD]


def forward_matrix(stiff_ref):
    return tripled(jnp.concatenate([wide(stiff_ref[d]) for d in range(3)], axis=0))


def prepare(stiff_ref, lift_ref, project_ref, update_ref, lifts_ref, pair_ref, rows_ref):
    backward = [
        jnp.transpose(tall(wide(stiff_ref[d]), LANES))[0:MODES, :] for d in range(3)
    ]
    project = jnp.concatenate(
        [wide(tall(project_ref[:, j, :], NPAD)) for j in range(4)], axis=0
    )
    update_ref[...] = tripled(jnp.concatenate(backward + [project], axis=0))
    high, low = float_parts(project)
    moved = [pltpu.roll(part, MPAD, 1) for part in (high, low)]
    highs = jnp.concatenate([high, moved[0]], axis=0).astype(BF)
    lows = jnp.concatenate([low, moved[1]], axis=0).astype(BF)
    pair_ref[...] = jnp.concatenate([highs, highs, lows], axis=1)
    rows_ref[...] = jnp.zeros(rows_ref.shape, F32)
    tables = rotations()
    for block, h in enumerate((0, 1, 2, 0)):
        for i in range(4):
            for p in range(NODES):
                row = block * FACES + i * NPAD + int(tables[h][p])
                rows_ref[row : row + 1, 0:MODES] = lift_ref[p, i : i + 1, :]
    columns = []
    for t in range(4 * FACES // LANES):
        columns.append(jnp.transpose(rows_ref[t * LANES : (t + 1) * LANES, :])[0:MODES, :])
    high, low = float_parts(jnp.concatenate(columns, axis=1))
    lifts_ref[...] = jnp.concatenate([high, low], axis=0).astype(BF)


INPUTS = 13


def first_kernel(*refs):
    sources, rest = refs[:INPUTS], refs[INPUTS:]
    held, rest = rest[:INPUTS], rest[INPUTS:]
    first_ref, second_ref, forward_ref, s0, s1, s2, s3, xs_ref, y_ref, sems = rest
    copies = [
        pltpu.make_async_copy(source, target, sems.at[n])
        for n, (source, target) in enumerate(zip(sources, held))
    ]
    for copy in copies:
        copy.start()
    u_ref, star_ref, stiff_ref, halo_ref = held[:4]
    for copy in copies[:4]:
        copy.wait()
    forward_ref[...] = forward_matrix(stiff_ref)
    taylor(
        Steps(halo_ref), lambda f: u_ref[field_rows(f), :], star_ref, forward_ref, xs_ref, y_ref,
        [(first_ref, integral_weights(0.0, 0.5)), (second_ref, integral_weights(0.5, 1.0))],
    )
    for copy in copies[4:]:
        copy.wait()
    for f in range(FIELDS):
        put_operand(xs_ref, f, first_ref[field_rows(f), :])
    send_rims(xs_ref, halo_ref, (s0, s1, s2, s3))


def middle_local_kernel(
    u_ref, first_ref, star_ref, plus_ref, minus_ref, stiff_ref, face_lift_ref, project_ref,
    part_ref, slot_ref, face_ref, turn_ref, cluster_ref,
    base_ref, g_ref, marks_ref, update_ref, lift_ref, pair_ref, pack_ref, packed_ref,
    xs_ref, y_ref, table_ref, z_ref, rows_ref,
):
    width = marks_ref.shape[1] // 4
    prepare(stiff_ref, face_lift_ref, project_ref, update_ref, lift_ref, pair_ref, rows_ref)
    pack_ref[...] = pack_matrix(cluster_ref[...])
    pack_star(star_ref, pack_ref, packed_ref)
    part, slot, face = part_ref[...], slot_ref[...], face_ref[...]
    for f in range(FIELDS):
        put_operand(xs_ref, f, first_ref[field_rows(f), :])
    wide_dot(update_ref[...], xs_ref, y_ref)
    g_ref[...] = pick_faces(y_ref, 3 * MODES, table_ref, local_pick(part, slot, face))
    far = remote_pick(part, slot, width)
    rows = [jnp.where(face == j, 1.0, 0.0) for j in range(4)]
    kinds = jnp.concatenate(
        [jnp.concatenate([row[i : i + 1, :] for i in range(4)], axis=1) for row in rows], axis=0
    )
    kinds = jnp.concatenate([kinds, jnp.zeros_like(kinds)], axis=0).astype(BF)
    marks_ref[...] = lax.dot_general(
        kinds, far, (((1,), (1,)), ((), ())), preferred_element_type=F32
    )
    finish_local(
        lambda f: u_ref[field_rows(f), :], star_ref, plus_ref, minus_ref, lift_ref,
        turn_ref[...], y_ref, g_ref, z_ref, base_ref,
    )


def finish_local(base_of, star_ref, plus_ref, minus_ref, lift_ref, turn, y_ref, g_ref, z_ref, base_ref):
    masks = turn_masks(turn)
    top = 3 * MODES
    flux_sum(
        lambda i, f: y_ref[top + i * NPAD : top + (i + 1) * NPAD, field_lanes(f)],
        plus_ref,
        lambda g, value: stack_own(z_ref, g, value),
    )
    flux_sum(
        lambda i, f: g_ref[f * NPAD : (f + 1) * NPAD, i * LANES : (i + 1) * LANES],
        minus_ref,
        lambda g, value: stack_turned(z_ref, g, value, masks),
    )

    def emit(g, value):
        base_ref[field_rows(g), :] = base_of(g) + value

    star_sum(y_ref, star_ref, emit)
    subtract_lift(lift_ref, 4 * FACES, z_ref, base_ref, base_ref)


def middle_remote_kernel(
    r0, r1, r2, r3, u_ref, base_ref, g_ref, second_ref, star_ref, minus_ref,
    forward_ref, lift_ref, pair_ref, marks_ref, part_ref, slot_ref, turn_ref, cluster_ref, halo_ref,
    pack_ref,
    middle_ref, later_ref, gsum_ref, s0, s1, s2, s3,
    xs_ref, xp_ref, y_ref, sum_ref, z_ref, far_ref,
):
    pick = remote_pick(part_ref[...], slot_ref[...], r0.shape[0])
    far_ref[...] = received_faces((r0, r1, r2, r3), pair_ref[...], marks_ref, pick)
    gsum_ref[...] = g_ref[...] + far_ref[...]
    masks = turn_masks(turn_ref[...])
    flux_sum(
        lambda i, f: far_ref[f * NPAD : (f + 1) * NPAD, i * LANES : (i + 1) * LANES],
        minus_ref,
        lambda g, value: stack_turned(z_ref, g, value, masks),
    )
    subtract_lift(lift_ref, 3 * FACES, z_ref, base_ref, middle_ref)
    small = cluster_ref[...] == 0
    for f in range(FIELDS):
        value = jnp.where(small, middle_ref[field_rows(f), :], u_ref[field_rows(f), :])
        middle_ref[field_rows(f), :] = value
        put_operand(xs_ref, f, value)
    packed_taylor(
        xs_ref, pack_ref, star_ref, forward_ref[...], xp_ref, y_ref, sum_ref,
        integral_weights(0.0, 0.5),
    )

    def emit(f, value):
        later = jnp.where(small, value, second_ref[field_rows(f), :])
        later_ref[field_rows(f), :] = later
        put_operand(xs_ref, f, later)

    unpack(sum_ref, pack_ref, emit)
    send_rims(xs_ref, halo_ref, (s0, s1, s2, s3))


def last_local_kernel(
    u_ref, middle_ref, first_ref, second_ref, later_ref, gsum_ref, star_ref, plus_ref, minus_ref,
    update_ref, lift_ref, part_ref, slot_ref, face_ref, turn_ref, cluster_ref,
    base_ref, xs_ref, y_ref, table_ref, z_ref, g_ref,
):
    small = cluster_ref[...] == 0
    for f in range(FIELDS):
        put_operand(xs_ref, f, later_ref[field_rows(f), :])
    wide_dot(update_ref[3 * MODES :, :], xs_ref, y_ref)
    near = pick_faces(y_ref, 0, table_ref, local_pick(part_ref[...], slot_ref[...], face_ref[...]))
    large4 = jnp.concatenate([jnp.where(small, 0.0, 1.0)] * 4, axis=1)
    g_ref[...] = near + gsum_ref[...] * large4
    for f in range(FIELDS):
        rows = field_rows(f)
        put_operand(
            xs_ref, f, jnp.where(small, later_ref[rows, :], first_ref[rows, :] + second_ref[rows, :])
        )
    wide_dot(update_ref[...], xs_ref, y_ref)
    finish_local(
        lambda f: middle_ref[field_rows(f), :],
        star_ref, plus_ref, minus_ref, lift_ref, turn_ref[...], y_ref, g_ref, z_ref, base_ref,
    )


def last_remote_kernel(
    r0, r1, r2, r3, base_ref, minus_ref, lift_ref, pair_ref, marks_ref, part_ref, slot_ref, turn_ref,
    out_ref, z_ref, far_ref,
):
    pick = remote_pick(part_ref[...], slot_ref[...], r0.shape[0])
    far_ref[...] = received_faces((r0, r1, r2, r3), pair_ref[...], marks_ref, pick)
    masks = turn_masks(turn_ref[...])
    flux_sum(
        lambda i, f: far_ref[f * NPAD : (f + 1) * NPAD, i * LANES : (i + 1) * LANES],
        minus_ref,
        lambda g, value: stack_turned(z_ref, g, value, masks),
    )
    subtract_lift(lift_ref, 3 * FACES, z_ref, base_ref, out_ref)


VM = pl.BlockSpec(memory_space=pltpu.VMEM)
STATE = (FIELDS * MODES, LANES)
GATHERED = (FIELDS * NPAD, 4 * LANES)


def call(kernel, inputs, outs, scratch, name, space=pltpu.VMEM):
    out_shape = [jax.ShapeDtypeStruct(shape, kind) for shape, kind in outs]
    return pl.pallas_call(
        kernel,
        out_shape=out_shape,
        in_specs=[pl.BlockSpec(memory_space=space)] * len(inputs),
        out_specs=[VM] * len(out_shape),
        scratch_shapes=scratch,
        compiler_params=pltpu.CompilerParams(vmem_limit_bytes=24 << 20),
        cost_estimate=pl.CostEstimate(flops=10**9, bytes_accessed=10**6, transcendentals=0),
        name=name,
    )(*inputs)


def scratch_xs():
    return pltpu.VMEM((3 * MPAD, FIELDS * LANES), BF)


def scratch_y(rows):
    return pltpu.VMEM((rows, FIELDS * LANES), F32)


def scratch_z(rows):
    return pltpu.VMEM((2, rows, FIELDS * LANES), BF)


def swap(x, axis, kind):
    count = lax.axis_size(axis)
    pairs = []
    for a in range(kind, count, 2):
        b = (a + 1) % count
        pairs += [(a, b), (b, a)]
    return lax.ppermute(x, axis, pairs)


def trade(sends):
    return [
        swap(send, axis, kind)
        for send, (axis, kind) in zip(sends, (("dom", 1), ("dom", 0), ("near", 1), ("near", 0)))
    ]


def on_device(
    u, star, plus, minus, stiffness, face_lift, face_project,
    cluster, part, slot, face, turn, halo,
):
    width = halo.shape[1]
    u = jnp.transpose(u, (1, 0, 2)).reshape(STATE)
    star, plus, minus = [jnp.transpose(x, (1, 2, 0, 3)) for x in (star, plus, minus)]
    face_lift = jnp.transpose(face_lift, (2, 0, 1))
    face_project = jnp.transpose(face_project, (1, 0, 2))
    state, gathered = (STATE, F32), (GATHERED, F32)
    rims = [((width, 5 * LANES), F32)] * 4
    update_rows = 3 * MODES + FACES
    inputs = (
        u, star, stiffness, halo, plus, minus, face_lift, face_project,
        part, slot, face, turn, cluster.reshape(1, LANES),
    )
    inputs = [pltpu.with_memory_space_constraint(x, pltpu.HBM) for x in inputs]
    *held, first, second, forward, s0, s1, s2, s3 = call(
        first_kernel, inputs,
        [(x.shape, x.dtype) for x in inputs]
        + [state, state, ((3 * MODES, 3 * MPAD), BF)] + rims,
        [scratch_xs(), scratch_y(3 * MODES), pltpu.SemaphoreType.DMA((INPUTS,))], "first",
        pltpu.HBM,
    )
    u, star, stiffness, halo, plus, minus, face_lift, face_project = held[:8]
    part, slot, face, turn, cluster = held[8:]
    sends = s0, s1, s2, s3
    received = trade(sends)
    base, g, marks, update, lift, pair, pack, packed = call(
        middle_local_kernel,
        (u, first, star, plus, minus, stiffness, face_lift, face_project,
         part, slot, face, turn, cluster),
        [
            state, gathered, ((8, 4 * width), F32), ((update_rows, 3 * MPAD), BF),
            ((2 * MODES, 4 * FACES), BF), ((2 * FACES, 3 * LANES), BF),
            ((LANES, 2 * LANES), BF), ((PAIRS, 3 * DROWS, LANES), F32),
        ],
        [
            scratch_xs(), scratch_y(update_rows), pltpu.VMEM(GATHERED, F32), scratch_z(4 * FACES),
            pltpu.VMEM((4 * FACES, LANES), F32),
        ],
        "middle_local",
    )
    middle, later, gsum, *sends = call(
        middle_remote_kernel,
        (
            *received, u, base, g, second, packed, minus, forward, lift, pair, marks,
            part, slot, turn, cluster, halo, pack,
        ),
        [state, state, gathered] + rims,
        [
            scratch_xs(), pltpu.VMEM((3 * MPAD, PAIRS * LANES), BF),
            pltpu.VMEM((3 * MODES, PAIRS * LANES), F32), pltpu.VMEM((PAIRS * MODES, LANES), F32),
            scratch_z(3 * FACES), pltpu.VMEM(GATHERED, F32),
        ],
        "middle_remote",
    )
    received = trade(sends)
    (base,) = call(
        last_local_kernel,
        (
            u, middle, first, second, later, gsum, star, plus, minus, update, lift,
            part, slot, face, turn, cluster,
        ),
        [state],
        [
            scratch_xs(), scratch_y(update_rows), pltpu.VMEM(GATHERED, F32), scratch_z(4 * FACES),
            pltpu.VMEM(GATHERED, F32),
        ],
        "last_local",
    )
    (out,) = call(
        last_remote_kernel,
        (*received, base, minus, lift, pair, marks, part, slot, turn),
        [state],
        [scratch_z(3 * FACES), pltpu.VMEM(GATHERED, F32)],
        "last_remote",
    )
    return jnp.transpose(out.reshape(FIELDS, MODES, LANES), (1, 0, 2))


def solution(mesh):
    both = ("dom", "near")
    in_specs = (
        P(None, None, both), P(None, None, None, both), P(None, None, None, both),
        P(None, None, None, both), P(), P(), P(), P(both),
        P(None, both), P(None, both), P(None, both), P(None, both), P(None, both),
    )
    return jax.shard_map(
        on_device, mesh=mesh, in_specs=in_specs, out_specs=P(None, None, both), check_vma=False
    )
```

```python
import functools
import math

import jax
import jax.numpy as jnp
import numpy as np
from jax import lax
from jax.experimental import pallas as pl
from jax.experimental.pallas import tpu as pltpu
from jax.sharding import PartitionSpec as P

MODES = 56
FIELDS = 9
NODES = 21
ORDER = 6
MPAD = 64
NPAD = 24
LANES = 128
FACES = 4 * NPAD
BF = jnp.bfloat16
F32 = jnp.float32


def rotations():
    degree = ORDER - 1
    nodes = [(a, b) for a in range(degree + 1) for b in range(degree + 1 - a)]
    lookup = {point: number for number, point in enumerate(nodes)}
    tables = []
    for rotation in range(3):
        row = []
        for a, b in nodes:
            triple = (a, b, degree - a - b)
            rolled = triple[rotation:] + triple[:rotation]
            row.append(lookup[rolled[0], rolled[1]])
        tables.append(row)
    return np.array(tables, dtype=np.int32)


def integral_weights(begin, end):
    return [(end ** (k + 1) - begin ** (k + 1)) / math.factorial(k + 1) for k in range(ORDER)]


def two_parts(x):
    high = x.astype(BF)
    low = (x - high.astype(F32)).astype(BF)
    return high, low


def float_parts(x):
    high = x.astype(BF).astype(F32)
    return high, x - high


def field_lanes(f):
    return slice(f * LANES, (f + 1) * LANES)


def field_rows(f):
    return slice(f * MODES, (f + 1) * MODES)


def put_operand(xs_ref, f, x):
    x = jnp.concatenate([x, jnp.zeros((MPAD - MODES, LANES), F32)], axis=0)
    high, low = two_parts(x)
    lanes = field_lanes(f)
    xs_ref[0:MPAD, lanes] = high
    xs_ref[MPAD : 2 * MPAD, lanes] = low
    xs_ref[2 * MPAD : 3 * MPAD, lanes] = high


def big_dot(lhs, rhs):
    return jnp.dot(lhs, rhs, preferred_element_type=F32)


def wide_dot(lhs, xs_ref, y_ref):
    rows = lhs.shape[0]
    for f in range(0, FIELDS, 2):
        lanes = slice(f * LANES, min(f + 2, FIELDS) * LANES)
        y_ref[0:rows, lanes] = big_dot(lhs, xs_ref[:, lanes])


def star_sum(y_ref, star_ref, emit):
    for first in range(0, FIELDS, 3):
        sums = [None] * 3
        for d in range(3):
            for f in range(FIELDS):
                y = y_ref[d * MODES : (d + 1) * MODES, field_lanes(f)]
                for k in range(3):
                    scale = star_ref[f, first + k, d : d + 1, :]
                    term = y * scale
                    sums[k] = term if sums[k] is None else sums[k] + term
        for k in range(3):
            emit(first + k, sums[k])


GROUP = 3


class Steps:
    def __init__(self, halo_ref):
        self.value = halo_ref[0, 0]
        self.bound = 4096

    def __call__(self, body):
        self.bound += 1
        pl.when(self.value < self.bound)(body)


def star_group(y_ref, star_ref, first, emit, order):
    sums = [None] * GROUP
    for f in order:
        for d in range(3):
            y = y_ref[d * MODES : (d + 1) * MODES, field_lanes(f)]
            for k in range(GROUP):
                term = y * star_ref[f, first + k, d : d + 1, :]
                sums[k] = term if sums[k] is None else sums[k] + term
    for k in range(GROUP):
        emit(first + k, sums[k])


def taylor(block, start_of, star_ref, forward_ref, xs_ref, y_ref, integrals):
    def start():
        for f in range(FIELDS):
            value = start_of(f)
            put_operand(xs_ref, f, value)
            for ref, weights in integrals:
                ref[field_rows(f), :] = weights[0] * value

    def step(k, n):

        def emit(g, value):
            if k < ORDER - 1:
                put_operand(xs_ref, g, value)
            for ref, weights in integrals:
                ref[field_rows(g), :] = ref[field_rows(g), :] + weights[k] * value

        if n == 0:
            wide_dot(forward_ref[...], xs_ref, y_ref)
        star_group(y_ref, star_ref, n * GROUP, emit, range(FIELDS))

    block(start)
    for k in range(1, ORDER):
        block(functools.partial(step, k, 0))

        def rest(k=k):
            step(k, 1)
            step(k, 2)

        block(rest)


PAIRS = (FIELDS + 1) // 2
DROWS = 16


def nt_dot(lhs, rhs):
    return lax.dot_general(lhs, rhs, (((1,), (1,)), ((), ())), preferred_element_type=F32)


def pair_lanes(j):
    return slice(2 * j * LANES, min(2 * j + 2, FIELDS) * LANES)


def pack_matrix(cluster):
    small = jnp.where(cluster == 0, 1.0, 0.0)
    before = lax.broadcasted_iota(jnp.int32, (LANES, LANES), 0)
    after = lax.broadcasted_iota(jnp.int32, (LANES, LANES), 1)
    upper = jnp.where(before < after, 1.0, 0.0).astype(BF)
    place = big_dot(jnp.broadcast_to(small, (8, LANES)).astype(BF), upper)[0:1, :]
    place = jnp.where(cluster == 0, place, -1.0).astype(jnp.int32)
    row = lax.broadcasted_iota(jnp.int32, (MPAD, LANES), 0)
    pick = jnp.where(row == place, 1.0, 0.0)
    none = jnp.zeros_like(pick)
    return jnp.concatenate(
        [jnp.concatenate([pick, none], axis=1), jnp.concatenate([none, pick], axis=1)], axis=0
    )


def pack_star(star_ref, pack_ref, packed_ref):
    pad = jnp.zeros((DROWS - FIELDS, LANES), F32)
    rows = []
    for f in range(FIELDS):
        parts = []
        for d in range(3):
            parts += [star_ref[f, :, d, :], pad]
        rows.append(jnp.concatenate(parts, axis=0))
    for j in range(PAIRS):
        both = jnp.concatenate(rows[2 * j : 2 * j + 2], axis=1)
        pick = pack_ref[:, 0 : both.shape[1]]
        high, low = two_parts(both)
        packed_ref[j] = nt_dot(high, pick) + nt_dot(low, pick)


def packed_taylor(star_ref, forward, xp_ref, y_ref, sum_ref, weights):
    for k in range(1, ORDER):
        for j in range(0, PAIRS, 2):
            lanes = slice(j * LANES, min(j + 2, PAIRS) * LANES)
            y_ref[:, lanes] = big_dot(forward, xp_ref[:, lanes])
        for j in range(PAIRS):
            sums = []
            for g in range(2 * j, min(2 * j + 2, FIELDS)):
                total = None
                for i in range(PAIRS):
                    for d in range(3):
                        y = y_ref[d * MODES : (d + 1) * MODES, field_lanes(i)]
                        term = y * star_ref[i, d * DROWS + g : d * DROWS + g + 1, :]
                        total = term if total is None else total + term
                sums.append(total)
            if len(sums) == 1:
                sums.append(jnp.zeros_like(sums[0]))
            value = join_halves(*sums)
            if k < ORDER - 1:
                put_operand(xp_ref, j, value)
            sum_ref[field_rows(j), :] = sum_ref[field_rows(j), :] + weights[k] * value


def pack_state(base_ref, turned_ref, packed_ref):
    for j in range(PAIRS):
        fields = range(2 * j, min(2 * j + 2, FIELDS))
        both = jnp.concatenate([base_ref[field_rows(f), :] for f in fields], axis=1)
        pick = turned_ref[0 : both.shape[1], :]
        high, low = two_parts(both)
        packed_ref[field_rows(j), :] = big_dot(high, pick) + big_dot(low, pick)


def unpack(sum_ref, pack_ref, emit):
    for j in range(PAIRS):
        high, low = two_parts(sum_ref[field_rows(j), :])
        pick = pack_ref[:, 0 : min(2, FIELDS - 2 * j) * LANES]
        value = big_dot(high, pick) + big_dot(low, pick)
        for n in range(min(2, FIELDS - 2 * j)):
            emit(2 * j + n, value[:, field_lanes(n)])


def evens():
    return [lax.rem(lax.axis_index(axis), 2) == 0 for axis in ("near", "dom")]


def send_pick(halo_ref):
    width = halo_ref.shape[1]
    element = lax.broadcasted_iota(jnp.int32, (LANES, width), 0)
    near_even, dom_even = evens()
    picks = []
    for even, first in ((dom_even, 2), (near_even, 0)):
        up, down = halo_ref[first : first + 1, :], halo_ref[first + 1 : first + 2, :]
        for row in (jnp.where(even, down, up), jnp.where(even, up, down)):
            pick = jnp.where(element == row, 1.0, 0.0).astype(F32)
            picks.append(jnp.transpose(pick))
    return jnp.concatenate(picks, axis=0).astype(BF)


def send_rims(xs_ref, pick, sends):
    width = sends[0].shape[0]
    for q in range((FIELDS + 1) // 2):
        fields = (2 * q, min(2 * q + 1, FIELDS - 1))
        total = None
        for piece in range(2):
            rows = slice(piece * MPAD, (piece + 1) * MPAD)
            both = jnp.concatenate([xs_ref[rows, field_lanes(f)] for f in fields], axis=0)
            part = lax.dot_general(
                pick, both, (((1,), (1,)), ((), ())), preferred_element_type=F32
            )
            total = part if total is None else total + part
        for r in range(4):
            sends[r][:, field_lanes(q)] = total[r * width : (r + 1) * width, :]


def send_packed(sum_ref, pick, large_sends, sends):
    width = sends[0].shape[0]
    half = 4 * width
    for j in range(PAIRS):
        value = tall(sum_ref[field_rows(j), :], MPAD)
        high, low = two_parts(jnp.concatenate([value, value], axis=0))
        out = nt_dot(pick, high) + nt_dot(pick, low)
        total = jnp.where(low_half(half), out[0:half], out[half:])
        for r in range(4):
            rows = slice(r * width, (r + 1) * width)
            sends[r][:, field_lanes(j)] = large_sends[r][:, field_lanes(j)] + total[rows, :]


def local_pick(part, slot, face):
    target = jnp.where(part == 0, face * LANES + slot, -1)
    target = jnp.concatenate([target[i : i + 1, :] for i in range(4)], axis=1)
    row = lax.broadcasted_iota(jnp.int32, (4 * LANES, 4 * LANES), 0)
    return jnp.where(row == target, 1.0, 0.0).astype(BF)


def remote_pick(part, slot, width):
    near_even, dom_even = evens()
    near_block = jnp.where(near_even, part + 1, 4 - part)
    dom_block = jnp.where(dom_even, part - 3, 4 - part)
    block = jnp.where(part > 2, dom_block, near_block)
    target = jnp.where(part > 0, block * width + slot, -1)
    target = jnp.concatenate([target[i : i + 1, :] for i in range(4)], axis=1)
    row = lax.broadcasted_iota(jnp.int32, (4 * width, 4 * LANES), 0)
    return jnp.where(row == target, 1.0, 0.0).astype(BF)


def pick_faces(y_ref, base_row, table_ref, pick):
    for f in range(FIELDS):
        for j in range(4):
            table_ref[f * NPAD : (f + 1) * NPAD, j * LANES : (j + 1) * LANES] = y_ref[
                base_row + j * NPAD : base_row + (j + 1) * NPAD, field_lanes(f)
            ]
    high, low = two_parts(table_ref[...])
    return big_dot(high, pick) + big_dot(low, pick)


def flux_sum(values_of, flux_ref, emit):
    for first in range(0, FIELDS, 3):
        sums = [[None] * 4 for _ in range(3)]
        for i in range(4):
            for f in range(FIELDS):
                value = values_of(i, f)
                for k in range(3):
                    term = value * flux_ref[f, first + k, i : i + 1, :]
                    old = sums[k][i]
                    sums[k][i] = term if old is None else old + term
        for k in range(3):
            emit(first + k, jnp.concatenate(sums[k], axis=0))


def turn_masks(turn):
    masks = []
    for h in range(3):
        rows = [
            jnp.broadcast_to(jnp.where(turn[i : i + 1, :] == h, 1.0, 0.0), (NPAD, LANES))
            for i in range(4)
        ]
        masks.append(jnp.concatenate(rows, axis=0).astype(BF))
    return masks


def stack_own(z_ref, g, value):
    lanes = field_lanes(g)
    for piece, part in enumerate(two_parts(value)):
        z_ref[piece, 3 * FACES : 4 * FACES, lanes] = part


def stack_turned(z_ref, g, value, masks):
    lanes = field_lanes(g)
    for piece, part in enumerate(two_parts(value)):
        for h in range(3):
            z_ref[piece, h * FACES : (h + 1) * FACES, lanes] = part * masks[h]


def subtract_lift(lift_ref, rows, z_ref, base_ref, out_ref):
    both = lift_ref[:, 0:rows]
    for f in range(0, FIELDS, 2):
        fields = range(f, min(f + 2, FIELDS))
        lanes = slice(f * LANES, (fields[-1] + 1) * LANES)
        high = big_dot(both, z_ref[0, 0:rows, lanes])
        lifted = high[0:MODES] + high[MODES:] + big_dot(both[0:MODES], z_ref[1, 0:rows, lanes])
        for n, g in enumerate(fields):
            out_ref[field_rows(g), :] = base_ref[field_rows(g), :] - lifted[:, field_lanes(n)]


KINDS = 32
LARGE_ROW = 16


def slot_tables(
    far, part, face, turn, cluster, minus_ref, marks_ref, slot_flux_ref, scatter_ref,
    turned_ref, packed_scatter_ref,
):
    far2 = jnp.concatenate([far, far], axis=0)
    rows = [jnp.where(face == j, 1.0, 0.0) for j in range(4)]
    rows = [jnp.concatenate([row[i : i + 1, :] for i in range(4)], axis=1) for row in rows]
    none = jnp.zeros((1, LANES), F32)
    for h in range(3):
        turned = jnp.where(turn == h, 1.0, 0.0)
        for i in range(4):
            pieces = [none] * 4
            pieces[i] = turned[i : i + 1, :]
            rows.append(jnp.concatenate(pieces, axis=1))
    rows.append(jnp.concatenate([jnp.where(cluster == 0, 0.0, 1.0)] * 4, axis=1))
    kinds = tall(jnp.concatenate(rows, axis=0), KINDS).astype(BF)
    marks_ref[...] = nt_dot(kinds, far2)
    tiles = []
    for f in range(2 * PAIRS):
        if f < FIELDS:
            row = jnp.concatenate([minus_ref[f, :, i, :] for i in range(4)], axis=1)
            tiles.append(tall(row, DROWS))
        else:
            tiles.append(jnp.zeros((DROWS, 4 * LANES), F32))
    flux = jnp.concatenate(
        [jnp.concatenate(tiles[2 * j : 2 * j + 2], axis=1) for j in range(PAIRS)], axis=0
    )
    none = jnp.zeros_like(far)
    pick = jnp.concatenate(
        [jnp.concatenate([far, none], axis=1), jnp.concatenate([none, far], axis=1)], axis=0
    )
    high, low = two_parts(flux)
    slot_flux_ref[...] = nt_dot(high, pick) + nt_dot(low, pick)
    place = far[:, 0:LANES] + far[:, LANES : 2 * LANES]
    place = place + far[:, 2 * LANES : 3 * LANES] + far[:, 3 * LANES :]
    packed_scatter_ref[...] = packed_pick(place, turned_ref)
    none = jnp.zeros_like(place)
    scatter_ref[...] = jnp.concatenate(
        [jnp.concatenate([place, none], axis=1), jnp.concatenate([none, place], axis=1)], axis=0
    )


def packed_pick(pick, turned_ref):
    halves = [big_dot(pick, turned_ref[n * LANES : (n + 1) * LANES, :]) for n in range(2)]
    return jnp.concatenate(halves, axis=0).astype(BF)


def low_half(rows):
    return lax.broadcasted_iota(jnp.int32, (rows, LANES), 1) < MPAD


def slot_traces(received, pair_matrix, marks_ref):
    rims = jnp.concatenate([ref[...] for ref in received], axis=0)
    rims = jnp.concatenate([rims, rims], axis=0)
    rhs = []
    for q in range(PAIRS):
        high, low = two_parts(jnp.transpose(rims[:, field_lanes(q)]))
        rhs.append(jnp.concatenate([high, low, high], axis=0))
    traces = []
    for q in range(0, PAIRS, 2):
        out = big_dot(pair_matrix, jnp.concatenate(rhs[q : q + 2], axis=1))
        for n in range(min(2, PAIRS - q)):
            tile = out[:, field_lanes(n)]
            both = jnp.where(low_half(FACES), tile[0:FACES], tile[FACES:])
            total = None
            for j in range(4):
                term = both[j * NPAD : (j + 1) * NPAD, :] * marks_ref[j : j + 1, :]
                total = term if total is None else total + term
            traces.append(total)
    return traces


def join_halves(first, second):
    low = low_half(first.shape[0])
    same = jnp.where(low, first, second)
    other = jnp.where(low, second, first)
    return same + pltpu.roll(other, MPAD, 1)


def slot_lift(traces, slot_flux_ref, marks_ref, lift_ref, scatter_ref, z_ref, emit):
    masks = []
    for n in range(0, 12, 2):
        rows = [
            jnp.broadcast_to(marks_ref[4 + n + i : 5 + n + i, :], (NPAD, LANES)) for i in range(2)
        ]
        masks.append(jnp.concatenate(rows, axis=0).astype(BF))
    for j in range(PAIRS):
        sums = []
        for g in range(2 * j, 2 * j + 2):
            total = None
            if g < FIELDS:
                for i in range(PAIRS):
                    row = i * DROWS + g
                    term = traces[i] * slot_flux_ref[row : row + 1, :]
                    total = term if total is None else total + term
            else:
                total = jnp.zeros_like(traces[0])
            sums.append(total)
        value = join_halves(*sums)
        for piece, part in enumerate(two_parts(jnp.concatenate([value, value], axis=0))):
            for n in range(6):
                z_ref[piece, 2 * n * NPAD : 2 * (n + 1) * NPAD, field_lanes(j)] = part * masks[n]
    both = lift_ref[:, 0 : 3 * FACES]
    for j in range(0, PAIRS, 2):
        tiles = range(j, min(j + 2, PAIRS))
        lanes = slice(j * LANES, (tiles[-1] + 1) * LANES)
        high = big_dot(both, z_ref[0, :, lanes])
        lifted = high[0:MODES] + high[MODES:] + big_dot(both[0:MODES], z_ref[1, :, lanes])
        for n, tile in enumerate(tiles):
            high, low = two_parts(lifted[:, field_lanes(n)])
            count = min(scatter_ref.shape[1], (FIELDS - 2 * tile) * LANES)
            pick = scatter_ref[:, 0:count]
            emit(tile, big_dot(high, pick) + big_dot(low, pick))


def wide(x):
    return jnp.concatenate([x, jnp.zeros((x.shape[0], LANES - x.shape[1]), F32)], axis=1)


def tall(x, rows):
    return jnp.concatenate([x, jnp.zeros((rows - x.shape[0], x.shape[1]), F32)], axis=0)


def tripled(x):
    high, low = float_parts(x)
    first = high + pltpu.roll(high, MPAD, 1)
    return jnp.concatenate([first, low], axis=1).astype(BF)[:, 0 : 3 * MPAD]


def forward_matrix(stiff_ref):
    return tripled(jnp.concatenate([wide(stiff_ref[d]) for d in range(3)], axis=0))


def prepare(stiff_ref, lift_ref, project_ref, update_ref, lifts_ref, pair_ref, rows_ref):
    backward = [
        jnp.transpose(tall(wide(stiff_ref[d]), LANES))[0:MODES, :] for d in range(3)
    ]
    project = jnp.concatenate(
        [wide(tall(project_ref[:, j, :], NPAD)) for j in range(4)], axis=0
    )
    update_ref[...] = tripled(jnp.concatenate(backward + [project], axis=0))
    high, low = float_parts(project)
    moved = [pltpu.roll(part, MPAD, 1) for part in (high, low)]
    highs = jnp.concatenate([high, moved[0]], axis=0).astype(BF)
    lows = jnp.concatenate([low, moved[1]], axis=0).astype(BF)
    pair_ref[...] = jnp.concatenate([highs, highs, lows], axis=1)
    rows_ref[...] = jnp.zeros(rows_ref.shape, F32)
    tables = rotations()
    for block, h in enumerate((0, 1, 2, 0)):
        for i in range(4):
            for p in range(NODES):
                row = block * FACES + i * NPAD + int(tables[h][p])
                rows_ref[row : row + 1, 0:MODES] = lift_ref[p, i : i + 1, :]
    columns = []
    for t in range(4 * FACES // LANES):
        columns.append(jnp.transpose(rows_ref[t * LANES : (t + 1) * LANES, :])[0:MODES, :])
    high, low = float_parts(jnp.concatenate(columns, axis=1))
    lifts_ref[...] = jnp.concatenate([high, low], axis=0).astype(BF)


INPUTS = 13


def first_kernel(*refs):
    sources, rest = refs[:INPUTS], refs[INPUTS:]
    held, rest = rest[:INPUTS], rest[INPUTS:]
    first_ref, second_ref, forward_ref, s0, s1, s2, s3, xs_ref, y_ref, sems = rest
    copies = [
        pltpu.make_async_copy(source, target, sems.at[n])
        for n, (source, target) in enumerate(zip(sources, held))
    ]
    for copy in copies:
        copy.start()
    u_ref, star_ref, stiff_ref, halo_ref = held[:4]
    for copy in copies[:4]:
        copy.wait()
    forward_ref[...] = forward_matrix(stiff_ref)
    taylor(
        Steps(halo_ref), lambda f: u_ref[field_rows(f), :], star_ref, forward_ref, xs_ref, y_ref,
        [(first_ref, integral_weights(0.0, 0.5)), (second_ref, integral_weights(0.5, 1.0))],
    )
    for copy in copies[4:]:
        copy.wait()
    for f in range(FIELDS):
        put_operand(xs_ref, f, first_ref[field_rows(f), :])
    send_rims(xs_ref, send_pick(halo_ref), (s0, s1, s2, s3))


def middle_local_kernel(
    u_ref, first_ref, second_ref, star_ref, plus_ref, minus_ref, stiff_ref, face_lift_ref, project_ref,
    part_ref, slot_ref, face_ref, turn_ref, cluster_ref, halo_ref,
    start_ref, g_ref, marks_ref, update_ref, lift_ref, pair_ref, pack_ref, packed_ref,
    slot_flux_ref, scatter_ref, pick_ref, packed_scatter_ref, packed_send_ref, s0, s1, s2, s3,
    turned_ref, base_ref, xs_ref, y_ref, table_ref, z_ref, rows_ref,
):
    width = halo_ref.shape[1]
    prepare(stiff_ref, face_lift_ref, project_ref, update_ref, lift_ref, pair_ref, rows_ref)
    pack = pack_matrix(cluster_ref[...])
    pack_ref[...] = pack.astype(BF)
    turned_ref[...] = jnp.concatenate(
        [jnp.transpose(pack[:, 0:LANES]), jnp.transpose(pack[:, LANES:])], axis=0
    ).astype(BF)
    pack_star(star_ref, pack_ref, packed_ref)
    part, slot, face = part_ref[...], slot_ref[...], face_ref[...]
    for f in range(FIELDS):
        put_operand(xs_ref, f, first_ref[field_rows(f), :])
    wide_dot(update_ref[...], xs_ref, y_ref)
    pick_ref[...] = local_pick(part, slot, face)
    g_ref[...] = pick_faces(y_ref, 3 * MODES, table_ref, pick_ref[...])
    slot_tables(
        remote_pick(part, slot, width), part, face, turn_ref[...], cluster_ref[...], minus_ref,
        marks_ref, slot_flux_ref, scatter_ref, turned_ref, packed_scatter_ref,
    )
    finish_local(
        lambda f: u_ref[field_rows(f), :], star_ref, plus_ref, minus_ref, lift_ref,
        turn_ref[...], y_ref, g_ref, z_ref, base_ref,
    )
    pack_state(base_ref, turned_ref, start_ref)
    large = cluster_ref[...] != 0
    for f in range(FIELDS):
        put_operand(xs_ref, f, jnp.where(large, second_ref[field_rows(f), :], 0.0))
    pick = send_pick(halo_ref)
    send_rims(xs_ref, pick, (s0, s1, s2, s3))
    packed_send_ref[...] = packed_pick(pick, turned_ref)


def finish_local(base_of, star_ref, plus_ref, minus_ref, lift_ref, turn, y_ref, g_ref, z_ref, base_ref):
    masks = turn_masks(turn)
    top = 3 * MODES
    flux_sum(
        lambda i, f: y_ref[top + i * NPAD : top + (i + 1) * NPAD, field_lanes(f)],
        plus_ref,
        lambda g, value: stack_own(z_ref, g, value),
    )
    flux_sum(
        lambda i, f: g_ref[f * NPAD : (f + 1) * NPAD, i * LANES : (i + 1) * LANES],
        minus_ref,
        lambda g, value: stack_turned(z_ref, g, value, masks),
    )

    def emit(g, value):
        base_ref[field_rows(g), :] = base_of(g) + value

    star_sum(y_ref, star_ref, emit)
    subtract_lift(lift_ref, 4 * FACES, z_ref, base_ref, base_ref)


def middle_remote_kernel(
    r0, r1, r2, r3, start_ref, star_ref, slot_flux_ref, scatter_ref, forward_ref, lift_ref, pair_ref,
    marks_ref, pick_ref, l0, l1, l2, l3,
    middle_ref, sum_ref, traces_ref, s0, s1, s2, s3,
    xp_ref, y_ref, z_ref,
):
    weights = integral_weights(0.0, 0.5)
    traces = slot_traces((r0, r1, r2, r3), pair_ref[...], marks_ref)
    traces_ref[...] = jnp.concatenate(traces, axis=0)

    def take(j, lifted):
        rows = field_rows(j)
        value = start_ref[rows, :] - lifted
        middle_ref[rows, :] = value
        sum_ref[rows, :] = weights[0] * value
        put_operand(xp_ref, j, value)

    slot_lift(traces, slot_flux_ref, marks_ref, lift_ref, scatter_ref, z_ref, take)
    packed_taylor(star_ref, forward_ref[...], xp_ref, y_ref, sum_ref, weights)
    send_packed(sum_ref, pick_ref[...], (l0, l1, l2, l3), (s0, s1, s2, s3))


def last_local_kernel(
    u_ref, packed_middle_ref, first_ref, second_ref, packed_later_ref, gfirst_ref, star_ref, plus_ref,
    minus_ref, update_ref, lift_ref, pick_ref, turn_ref, cluster_ref, pack_ref,
    base_ref, xs_ref, y_ref, table_ref, z_ref, g_ref, middle_ref, later_ref,
):
    small = cluster_ref[...] == 0

    def choose(target, other):
        def emit(f, value):
            rows = field_rows(f)
            target[rows, :] = jnp.where(small, value, other[rows, :])

        return emit

    unpack(packed_later_ref, pack_ref, choose(later_ref, second_ref))
    unpack(packed_middle_ref, pack_ref, choose(middle_ref, u_ref))
    for f in range(FIELDS):
        put_operand(xs_ref, f, later_ref[field_rows(f), :])
    wide_dot(update_ref[3 * MODES :, :], xs_ref, y_ref)
    near = pick_faces(y_ref, 0, table_ref, pick_ref[...])
    large4 = jnp.concatenate([jnp.where(small, 0.0, 1.0)] * 4, axis=1)
    g_ref[...] = near + gfirst_ref[...] * large4
    for f in range(FIELDS):
        rows = field_rows(f)
        put_operand(
            xs_ref, f, jnp.where(small, later_ref[rows, :], first_ref[rows, :] + second_ref[rows, :])
        )
    wide_dot(update_ref[...], xs_ref, y_ref)
    finish_local(
        lambda f: middle_ref[field_rows(f), :],
        star_ref, plus_ref, minus_ref, lift_ref, turn_ref[...], y_ref, g_ref, z_ref, base_ref,
    )


def last_remote_kernel(
    r0, r1, r2, r3, base_ref, traces_ref, slot_flux_ref, scatter_ref, lift_ref, pair_ref, marks_ref,
    out_hbm, z_ref, done_ref, sems,
):
    large = marks_ref[LARGE_ROW : LARGE_ROW + 1, :]
    traces = slot_traces((r0, r1, r2, r3), pair_ref[...], marks_ref)
    for j in range(PAIRS):
        traces[j] = traces[j] + traces_ref[j * NPAD : (j + 1) * NPAD, :] * large
    copies = []

    def emit(tile, lifted):
        for k in range(lifted.shape[1] // LANES):
            rows = field_rows(2 * tile + k)
            done_ref[rows, :] = base_ref[rows, :] - lifted[:, field_lanes(k)]
            copy = pltpu.make_async_copy(
                done_ref.at[rows, :], out_hbm.at[rows, :], sems.at[2 * tile + k]
            )
            copy.start()
            copies.append(copy)

    slot_lift(traces, slot_flux_ref, marks_ref, lift_ref, scatter_ref, z_ref, emit)
    for copy in copies:
        copy.wait()


STATE = (FIELDS * MODES, LANES)
GATHERED = (FIELDS * NPAD, 4 * LANES)


def call(kernel, inputs, outs, scratch, name, space=pltpu.VMEM, out_space=pltpu.VMEM):
    out_shape = [jax.ShapeDtypeStruct(shape, kind) for shape, kind in outs]
    return pl.pallas_call(
        kernel,
        out_shape=out_shape,
        in_specs=[pl.BlockSpec(memory_space=space)] * len(inputs),
        out_specs=[pl.BlockSpec(memory_space=out_space)] * len(out_shape),
        scratch_shapes=scratch,
        compiler_params=pltpu.CompilerParams(vmem_limit_bytes=24 << 20),
        cost_estimate=pl.CostEstimate(flops=10**9, bytes_accessed=10**6, transcendentals=0),
        name=name,
    )(*inputs)


def scratch_xs():
    return pltpu.VMEM((3 * MPAD, FIELDS * LANES), BF)


def scratch_y(rows):
    return pltpu.VMEM((rows, FIELDS * LANES), F32)


def scratch_slots():
    return pltpu.VMEM((2, 3 * FACES, PAIRS * LANES), BF)


def scratch_z(rows):
    return pltpu.VMEM((2, rows, FIELDS * LANES), BF)


def swap(x, axis, kind):
    count = lax.axis_size(axis)
    pairs = []
    for a in range(kind, count, 2):
        b = (a + 1) % count
        pairs += [(a, b), (b, a)]
    return lax.ppermute(x, axis, pairs)


def trade(sends):
    return [
        swap(send, axis, kind)
        for send, (axis, kind) in zip(sends, (("dom", 1), ("dom", 0), ("near", 1), ("near", 0)))
    ]


def on_device(
    u, star, plus, minus, stiffness, face_lift, face_project,
    cluster, part, slot, face, turn, halo,
):
    width = halo.shape[1]
    u = jnp.transpose(u, (1, 0, 2)).reshape(STATE)
    star, plus, minus = [jnp.transpose(x, (1, 2, 0, 3)) for x in (star, plus, minus)]
    face_lift = jnp.transpose(face_lift, (2, 0, 1))
    face_project = jnp.transpose(face_project, (1, 0, 2))
    state, gathered = (STATE, F32), (GATHERED, F32)
    rims = [((width, 5 * LANES), F32)] * 4
    update_rows = 3 * MODES + FACES
    inputs = (
        u, star, stiffness, halo, plus, minus, face_lift, face_project,
        part, slot, face, turn, cluster.reshape(1, LANES),
    )
    inputs = [pltpu.with_memory_space_constraint(x, pltpu.HBM) for x in inputs]
    *held, first, second, forward, s0, s1, s2, s3 = call(
        first_kernel, inputs,
        [(x.shape, x.dtype) for x in inputs]
        + [state, state, ((3 * MODES, 3 * MPAD), BF)] + rims,
        [scratch_xs(), scratch_y(3 * MODES), pltpu.SemaphoreType.DMA((INPUTS,))], "first",
        pltpu.HBM,
    )
    u, star, stiffness, halo, plus, minus, face_lift, face_project = held[:8]
    part, slot, face, turn, cluster = held[8:]
    sends = s0, s1, s2, s3
    received = trade(sends)
    packed_state = ((PAIRS * MODES, LANES), F32)
    square, tall_square = ((LANES, LANES), BF), ((LANES, 2 * LANES), BF)
    (
        start, g, marks, update, lift, pair, pack, packed, slot_flux, scatter, pick,
        packed_scatter, packed_send, *large_sends,
    ) = call(
        middle_local_kernel,
        (
            u, first, second, star, plus, minus, stiffness, face_lift, face_project,
            part, slot, face, turn, cluster, halo,
        ),
        [
            packed_state, gathered, ((KINDS, LANES), F32), ((update_rows, 3 * MPAD), BF),
            ((2 * MODES, 4 * FACES), BF), ((2 * FACES, 3 * LANES), BF),
            tall_square, ((PAIRS, 3 * DROWS, LANES), F32),
            ((PAIRS * DROWS, LANES), F32), tall_square, ((4 * LANES, 4 * LANES), BF),
            square, square,
        ] + rims,
        [
            pltpu.VMEM((2 * LANES, LANES), BF), pltpu.VMEM(STATE, F32),
            scratch_xs(), scratch_y(update_rows), pltpu.VMEM(GATHERED, F32), scratch_z(4 * FACES),
            pltpu.VMEM((4 * FACES, LANES), F32),
        ],
        "middle_local",
    )
    middle, later, traces, *sends = call(
        middle_remote_kernel,
        (
            *received, start, packed, slot_flux, packed_scatter, forward, lift, pair, marks,
            packed_send, *large_sends,
        ),
        [packed_state, packed_state, ((PAIRS * NPAD, LANES), F32)] + rims,
        [
            pltpu.VMEM((3 * MPAD, PAIRS * LANES), BF), pltpu.VMEM((3 * MODES, PAIRS * LANES), F32),
            scratch_slots(),
        ],
        "middle_remote",
    )
    received = trade(sends)
    (base,) = call(
        last_local_kernel,
        (
            u, middle, first, second, later, g, star, plus, minus, update, lift,
            pick, turn, cluster, pack,
        ),
        [state],
        [
            scratch_xs(), scratch_y(update_rows), pltpu.VMEM(GATHERED, F32), scratch_z(4 * FACES),
            pltpu.VMEM(GATHERED, F32), pltpu.VMEM(STATE, F32), pltpu.VMEM(STATE, F32),
        ],
        "last_local",
    )
    (out,) = call(
        last_remote_kernel,
        (*received, base, traces, slot_flux, scatter, lift, pair, marks),
        [state],
        [scratch_slots(), pltpu.VMEM(STATE, F32), pltpu.SemaphoreType.DMA((FIELDS,))],
        "last_remote", out_space=pltpu.HBM,
    )
    return jnp.transpose(out.reshape(FIELDS, MODES, LANES), (1, 0, 2))


def solution(mesh):
    both = ("dom", "near")
    in_specs = (
        P(None, None, both), P(None, None, None, both), P(None, None, None, both),
        P(None, None, None, both), P(), P(), P(), P(both),
        P(None, both), P(None, both), P(None, both), P(None, both), P(None, both),
    )
    return jax.shard_map(
        on_device, mesh=mesh, in_specs=in_specs, out_specs=P(None, None, both), check_vma=False
    )
```

```python
import functools
import math

import jax
import jax.numpy as jnp
import numpy as np
from jax import lax
from jax.experimental import pallas as pl
from jax.experimental.pallas import tpu as pltpu
from jax.sharding import PartitionSpec as P

MODES = 56
FIELDS = 9
NODES = 21
ORDER = 6
MPAD = 64
NPAD = 24
LANES = 128
FACES = 4 * NPAD
BF = jnp.bfloat16
F32 = jnp.float32


def rotations():
    degree = ORDER - 1
    nodes = [(a, b) for a in range(degree + 1) for b in range(degree + 1 - a)]
    lookup = {point: number for number, point in enumerate(nodes)}
    tables = []
    for rotation in range(3):
        row = []
        for a, b in nodes:
            triple = (a, b, degree - a - b)
            rolled = triple[rotation:] + triple[:rotation]
            row.append(lookup[rolled[0], rolled[1]])
        tables.append(row)
    return np.array(tables, dtype=np.int32)


def integral_weights(begin, end):
    return [(end ** (k + 1) - begin ** (k + 1)) / math.factorial(k + 1) for k in range(ORDER)]


def two_parts(x):
    high = x.astype(BF)
    low = (x - high.astype(F32)).astype(BF)
    return high, low


def float_parts(x):
    high = x.astype(BF).astype(F32)
    return high, x - high


def field_lanes(f):
    return slice(f * LANES, (f + 1) * LANES)


def field_rows(f):
    return slice(f * MODES, (f + 1) * MODES)


def put_operand(xs_ref, f, x):
    x = jnp.concatenate([x, jnp.zeros((MPAD - MODES, LANES), F32)], axis=0)
    high, low = two_parts(x)
    lanes = field_lanes(f)
    xs_ref[0:MPAD, lanes] = high
    xs_ref[MPAD : 2 * MPAD, lanes] = low
    xs_ref[2 * MPAD : 3 * MPAD, lanes] = high


def big_dot(lhs, rhs):
    return jnp.dot(lhs, rhs, preferred_element_type=F32)


def wide_dot(lhs, xs_ref, y_ref):
    rows = lhs.shape[0]
    for f in range(0, FIELDS, 2):
        lanes = slice(f * LANES, min(f + 2, FIELDS) * LANES)
        y_ref[0:rows, lanes] = big_dot(lhs, xs_ref[:, lanes])


def star_sum(y_ref, star_ref, emit):
    for first in range(0, FIELDS, 3):
        sums = [None] * 3
        for d in range(3):
            for f in range(FIELDS):
                y = y_ref[d * MODES : (d + 1) * MODES, field_lanes(f)]
                for k in range(3):
                    scale = star_ref[f, first + k, d : d + 1, :]
                    term = y * scale
                    sums[k] = term if sums[k] is None else sums[k] + term
        for k in range(3):
            emit(first + k, sums[k])


GROUP = 3


class Steps:
    def __init__(self, halo_ref):
        self.value = halo_ref[0, 0]
        self.bound = 4096

    def __call__(self, body):
        self.bound += 1
        pl.when(self.value < self.bound)(body)


def star_group(y_ref, star_ref, first, emit, order):
    sums = [None] * GROUP
    for f in order:
        for d in range(3):
            y = y_ref[d * MODES : (d + 1) * MODES, field_lanes(f)]
            for k in range(GROUP):
                term = y * star_ref[f, first + k, d : d + 1, :]
                sums[k] = term if sums[k] is None else sums[k] + term
    for k in range(GROUP):
        emit(first + k, sums[k])


def taylor(block, start_of, star_ref, forward_ref, xs_ref, ys, integrals, star_ready):
    def start():
        for f in range(FIELDS):
            value = start_of(f)
            put_operand(xs_ref, f, value)
            for ref, weights in integrals:
                ref[field_rows(f), :] = weights[0] * value

    def step(k, n):
        y_ref = ys[k % 2]

        def emit(g, value):
            if k < ORDER - 1:
                put_operand(xs_ref, g, value)
            for ref, weights in integrals:
                ref[field_rows(g), :] = ref[field_rows(g), :] + weights[k] * value

        if n == 0:
            wide_dot(forward_ref[...], xs_ref, y_ref)
        star_group(y_ref, star_ref, n * GROUP, emit, range(FIELDS))

    block(start)
    star_ready()
    block(functools.partial(step, 1, 0))
    for k in range(1, ORDER):

        def rest(k=k):
            step(k, 1)
            step(k, 2)
            if k < ORDER - 1:
                step(k + 1, 0)

        block(rest)


PAIRS = (FIELDS + 1) // 2
DROWS = 16


def nt_dot(lhs, rhs):
    return lax.dot_general(lhs, rhs, (((1,), (1,)), ((), ())), preferred_element_type=F32)


def pair_lanes(j):
    return slice(2 * j * LANES, min(2 * j + 2, FIELDS) * LANES)


def pack_matrix(cluster):
    small = jnp.where(cluster == 0, 1.0, 0.0)
    before = lax.broadcasted_iota(jnp.int32, (LANES, LANES), 0)
    after = lax.broadcasted_iota(jnp.int32, (LANES, LANES), 1)
    upper = jnp.where(before < after, 1.0, 0.0).astype(BF)
    place = big_dot(jnp.broadcast_to(small, (8, LANES)).astype(BF), upper)[0:1, :]
    place = jnp.where(cluster == 0, place, -1.0).astype(jnp.int32)
    row = lax.broadcasted_iota(jnp.int32, (MPAD, LANES), 0)
    pick = jnp.where(row == place, 1.0, 0.0)
    none = jnp.zeros_like(pick)
    return jnp.concatenate(
        [jnp.concatenate([pick, none], axis=1), jnp.concatenate([none, pick], axis=1)], axis=0
    )


def pack_star(star_ref, pack_ref, packed_ref):
    pad = jnp.zeros((DROWS - FIELDS, LANES), F32)
    rows = []
    for f in range(FIELDS):
        parts = []
        for d in range(3):
            parts += [star_ref[f, :, d, :], pad]
        rows.append(jnp.concatenate(parts, axis=0))
    for j in range(PAIRS):
        both = jnp.concatenate(rows[2 * j : 2 * j + 2], axis=1)
        pick = pack_ref[:, 0 : both.shape[1]]
        high, low = two_parts(both)
        packed_ref[j] = nt_dot(high, pick) + nt_dot(low, pick)


def packed_taylor(xs_ref, turned_ref, star_ref, forward, xp_ref, y_ref, sum_ref, weights):
    for j in range(PAIRS):
        lanes = pair_lanes(j)
        pick = turned_ref[0 : lanes.stop - lanes.start, :]
        value = big_dot(xs_ref[0:MPAD, lanes], pick) + big_dot(xs_ref[MPAD : 2 * MPAD, lanes], pick)
        value = value[0:MODES]
        put_operand(xp_ref, j, value)
        sum_ref[field_rows(j), :] = weights[0] * value
    for k in range(1, ORDER):
        for j in range(0, PAIRS, 2):
            lanes = slice(j * LANES, min(j + 2, PAIRS) * LANES)
            y_ref[:, lanes] = big_dot(forward, xp_ref[:, lanes])
        for j in range(PAIRS):
            sums = []
            for g in range(2 * j, min(2 * j + 2, FIELDS)):
                total = None
                for i in range(PAIRS):
                    for d in range(3):
                        y = y_ref[d * MODES : (d + 1) * MODES, field_lanes(i)]
                        term = y * star_ref[i, d * DROWS + g : d * DROWS + g + 1, :]
                        total = term if total is None else total + term
                sums.append(total)
            if len(sums) == 1:
                sums.append(jnp.zeros_like(sums[0]))
            value = join_halves(*sums)
            if k < ORDER - 1:
                put_operand(xp_ref, j, value)
            sum_ref[field_rows(j), :] = sum_ref[field_rows(j), :] + weights[k] * value


def unpack(sum_ref, pack_ref, emit):
    for j in range(PAIRS):
        high, low = two_parts(sum_ref[field_rows(j), :])
        pick = pack_ref[:, 0 : min(2, FIELDS - 2 * j) * LANES]
        value = big_dot(high, pick) + big_dot(low, pick)
        for n in range(min(2, FIELDS - 2 * j)):
            emit(2 * j + n, value[:, field_lanes(n)])


def evens():
    return [lax.rem(lax.axis_index(axis), 2) == 0 for axis in ("near", "dom")]


def send_rims(xs_ref, halo_ref, sends):
    width = halo_ref.shape[1]
    element = lax.broadcasted_iota(jnp.int32, (LANES, width), 0)
    near_even, dom_even = evens()
    picks = []
    for even, first in ((dom_even, 2), (near_even, 0)):
        up, down = halo_ref[first : first + 1, :], halo_ref[first + 1 : first + 2, :]
        for row in (jnp.where(even, down, up), jnp.where(even, up, down)):
            pick = jnp.where(element == row, 1.0, 0.0).astype(F32)
            picks.append(jnp.transpose(pick))
    pick = jnp.concatenate(picks, axis=0).astype(BF)
    for q in range((FIELDS + 1) // 2):
        fields = (2 * q, min(2 * q + 1, FIELDS - 1))
        total = None
        for piece in range(2):
            rows = slice(piece * MPAD, (piece + 1) * MPAD)
            both = jnp.concatenate([xs_ref[rows, field_lanes(f)] for f in fields], axis=0)
            part = lax.dot_general(
                pick, both, (((1,), (1,)), ((), ())), preferred_element_type=F32
            )
            total = part if total is None else total + part
        for r in range(4):
            sends[r][:, field_lanes(q)] = total[r * width : (r + 1) * width, :]


def local_pick(part, slot, face):
    target = jnp.where(part == 0, face * LANES + slot, -1)
    target = jnp.concatenate([target[i : i + 1, :] for i in range(4)], axis=1)
    row = lax.broadcasted_iota(jnp.int32, (4 * LANES, 4 * LANES), 0)
    return jnp.where(row == target, 1.0, 0.0).astype(BF)


def remote_pick(part, slot, width):
    near_even, dom_even = evens()
    near_block = jnp.where(near_even, part + 1, 4 - part)
    dom_block = jnp.where(dom_even, part - 3, 4 - part)
    block = jnp.where(part > 2, dom_block, near_block)
    target = jnp.where(part > 0, block * width + slot, -1)
    target = jnp.concatenate([target[i : i + 1, :] for i in range(4)], axis=1)
    row = lax.broadcasted_iota(jnp.int32, (4 * width, 4 * LANES), 0)
    return jnp.where(row == target, 1.0, 0.0).astype(BF)


def pick_faces(y_ref, base_row, table_ref, pick):
    for f in range(FIELDS):
        for j in range(4):
            table_ref[f * NPAD : (f + 1) * NPAD, j * LANES : (j + 1) * LANES] = y_ref[
                base_row + j * NPAD : base_row + (j + 1) * NPAD, field_lanes(f)
            ]
    high, low = two_parts(table_ref[...])
    return big_dot(high, pick) + big_dot(low, pick)


def flux_sum(values_of, flux_ref, emit):
    for first in range(0, FIELDS, 3):
        sums = [[None] * 4 for _ in range(3)]
        for i in range(4):
            for f in range(FIELDS):
                value = values_of(i, f)
                for k in range(3):
                    term = value * flux_ref[f, first + k, i : i + 1, :]
                    old = sums[k][i]
                    sums[k][i] = term if old is None else old + term
        for k in range(3):
            emit(first + k, jnp.concatenate(sums[k], axis=0))


def turn_masks(turn):
    masks = []
    for h in range(3):
        rows = [
            jnp.broadcast_to(jnp.where(turn[i : i + 1, :] == h, 1.0, 0.0), (NPAD, LANES))
            for i in range(4)
        ]
        masks.append(jnp.concatenate(rows, axis=0).astype(BF))
    return masks


def stack_own(z_ref, g, value):
    lanes = field_lanes(g)
    for piece, part in enumerate(two_parts(value)):
        z_ref[piece, 3 * FACES : 4 * FACES, lanes] = part


def stack_turned(z_ref, g, value, masks):
    lanes = field_lanes(g)
    for piece, part in enumerate(two_parts(value)):
        for h in range(3):
            z_ref[piece, h * FACES : (h + 1) * FACES, lanes] = part * masks[h]


def subtract_lift(lift_ref, rows, z_ref, base_ref, out_ref):
    both = lift_ref[:, 0:rows]
    for f in range(0, FIELDS, 2):
        fields = range(f, min(f + 2, FIELDS))
        lanes = slice(f * LANES, (fields[-1] + 1) * LANES)
        high = big_dot(both, z_ref[0, 0:rows, lanes])
        lifted = high[0:MODES] + high[MODES:] + big_dot(both[0:MODES], z_ref[1, 0:rows, lanes])
        for n, g in enumerate(fields):
            out_ref[field_rows(g), :] = base_ref[field_rows(g), :] - lifted[:, field_lanes(n)]


KINDS = 32
LARGE_ROW = 16


def slot_tables(far, part, face, turn, cluster, minus_ref, marks_ref, slot_flux_ref, scatter_ref):
    far2 = jnp.concatenate([far, far], axis=0)
    rows = [jnp.where(face == j, 1.0, 0.0) for j in range(4)]
    rows = [jnp.concatenate([row[i : i + 1, :] for i in range(4)], axis=1) for row in rows]
    none = jnp.zeros((1, LANES), F32)
    for h in range(3):
        turned = jnp.where(turn == h, 1.0, 0.0)
        for i in range(4):
            pieces = [none] * 4
            pieces[i] = turned[i : i + 1, :]
            rows.append(jnp.concatenate(pieces, axis=1))
    rows.append(jnp.concatenate([jnp.where(cluster == 0, 0.0, 1.0)] * 4, axis=1))
    kinds = tall(jnp.concatenate(rows, axis=0), KINDS).astype(BF)
    marks_ref[...] = nt_dot(kinds, far2)
    tiles = []
    for f in range(2 * PAIRS):
        if f < FIELDS:
            row = jnp.concatenate([minus_ref[f, :, i, :] for i in range(4)], axis=1)
            tiles.append(tall(row, DROWS))
        else:
            tiles.append(jnp.zeros((DROWS, 4 * LANES), F32))
    flux = jnp.concatenate(
        [jnp.concatenate(tiles[2 * j : 2 * j + 2], axis=1) for j in range(PAIRS)], axis=0
    )
    none = jnp.zeros_like(far)
    pick = jnp.concatenate(
        [jnp.concatenate([far, none], axis=1), jnp.concatenate([none, far], axis=1)], axis=0
    )
    high, low = two_parts(flux)
    slot_flux_ref[...] = nt_dot(high, pick) + nt_dot(low, pick)
    place = far[:, 0:LANES] + far[:, LANES : 2 * LANES]
    place = place + far[:, 2 * LANES : 3 * LANES] + far[:, 3 * LANES :]
    none = jnp.zeros_like(place)
    scatter_ref[...] = jnp.concatenate(
        [jnp.concatenate([place, none], axis=1), jnp.concatenate([none, place], axis=1)], axis=0
    )


def low_half(rows):
    return lax.broadcasted_iota(jnp.int32, (rows, LANES), 1) < MPAD


def slot_traces(received, pair_matrix, marks_ref):
    rims = jnp.concatenate([ref[...] for ref in received], axis=0)
    rims = jnp.concatenate([rims, rims], axis=0)
    rhs = []
    for q in range(PAIRS):
        high, low = two_parts(jnp.transpose(rims[:, field_lanes(q)]))
        rhs.append(jnp.concatenate([high, low, high], axis=0))
    traces = []
    for q in range(0, PAIRS, 2):
        out = big_dot(pair_matrix, jnp.concatenate(rhs[q : q + 2], axis=1))
        for n in range(min(2, PAIRS - q)):
            tile = out[:, field_lanes(n)]
            both = jnp.where(low_half(FACES), tile[0:FACES], tile[FACES:])
            total = None
            for j in range(4):
                term = both[j * NPAD : (j + 1) * NPAD, :] * marks_ref[j : j + 1, :]
                total = term if total is None else total + term
            traces.append(total)
    return traces


def join_halves(first, second):
    low = low_half(first.shape[0])
    same = jnp.where(low, first, second)
    other = jnp.where(low, second, first)
    return same + pltpu.roll(other, MPAD, 1)


def slot_lift(traces, slot_flux_ref, marks_ref, lift_ref, scatter_ref, z_ref, emit):
    masks = []
    for n in range(0, 12, 2):
        rows = [
            jnp.broadcast_to(marks_ref[4 + n + i : 5 + n + i, :], (NPAD, LANES)) for i in range(2)
        ]
        masks.append(jnp.concatenate(rows, axis=0).astype(BF))
    for j in range(PAIRS):
        sums = []
        for g in range(2 * j, 2 * j + 2):
            total = None
            if g < FIELDS:
                for i in range(PAIRS):
                    row = i * DROWS + g
                    term = traces[i] * slot_flux_ref[row : row + 1, :]
                    total = term if total is None else total + term
            else:
                total = jnp.zeros_like(traces[0])
            sums.append(total)
        value = join_halves(*sums)
        for piece, part in enumerate(two_parts(jnp.concatenate([value, value], axis=0))):
            for n in range(6):
                z_ref[piece, 2 * n * NPAD : 2 * (n + 1) * NPAD, field_lanes(j)] = part * masks[n]
    both = lift_ref[:, 0 : 3 * FACES]
    for j in range(0, PAIRS, 2):
        tiles = range(j, min(j + 2, PAIRS))
        lanes = slice(j * LANES, (tiles[-1] + 1) * LANES)
        high = big_dot(both, z_ref[0, :, lanes])
        lifted = high[0:MODES] + high[MODES:] + big_dot(both[0:MODES], z_ref[1, :, lanes])
        for n, tile in enumerate(tiles):
            high, low = two_parts(lifted[:, field_lanes(n)])
            count = min(2, FIELDS - 2 * tile)
            pick = scatter_ref[:, 0 : count * LANES]
            value = big_dot(high, pick) + big_dot(low, pick)
            for k in range(count):
                emit(2 * tile + k, value[:, field_lanes(k)])


def wide(x):
    return jnp.concatenate([x, jnp.zeros((x.shape[0], LANES - x.shape[1]), F32)], axis=1)


def tall(x, rows):
    return jnp.concatenate([x, jnp.zeros((rows - x.shape[0], x.shape[1]), F32)], axis=0)


def tripled(x):
    high, low = float_parts(x)
    first = high + pltpu.roll(high, MPAD, 1)
    return jnp.concatenate([first, low], axis=1).astype(BF)[:, 0 : 3 * MPAD]


def forward_matrix(stiff_ref):
    return tripled(jnp.concatenate([wide(stiff_ref[d]) for d in range(3)], axis=0))


def prepare(stiff_ref, lift_ref, project_ref, update_ref, lifts_ref, pair_ref, rows_ref):
    backward = [
        jnp.transpose(tall(wide(stiff_ref[d]), LANES))[0:MODES, :] for d in range(3)
    ]
    project = jnp.concatenate(
        [wide(tall(project_ref[:, j, :], NPAD)) for j in range(4)], axis=0
    )
    update_ref[...] = tripled(jnp.concatenate(backward + [project], axis=0))
    high, low = float_parts(project)
    moved = [pltpu.roll(part, MPAD, 1) for part in (high, low)]
    highs = jnp.concatenate([high, moved[0]], axis=0).astype(BF)
    lows = jnp.concatenate([low, moved[1]], axis=0).astype(BF)
    pair_ref[...] = jnp.concatenate([highs, highs, lows], axis=1)
    rows_ref[...] = jnp.zeros(rows_ref.shape, F32)
    tables = rotations()
    for block, h in enumerate((0, 1, 2, 0)):
        for i in range(4):
            for p in range(NODES):
                row = block * FACES + i * NPAD + int(tables[h][p])
                rows_ref[row : row + 1, 0:MODES] = lift_ref[p, i : i + 1, :]
    columns = []
    for t in range(4 * FACES // LANES):
        columns.append(jnp.transpose(rows_ref[t * LANES : (t + 1) * LANES, :])[0:MODES, :])
    high, low = float_parts(jnp.concatenate(columns, axis=1))
    lifts_ref[...] = jnp.concatenate([high, low], axis=0).astype(BF)


INPUTS = 13


def first_kernel(*refs):
    sources, rest = refs[:INPUTS], refs[INPUTS:]
    held, rest = rest[:INPUTS], rest[INPUTS:]
    first_ref, second_ref, forward_ref, s0, s1, s2, s3, xs_ref, y_ref, y2_ref, sems = rest
    copies = [
        pltpu.make_async_copy(source, target, sems.at[n])
        for n, (source, target) in enumerate(zip(sources, held))
    ]
    for n in (0, 2, 3, 1, *range(4, INPUTS)):
        copies[n].start()
    u_ref, star_ref, stiff_ref, halo_ref = held[:4]
    for n in (0, 2, 3):
        copies[n].wait()
    forward_ref[...] = forward_matrix(stiff_ref)
    taylor(
        Steps(halo_ref), lambda f: u_ref[field_rows(f), :], star_ref, forward_ref, xs_ref, (y_ref, y2_ref),
        [(first_ref, integral_weights(0.0, 0.5)), (second_ref, integral_weights(0.5, 1.0))],
        copies[1].wait,
    )
    for copy in copies[4:]:
        copy.wait()
    for f in range(FIELDS):
        put_operand(xs_ref, f, first_ref[field_rows(f), :])
    send_rims(xs_ref, halo_ref, (s0, s1, s2, s3))


def middle_local_kernel(
    u_ref, first_ref, star_ref, plus_ref, minus_ref, stiff_ref, face_lift_ref, project_ref,
    part_ref, slot_ref, face_ref, turn_ref, cluster_ref, halo_ref,
    base_ref, g_ref, marks_ref, update_ref, lift_ref, pair_ref, pack_ref, packed_ref,
    slot_flux_ref, scatter_ref, pick_ref, turned_ref,
    xs_ref, y_ref, table_ref, z_ref, rows_ref,
):
    width = halo_ref.shape[1]
    prepare(stiff_ref, face_lift_ref, project_ref, update_ref, lift_ref, pair_ref, rows_ref)
    pack = pack_matrix(cluster_ref[...])
    pack_ref[...] = pack.astype(BF)
    turned_ref[...] = jnp.concatenate(
        [jnp.transpose(pack[:, 0:LANES]), jnp.transpose(pack[:, LANES:])], axis=0
    ).astype(BF)
    pack_star(star_ref, pack_ref, packed_ref)
    part, slot, face = part_ref[...], slot_ref[...], face_ref[...]
    for f in range(FIELDS):
        put_operand(xs_ref, f, first_ref[field_rows(f), :])
    wide_dot(update_ref[...], xs_ref, y_ref)
    pick_ref[...] = local_pick(part, slot, face)
    g_ref[...] = pick_faces(y_ref, 3 * MODES, table_ref, pick_ref[...])
    slot_tables(
        remote_pick(part, slot, width), part, face, turn_ref[...], cluster_ref[...], minus_ref,
        marks_ref, slot_flux_ref, scatter_ref,
    )
    finish_local(
        lambda f: u_ref[field_rows(f), :], star_ref, plus_ref, minus_ref, lift_ref,
        turn_ref[...], y_ref, g_ref, z_ref, base_ref,
    )


def finish_local(base_of, star_ref, plus_ref, minus_ref, lift_ref, turn, y_ref, g_ref, z_ref, base_ref):
    masks = turn_masks(turn)
    top = 3 * MODES
    flux_sum(
        lambda i, f: y_ref[top + i * NPAD : top + (i + 1) * NPAD, field_lanes(f)],
        plus_ref,
        lambda g, value: stack_own(z_ref, g, value),
    )
    flux_sum(
        lambda i, f: g_ref[f * NPAD : (f + 1) * NPAD, i * LANES : (i + 1) * LANES],
        minus_ref,
        lambda g, value: stack_turned(z_ref, g, value, masks),
    )

    def emit(g, value):
        base_ref[field_rows(g), :] = base_of(g) + value

    star_sum(y_ref, star_ref, emit)
    subtract_lift(lift_ref, 4 * FACES, z_ref, base_ref, base_ref)


def middle_remote_kernel(
    r0, r1, r2, r3, u_ref, base_ref, second_ref, star_ref, slot_flux_ref, scatter_ref,
    forward_ref, lift_ref, pair_ref, marks_ref, cluster_ref, halo_ref, pack_ref, turned_ref,
    middle_ref, later_ref, traces_ref, s0, s1, s2, s3,
    xs_ref, xp_ref, y_ref, sum_ref, z_ref,
):
    small = cluster_ref[...] == 0
    traces = slot_traces((r0, r1, r2, r3), pair_ref[...], marks_ref)
    traces_ref[...] = jnp.concatenate(traces, axis=0)

    def take(f, lifted):
        value = base_ref[field_rows(f), :] - lifted
        value = jnp.where(small, value, u_ref[field_rows(f), :])
        middle_ref[field_rows(f), :] = value
        put_operand(xs_ref, f, value)

    slot_lift(traces, slot_flux_ref, marks_ref, lift_ref, scatter_ref, z_ref, take)
    packed_taylor(
        xs_ref, turned_ref, star_ref, forward_ref[...], xp_ref, y_ref, sum_ref,
        integral_weights(0.0, 0.5),
    )

    def emit(f, value):
        later = jnp.where(small, value, second_ref[field_rows(f), :])
        later_ref[field_rows(f), :] = later
        put_operand(xs_ref, f, later)

    unpack(sum_ref, pack_ref, emit)
    send_rims(xs_ref, halo_ref, (s0, s1, s2, s3))


def last_local_kernel(
    u_ref, middle_ref, first_ref, second_ref, later_ref, gfirst_ref, star_ref, plus_ref, minus_ref,
    update_ref, lift_ref, pick_ref, turn_ref, cluster_ref,
    base_ref, xs_ref, y_ref, table_ref, z_ref, g_ref,
):
    small = cluster_ref[...] == 0
    for f in range(FIELDS):
        put_operand(xs_ref, f, later_ref[field_rows(f), :])
    wide_dot(update_ref[3 * MODES :, :], xs_ref, y_ref)
    near = pick_faces(y_ref, 0, table_ref, pick_ref[...])
    large4 = jnp.concatenate([jnp.where(small, 0.0, 1.0)] * 4, axis=1)
    g_ref[...] = near + gfirst_ref[...] * large4
    for f in range(FIELDS):
        rows = field_rows(f)
        put_operand(
            xs_ref, f, jnp.where(small, later_ref[rows, :], first_ref[rows, :] + second_ref[rows, :])
        )
    wide_dot(update_ref[...], xs_ref, y_ref)
    finish_local(
        lambda f: middle_ref[field_rows(f), :],
        star_ref, plus_ref, minus_ref, lift_ref, turn_ref[...], y_ref, g_ref, z_ref, base_ref,
    )


def last_remote_kernel(
    r0, r1, r2, r3, base_ref, traces_ref, slot_flux_ref, scatter_ref, lift_ref, pair_ref, marks_ref,
    out_hbm, z_ref, done_ref, sems,
):
    large = marks_ref[LARGE_ROW : LARGE_ROW + 1, :]
    traces = slot_traces((r0, r1, r2, r3), pair_ref[...], marks_ref)
    for j in range(PAIRS):
        traces[j] = traces[j] + traces_ref[j * NPAD : (j + 1) * NPAD, :] * large
    copies = []

    def emit(f, lifted):
        rows = field_rows(f)
        done_ref[rows, :] = base_ref[rows, :] - lifted
        copy = pltpu.make_async_copy(done_ref.at[rows, :], out_hbm.at[rows, :], sems.at[f])
        copy.start()
        copies.append(copy)

    slot_lift(traces, slot_flux_ref, marks_ref, lift_ref, scatter_ref, z_ref, emit)
    for copy in copies:
        copy.wait()


STATE = (FIELDS * MODES, LANES)
GATHERED = (FIELDS * NPAD, 4 * LANES)


def call(kernel, inputs, outs, scratch, name, space=pltpu.VMEM, out_space=pltpu.VMEM):
    out_shape = [jax.ShapeDtypeStruct(shape, kind) for shape, kind in outs]
    return pl.pallas_call(
        kernel,
        out_shape=out_shape,
        in_specs=[pl.BlockSpec(memory_space=space)] * len(inputs),
        out_specs=[pl.BlockSpec(memory_space=out_space)] * len(out_shape),
        scratch_shapes=scratch,
        compiler_params=pltpu.CompilerParams(vmem_limit_bytes=24 << 20),
        cost_estimate=pl.CostEstimate(flops=10**9, bytes_accessed=10**6, transcendentals=0),
        name=name,
    )(*inputs)


def scratch_xs():
    return pltpu.VMEM((3 * MPAD, FIELDS * LANES), BF)


def scratch_y(rows):
    return pltpu.VMEM((rows, FIELDS * LANES), F32)


def scratch_slots():
    return pltpu.VMEM((2, 3 * FACES, PAIRS * LANES), BF)


def scratch_z(rows):
    return pltpu.VMEM((2, rows, FIELDS * LANES), BF)


def swap(x, axis, kind):
    count = lax.axis_size(axis)
    pairs = []
    for a in range(kind, count, 2):
        b = (a + 1) % count
        pairs += [(a, b), (b, a)]
    return lax.ppermute(x, axis, pairs)


def trade(sends):
    return [
        swap(send, axis, kind)
        for send, (axis, kind) in zip(sends, (("dom", 1), ("dom", 0), ("near", 1), ("near", 0)))
    ]


def on_device(
    u, star, plus, minus, stiffness, face_lift, face_project,
    cluster, part, slot, face, turn, halo,
):
    width = halo.shape[1]
    u = jnp.transpose(u, (1, 0, 2)).reshape(STATE)
    star, plus, minus = [jnp.transpose(x, (1, 2, 0, 3)) for x in (star, plus, minus)]
    face_lift = jnp.transpose(face_lift, (2, 0, 1))
    face_project = jnp.transpose(face_project, (1, 0, 2))
    state, gathered = (STATE, F32), (GATHERED, F32)
    rims = [((width, 5 * LANES), F32)] * 4
    update_rows = 3 * MODES + FACES
    inputs = (
        u, star, stiffness, halo, plus, minus, face_lift, face_project,
        part, slot, face, turn, cluster.reshape(1, LANES),
    )
    inputs = [pltpu.with_memory_space_constraint(x, pltpu.HBM) for x in inputs]
    *held, first, second, forward, s0, s1, s2, s3 = call(
        first_kernel, inputs,
        [(x.shape, x.dtype) for x in inputs]
        + [state, state, ((3 * MODES, 3 * MPAD), BF)] + rims,
        [
            scratch_xs(), scratch_y(3 * MODES), scratch_y(3 * MODES),
            pltpu.SemaphoreType.DMA((INPUTS,)),
        ], "first",
        pltpu.HBM,
    )
    u, star, stiffness, halo, plus, minus, face_lift, face_project = held[:8]
    part, slot, face, turn, cluster = held[8:]
    sends = s0, s1, s2, s3
    received = trade(sends)
    base, g, marks, update, lift, pair, pack, packed, slot_flux, scatter, pick, turned = call(
        middle_local_kernel,
        (u, first, star, plus, minus, stiffness, face_lift, face_project,
         part, slot, face, turn, cluster, halo),
        [
            state, gathered, ((KINDS, LANES), F32), ((update_rows, 3 * MPAD), BF),
            ((2 * MODES, 4 * FACES), BF), ((2 * FACES, 3 * LANES), BF),
            ((LANES, 2 * LANES), BF), ((PAIRS, 3 * DROWS, LANES), F32),
            ((PAIRS * DROWS, LANES), F32), ((LANES, 2 * LANES), BF), ((4 * LANES, 4 * LANES), BF),
            ((2 * LANES, LANES), BF),
        ],
        [
            scratch_xs(), scratch_y(update_rows), pltpu.VMEM(GATHERED, F32), scratch_z(4 * FACES),
            pltpu.VMEM((4 * FACES, LANES), F32),
        ],
        "middle_local",
    )
    middle, later, traces, *sends = call(
        middle_remote_kernel,
        (
            *received, u, base, second, packed, slot_flux, scatter, forward, lift, pair, marks,
            cluster, halo, pack, turned,
        ),
        [state, state, ((PAIRS * NPAD, LANES), F32)] + rims,
        [
            scratch_xs(), pltpu.VMEM((3 * MPAD, PAIRS * LANES), BF),
            pltpu.VMEM((3 * MODES, PAIRS * LANES), F32),
            pltpu.VMEM((PAIRS * MODES, LANES), F32),
            scratch_slots(),
        ],
        "middle_remote",
    )
    received = trade(sends)
    (base,) = call(
        last_local_kernel,
        (
            u, middle, first, second, later, g, star, plus, minus, update, lift,
            pick, turn, cluster,
        ),
        [state],
        [
            scratch_xs(), scratch_y(update_rows), pltpu.VMEM(GATHERED, F32), scratch_z(4 * FACES),
            pltpu.VMEM(GATHERED, F32),
        ],
        "last_local",
    )
    (out,) = call(
        last_remote_kernel,
        (*received, base, traces, slot_flux, scatter, lift, pair, marks),
        [state],
        [scratch_slots(), pltpu.VMEM(STATE, F32), pltpu.SemaphoreType.DMA((FIELDS,))],
        "last_remote", out_space=pltpu.HBM,
    )
    return jnp.transpose(out.reshape(FIELDS, MODES, LANES), (1, 0, 2))


def solution(mesh):
    both = ("dom", "near")
    in_specs = (
        P(None, None, both), P(None, None, None, both), P(None, None, None, both),
        P(None, None, None, both), P(), P(), P(), P(both),
        P(None, both), P(None, both), P(None, both), P(None, both), P(None, both),
    )
    return jax.shard_map(
        on_device, mesh=mesh, in_specs=in_specs, out_specs=P(None, None, both), check_vma=False
    )
```

```python
import functools
import math

import jax
import jax.numpy as jnp
import numpy as np
from jax import lax
from jax.experimental import pallas as pl
from jax.experimental.pallas import tpu as pltpu
from jax.sharding import PartitionSpec as P

MODES = 56
FIELDS = 9
NODES = 21
ORDER = 6
MPAD = 64
NPAD = 24
LANES = 128
FACES = 4 * NPAD
BF = jnp.bfloat16
F32 = jnp.float32


def rotations():
    degree = ORDER - 1
    nodes = [(a, b) for a in range(degree + 1) for b in range(degree + 1 - a)]
    lookup = {point: number for number, point in enumerate(nodes)}
    tables = []
    for rotation in range(3):
        row = []
        for a, b in nodes:
            triple = (a, b, degree - a - b)
            rolled = triple[rotation:] + triple[:rotation]
            row.append(lookup[rolled[0], rolled[1]])
        tables.append(row)
    return np.array(tables, dtype=np.int32)


def integral_weights(begin, end):
    return [(end ** (k + 1) - begin ** (k + 1)) / math.factorial(k + 1) for k in range(ORDER)]


def two_parts(x):
    high = x.astype(BF)
    low = (x - high.astype(F32)).astype(BF)
    return high, low


def float_parts(x):
    high = x.astype(BF).astype(F32)
    return high, x - high


def field_lanes(f):
    return slice(f * LANES, (f + 1) * LANES)


def field_rows(f):
    return slice(f * MODES, (f + 1) * MODES)


def put_operand(xs_ref, f, x):
    x = jnp.concatenate([x, jnp.zeros((MPAD - MODES, LANES), F32)], axis=0)
    high, low = two_parts(x)
    lanes = field_lanes(f)
    xs_ref[0:MPAD, lanes] = high
    xs_ref[MPAD : 2 * MPAD, lanes] = low
    xs_ref[2 * MPAD : 3 * MPAD, lanes] = high


def big_dot(lhs, rhs):
    return jnp.dot(lhs, rhs, preferred_element_type=F32)


def wide_dot(lhs, xs_ref, y_ref):
    rows = lhs.shape[0]
    for f in range(0, FIELDS, 2):
        lanes = slice(f * LANES, min(f + 2, FIELDS) * LANES)
        y_ref[0:rows, lanes] = big_dot(lhs, xs_ref[:, lanes])


def star_sum(y_ref, star_ref, emit):
    for first in range(0, FIELDS, 3):
        sums = [None] * 3
        for d in range(3):
            for f in range(FIELDS):
                y = y_ref[d * MODES : (d + 1) * MODES, field_lanes(f)]
                for k in range(3):
                    scale = star_ref[f, first + k, d : d + 1, :]
                    term = y * scale
                    sums[k] = term if sums[k] is None else sums[k] + term
        for k in range(3):
            emit(first + k, sums[k])


GROUP = 3


class Steps:
    def __init__(self, halo_ref):
        self.value = halo_ref[0, 0]
        self.bound = 4096

    def __call__(self, body):
        self.bound += 1
        pl.when(self.value < self.bound)(body)


def star_group(y_ref, star_ref, first, emit, order):
    sums = [None] * GROUP
    for f in order:
        for d in range(3):
            y = y_ref[d * MODES : (d + 1) * MODES, field_lanes(f)]
            for k in range(GROUP):
                term = y * star_ref[f, first + k, d : d + 1, :]
                sums[k] = term if sums[k] is None else sums[k] + term
    for k in range(GROUP):
        emit(first + k, sums[k])


def taylor(block, start_of, star_ref, forward_ref, xs_ref, ys, integrals, star_ready):
    def start():
        for f in range(FIELDS):
            value = start_of(f)
            put_operand(xs_ref, f, value)
            for ref, weights in integrals:
                ref[field_rows(f), :] = weights[0] * value

    def step(k, n):
        y_ref = ys[k % 2]

        def emit(g, value):
            if k < ORDER - 1:
                put_operand(xs_ref, g, value)
            for ref, weights in integrals:
                ref[field_rows(g), :] = ref[field_rows(g), :] + weights[k] * value

        if n == 0:
            wide_dot(forward_ref[...], xs_ref, y_ref)
        star_group(y_ref, star_ref, n * GROUP, emit, range(FIELDS))

    block(start)
    star_ready()
    block(functools.partial(step, 1, 0))
    for k in range(1, ORDER):

        def rest(k=k):
            step(k, 1)
            step(k, 2)
            if k < ORDER - 1:
                step(k + 1, 0)

        block(rest)


PAIRS = (FIELDS + 1) // 2
DROWS = 16


def nt_dot(lhs, rhs):
    return lax.dot_general(lhs, rhs, (((1,), (1,)), ((), ())), preferred_element_type=F32)


def pair_lanes(j):
    return slice(2 * j * LANES, min(2 * j + 2, FIELDS) * LANES)


def pack_matrix(cluster):
    small = jnp.where(cluster == 0, 1.0, 0.0)
    before = lax.broadcasted_iota(jnp.int32, (LANES, LANES), 0)
    after = lax.broadcasted_iota(jnp.int32, (LANES, LANES), 1)
    upper = jnp.where(before < after, 1.0, 0.0).astype(BF)
    place = big_dot(jnp.broadcast_to(small, (8, LANES)).astype(BF), upper)[0:1, :]
    place = jnp.where(cluster == 0, place, -1.0).astype(jnp.int32)
    row = lax.broadcasted_iota(jnp.int32, (MPAD, LANES), 0)
    pick = jnp.where(row == place, 1.0, 0.0)
    none = jnp.zeros_like(pick)
    return jnp.concatenate(
        [jnp.concatenate([pick, none], axis=1), jnp.concatenate([none, pick], axis=1)], axis=0
    )


def pack_star(star_ref, pack_ref, packed_ref):
    pad = jnp.zeros((DROWS - FIELDS, LANES), F32)
    rows = []
    for f in range(FIELDS):
        parts = []
        for d in range(3):
            parts += [star_ref[f, :, d, :], pad]
        rows.append(jnp.concatenate(parts, axis=0))
    for j in range(PAIRS):
        both = jnp.concatenate(rows[2 * j : 2 * j + 2], axis=1)
        pick = pack_ref[:, 0 : both.shape[1]]
        high, low = two_parts(both)
        packed_ref[j] = nt_dot(high, pick) + nt_dot(low, pick)


def packed_taylor(xs_ref, turned_ref, star_ref, forward, xp_ref, y_ref, sum_ref, weights):
    for j in range(PAIRS):
        lanes = pair_lanes(j)
        pick = turned_ref[0 : lanes.stop - lanes.start, :]
        value = big_dot(xs_ref[0:MPAD, lanes], pick) + big_dot(xs_ref[MPAD : 2 * MPAD, lanes], pick)
        value = value[0:MODES]
        put_operand(xp_ref, j, value)
        sum_ref[field_rows(j), :] = weights[0] * value
    for k in range(1, ORDER):
        for j in range(0, PAIRS, 2):
            lanes = slice(j * LANES, min(j + 2, PAIRS) * LANES)
            y_ref[:, lanes] = big_dot(forward, xp_ref[:, lanes])
        for j in range(PAIRS):
            sums = []
            for g in range(2 * j, min(2 * j + 2, FIELDS)):
                total = None
                for i in range(PAIRS):
                    for d in range(3):
                        y = y_ref[d * MODES : (d + 1) * MODES, field_lanes(i)]
                        term = y * star_ref[i, d * DROWS + g : d * DROWS + g + 1, :]
                        total = term if total is None else total + term
                sums.append(total)
            if len(sums) == 1:
                sums.append(jnp.zeros_like(sums[0]))
            value = join_halves(*sums)
            if k < ORDER - 1:
                put_operand(xp_ref, j, value)
            sum_ref[field_rows(j), :] = sum_ref[field_rows(j), :] + weights[k] * value


def unpack(sum_ref, pack_ref, emit):
    for j in range(PAIRS):
        high, low = two_parts(sum_ref[field_rows(j), :])
        pick = pack_ref[:, 0 : min(2, FIELDS - 2 * j) * LANES]
        value = big_dot(high, pick) + big_dot(low, pick)
        for n in range(min(2, FIELDS - 2 * j)):
            emit(2 * j + n, value[:, field_lanes(n)])


def evens():
    return [lax.rem(lax.axis_index(axis), 2) == 0 for axis in ("near", "dom")]


def send_rims(xs_ref, halo_ref, sends):
    width = halo_ref.shape[1]
    element = lax.broadcasted_iota(jnp.int32, (LANES, width), 0)
    near_even, dom_even = evens()
    picks = []
    for even, first in ((dom_even, 2), (near_even, 0)):
        up, down = halo_ref[first : first + 1, :], halo_ref[first + 1 : first + 2, :]
        for row in (jnp.where(even, down, up), jnp.where(even, up, down)):
            pick = jnp.where(element == row, 1.0, 0.0).astype(F32)
            picks.append(jnp.transpose(pick))
    pick = jnp.concatenate(picks, axis=0).astype(BF)
    for q in range((FIELDS + 1) // 2):
        fields = (2 * q, min(2 * q + 1, FIELDS - 1))
        total = None
        for piece in range(2):
            rows = slice(piece * MPAD, (piece + 1) * MPAD)
            both = jnp.concatenate([xs_ref[rows, field_lanes(f)] for f in fields], axis=0)
            part = lax.dot_general(
                pick, both, (((1,), (1,)), ((), ())), preferred_element_type=F32
            )
            total = part if total is None else total + part
        for r in range(4):
            sends[r][:, field_lanes(q)] = total[r * width : (r + 1) * width, :]


def local_pick(part, slot, face):
    target = jnp.where(part == 0, face * LANES + slot, -1)
    target = jnp.concatenate([target[i : i + 1, :] for i in range(4)], axis=1)
    row = lax.broadcasted_iota(jnp.int32, (4 * LANES, 4 * LANES), 0)
    return jnp.where(row == target, 1.0, 0.0).astype(BF)


def remote_pick(part, slot, width):
    near_even, dom_even = evens()
    near_block = jnp.where(near_even, part + 1, 4 - part)
    dom_block = jnp.where(dom_even, part - 3, 4 - part)
    block = jnp.where(part > 2, dom_block, near_block)
    target = jnp.where(part > 0, block * width + slot, -1)
    target = jnp.concatenate([target[i : i + 1, :] for i in range(4)], axis=1)
    row = lax.broadcasted_iota(jnp.int32, (4 * width, 4 * LANES), 0)
    return jnp.where(row == target, 1.0, 0.0).astype(BF)


def pick_faces(y_ref, base_row, table_ref, pick):
    for f in range(FIELDS):
        for j in range(4):
            table_ref[f * NPAD : (f + 1) * NPAD, j * LANES : (j + 1) * LANES] = y_ref[
                base_row + j * NPAD : base_row + (j + 1) * NPAD, field_lanes(f)
            ]
    high, low = two_parts(table_ref[...])
    return big_dot(high, pick) + big_dot(low, pick)


def flux_sum(values_of, flux_ref, emit):
    for first in range(0, FIELDS, 3):
        sums = [[None] * 4 for _ in range(3)]
        for i in range(4):
            for f in range(FIELDS):
                value = values_of(i, f)
                for k in range(3):
                    term = value * flux_ref[f, first + k, i : i + 1, :]
                    old = sums[k][i]
                    sums[k][i] = term if old is None else old + term
        for k in range(3):
            emit(first + k, jnp.concatenate(sums[k], axis=0))


def turn_masks(turn):
    masks = []
    for h in range(3):
        rows = [
            jnp.broadcast_to(jnp.where(turn[i : i + 1, :] == h, 1.0, 0.0), (NPAD, LANES))
            for i in range(4)
        ]
        masks.append(jnp.concatenate(rows, axis=0).astype(BF))
    return masks


def stack_own(z_ref, g, value):
    lanes = field_lanes(g)
    for piece, part in enumerate(two_parts(value)):
        z_ref[piece, 3 * FACES : 4 * FACES, lanes] = part


def stack_turned(z_ref, g, value, masks):
    lanes = field_lanes(g)
    for piece, part in enumerate(two_parts(value)):
        for h in range(3):
            z_ref[piece, h * FACES : (h + 1) * FACES, lanes] = part * masks[h]


def subtract_lift(lift_ref, rows, z_ref, base_ref, out_ref):
    both = lift_ref[:, 0:rows]
    for f in range(0, FIELDS, 2):
        fields = range(f, min(f + 2, FIELDS))
        lanes = slice(f * LANES, (fields[-1] + 1) * LANES)
        high = big_dot(both, z_ref[0, 0:rows, lanes])
        lifted = high[0:MODES] + high[MODES:] + big_dot(both[0:MODES], z_ref[1, 0:rows, lanes])
        for n, g in enumerate(fields):
            out_ref[field_rows(g), :] = base_ref[field_rows(g), :] - lifted[:, field_lanes(n)]


KINDS = 32
LARGE_ROW = 16


def slot_tables(far, part, face, turn, cluster, minus_ref, marks_ref, slot_flux_ref, scatter_ref):
    far2 = jnp.concatenate([far, far], axis=0)
    rows = [jnp.where(face == j, 1.0, 0.0) for j in range(4)]
    rows = [jnp.concatenate([row[i : i + 1, :] for i in range(4)], axis=1) for row in rows]
    none = jnp.zeros((1, LANES), F32)
    for h in range(3):
        turned = jnp.where(turn == h, 1.0, 0.0)
        for i in range(4):
            pieces = [none] * 4
            pieces[i] = turned[i : i + 1, :]
            rows.append(jnp.concatenate(pieces, axis=1))
    rows.append(jnp.concatenate([jnp.where(cluster == 0, 0.0, 1.0)] * 4, axis=1))
    kinds = tall(jnp.concatenate(rows, axis=0), KINDS).astype(BF)
    marks_ref[...] = nt_dot(kinds, far2)
    tiles = []
    for f in range(2 * PAIRS):
        if f < FIELDS:
            row = jnp.concatenate([minus_ref[f, :, i, :] for i in range(4)], axis=1)
            tiles.append(tall(row, DROWS))
        else:
            tiles.append(jnp.zeros((DROWS, 4 * LANES), F32))
    flux = jnp.concatenate(
        [jnp.concatenate(tiles[2 * j : 2 * j + 2], axis=1) for j in range(PAIRS)], axis=0
    )
    none = jnp.zeros_like(far)
    pick = jnp.concatenate(
        [jnp.concatenate([far, none], axis=1), jnp.concatenate([none, far], axis=1)], axis=0
    )
    high, low = two_parts(flux)
    slot_flux_ref[...] = nt_dot(high, pick) + nt_dot(low, pick)
    place = far[:, 0:LANES] + far[:, LANES : 2 * LANES]
    place = place + far[:, 2 * LANES : 3 * LANES] + far[:, 3 * LANES :]
    none = jnp.zeros_like(place)
    scatter_ref[...] = jnp.concatenate(
        [jnp.concatenate([place, none], axis=1), jnp.concatenate([none, place], axis=1)], axis=0
    )


def low_half(rows):
    return lax.broadcasted_iota(jnp.int32, (rows, LANES), 1) < MPAD


def slot_traces(received, pair_matrix, marks_ref):
    rims = jnp.concatenate([ref[...] for ref in received], axis=0)
    rims = jnp.concatenate([rims, rims], axis=0)
    rhs = []
    for q in range(PAIRS):
        high, low = two_parts(jnp.transpose(rims[:, field_lanes(q)]))
        rhs.append(jnp.concatenate([high, low, high], axis=0))
    traces = []
    for q in range(0, PAIRS, 2):
        out = big_dot(pair_matrix, jnp.concatenate(rhs[q : q + 2], axis=1))
        for n in range(min(2, PAIRS - q)):
            tile = out[:, field_lanes(n)]
            both = jnp.where(low_half(FACES), tile[0:FACES], tile[FACES:])
            total = None
            for j in range(4):
                term = both[j * NPAD : (j + 1) * NPAD, :] * marks_ref[j : j + 1, :]
                total = term if total is None else total + term
            traces.append(total)
    return traces


def join_halves(first, second):
    low = low_half(first.shape[0])
    same = jnp.where(low, first, second)
    other = jnp.where(low, second, first)
    return same + pltpu.roll(other, MPAD, 1)


def slot_lift(traces, slot_flux_ref, marks_ref, lift_ref, scatter_ref, z_ref, emit):
    masks = []
    for n in range(0, 12, 2):
        rows = [
            jnp.broadcast_to(marks_ref[4 + n + i : 5 + n + i, :], (NPAD, LANES)) for i in range(2)
        ]
        masks.append(jnp.concatenate(rows, axis=0).astype(BF))
    for j in range(PAIRS):
        sums = []
        for g in range(2 * j, 2 * j + 2):
            total = None
            if g < FIELDS:
                for i in range(PAIRS):
                    row = i * DROWS + g
                    term = traces[i] * slot_flux_ref[row : row + 1, :]
                    total = term if total is None else total + term
            else:
                total = jnp.zeros_like(traces[0])
            sums.append(total)
        value = join_halves(*sums)
        for piece, part in enumerate(two_parts(jnp.concatenate([value, value], axis=0))):
            for n in range(6):
                z_ref[piece, 2 * n * NPAD : 2 * (n + 1) * NPAD, field_lanes(j)] = part * masks[n]
    both = lift_ref[:, 0 : 3 * FACES]
    for j in range(0, PAIRS, 2):
        tiles = range(j, min(j + 2, PAIRS))
        lanes = slice(j * LANES, (tiles[-1] + 1) * LANES)
        high = big_dot(both, z_ref[0, :, lanes])
        lifted = high[0:MODES] + high[MODES:] + big_dot(both[0:MODES], z_ref[1, :, lanes])
        for n, tile in enumerate(tiles):
            high, low = two_parts(lifted[:, field_lanes(n)])
            count = min(2, FIELDS - 2 * tile)
            pick = scatter_ref[:, 0 : count * LANES]
            value = big_dot(high, pick) + big_dot(low, pick)
            for k in range(count):
                emit(2 * tile + k, value[:, field_lanes(k)])


def wide(x):
    return jnp.concatenate([x, jnp.zeros((x.shape[0], LANES - x.shape[1]), F32)], axis=1)


def tall(x, rows):
    return jnp.concatenate([x, jnp.zeros((rows - x.shape[0], x.shape[1]), F32)], axis=0)


def tripled(x):
    high, low = float_parts(x)
    first = high + pltpu.roll(high, MPAD, 1)
    return jnp.concatenate([first, low], axis=1).astype(BF)[:, 0 : 3 * MPAD]


def forward_matrix(stiff_ref):
    return tripled(jnp.concatenate([wide(stiff_ref[d]) for d in range(3)], axis=0))


def prepare(stiff_ref, lift_ref, project_ref, update_ref, lifts_ref, pair_ref, rows_ref):
    backward = [
        jnp.transpose(tall(wide(stiff_ref[d]), LANES))[0:MODES, :] for d in range(3)
    ]
    project = jnp.concatenate(
        [wide(tall(project_ref[:, j, :], NPAD)) for j in range(4)], axis=0
    )
    update_ref[...] = tripled(jnp.concatenate(backward + [project], axis=0))
    high, low = float_parts(project)
    moved = [pltpu.roll(part, MPAD, 1) for part in (high, low)]
    highs = jnp.concatenate([high, moved[0]], axis=0).astype(BF)
    lows = jnp.concatenate([low, moved[1]], axis=0).astype(BF)
    pair_ref[...] = jnp.concatenate([highs, highs, lows], axis=1)
    rows_ref[...] = jnp.zeros(rows_ref.shape, F32)
    tables = rotations()
    for block, h in enumerate((0, 1, 2, 0)):
        for i in range(4):
            for p in range(NODES):
                row = block * FACES + i * NPAD + int(tables[h][p])
                rows_ref[row : row + 1, 0:MODES] = lift_ref[p, i : i + 1, :]
    columns = []
    for t in range(4 * FACES // LANES):
        columns.append(jnp.transpose(rows_ref[t * LANES : (t + 1) * LANES, :])[0:MODES, :])
    high, low = float_parts(jnp.concatenate(columns, axis=1))
    lifts_ref[...] = jnp.concatenate([high, low], axis=0).astype(BF)


INPUTS = 13


def first_kernel(*refs):
    sources, rest = refs[:INPUTS], refs[INPUTS:]
    held, rest = rest[:INPUTS], rest[INPUTS:]
    first_ref, second_ref, forward_ref, s0, s1, s2, s3, xs_ref, y_ref, y2_ref, sems = rest
    copies = [
        pltpu.make_async_copy(source, target, sems.at[n])
        for n, (source, target) in enumerate(zip(sources, held))
    ]
    for n in (0, 2, 3, 1, *range(4, INPUTS)):
        copies[n].start()
    u_ref, star_ref, stiff_ref, halo_ref = held[:4]
    for n in (0, 2, 3):
        copies[n].wait()
    forward_ref[...] = forward_matrix(stiff_ref)
    taylor(
        Steps(halo_ref), lambda f: u_ref[field_rows(f), :], star_ref, forward_ref, xs_ref, (y_ref, y2_ref),
        [(first_ref, integral_weights(0.0, 0.5)), (second_ref, integral_weights(0.5, 1.0))],
        copies[1].wait,
    )
    for copy in copies[4:]:
        copy.wait()
    for f in range(FIELDS):
        put_operand(xs_ref, f, first_ref[field_rows(f), :])
    send_rims(xs_ref, halo_ref, (s0, s1, s2, s3))


def middle_local_kernel(
    u_ref, first_ref, star_ref, plus_ref, minus_ref, stiff_ref, face_lift_ref, project_ref,
    part_ref, slot_ref, face_ref, turn_ref, cluster_ref, halo_ref,
    base_ref, g_ref, marks_ref, update_ref, lift_ref, pair_ref, pack_ref, packed_ref,
    slot_flux_ref, scatter_ref, pick_ref, turned_ref,
    xs_ref, y_ref, table_ref, z_ref, rows_ref,
):
    width = halo_ref.shape[1]
    prepare(stiff_ref, face_lift_ref, project_ref, update_ref, lift_ref, pair_ref, rows_ref)
    pack = pack_matrix(cluster_ref[...])
    pack_ref[...] = pack.astype(BF)
    turned_ref[...] = jnp.concatenate(
        [jnp.transpose(pack[:, 0:LANES]), jnp.transpose(pack[:, LANES:])], axis=0
    ).astype(BF)
    pack_star(star_ref, pack_ref, packed_ref)
    part, slot, face = part_ref[...], slot_ref[...], face_ref[...]
    for f in range(FIELDS):
        put_operand(xs_ref, f, first_ref[field_rows(f), :])
    wide_dot(update_ref[...], xs_ref, y_ref)
    pick_ref[...] = local_pick(part, slot, face)
    g_ref[...] = pick_faces(y_ref, 3 * MODES, table_ref, pick_ref[...])
    slot_tables(
        remote_pick(part, slot, width), part, face, turn_ref[...], cluster_ref[...], minus_ref,
        marks_ref, slot_flux_ref, scatter_ref,
    )
    finish_local(
        lambda f: u_ref[field_rows(f), :], star_ref, plus_ref, minus_ref, lift_ref,
        turn_ref[...], y_ref, g_ref, z_ref, base_ref,
    )


def finish_local(base_of, star_ref, plus_ref, minus_ref, lift_ref, turn, y_ref, g_ref, z_ref, base_ref):
    masks = turn_masks(turn)
    top = 3 * MODES
    flux_sum(
        lambda i, f: y_ref[top + i * NPAD : top + (i + 1) * NPAD, field_lanes(f)],
        plus_ref,
        lambda g, value: stack_own(z_ref, g, value),
    )
    flux_sum(
        lambda i, f: g_ref[f * NPAD : (f + 1) * NPAD, i * LANES : (i + 1) * LANES],
        minus_ref,
        lambda g, value: stack_turned(z_ref, g, value, masks),
    )

    def emit(g, value):
        base_ref[field_rows(g), :] = base_of(g) + value

    star_sum(y_ref, star_ref, emit)
    subtract_lift(lift_ref, 4 * FACES, z_ref, base_ref, base_ref)


def middle_remote_kernel(
    r0, r1, r2, r3, u_ref, base_ref, second_ref, star_ref, slot_flux_ref, scatter_ref,
    forward_ref, lift_ref, pair_ref, marks_ref, cluster_ref, halo_ref, pack_ref, turned_ref,
    middle_ref, later_ref, traces_ref, s0, s1, s2, s3,
    xs_ref, xp_ref, y_ref, sum_ref, z_ref,
):
    small = cluster_ref[...] == 0
    traces = slot_traces((r0, r1, r2, r3), pair_ref[...], marks_ref)
    traces_ref[...] = jnp.concatenate(traces, axis=0)

    def take(f, lifted):
        value = base_ref[field_rows(f), :] - lifted
        value = jnp.where(small, value, u_ref[field_rows(f), :])
        middle_ref[field_rows(f), :] = value
        put_operand(xs_ref, f, value)

    slot_lift(traces, slot_flux_ref, marks_ref, lift_ref, scatter_ref, z_ref, take)
    packed_taylor(
        xs_ref, turned_ref, star_ref, forward_ref[...], xp_ref, y_ref, sum_ref,
        integral_weights(0.0, 0.5),
    )

    def emit(f, value):
        later = jnp.where(small, value, second_ref[field_rows(f), :])
        later_ref[field_rows(f), :] = later
        put_operand(xs_ref, f, later)

    unpack(sum_ref, pack_ref, emit)
    send_rims(xs_ref, halo_ref, (s0, s1, s2, s3))


def last_local_kernel(
    u_ref, middle_ref, first_ref, second_ref, later_ref, gfirst_ref, star_ref, plus_ref, minus_ref,
    update_ref, lift_ref, pick_ref, turn_ref, cluster_ref,
    base_ref, xs_ref, y_ref, table_ref, z_ref, g_ref,
):
    small = cluster_ref[...] == 0
    for f in range(FIELDS):
        put_operand(xs_ref, f, later_ref[field_rows(f), :])
    wide_dot(update_ref[3 * MODES :, :], xs_ref, y_ref)
    near = pick_faces(y_ref, 0, table_ref, pick_ref[...])
    large4 = jnp.concatenate([jnp.where(small, 0.0, 1.0)] * 4, axis=1)
    g_ref[...] = near + gfirst_ref[...] * large4
    for f in range(FIELDS):
        rows = field_rows(f)
        put_operand(
            xs_ref, f, jnp.where(small, later_ref[rows, :], first_ref[rows, :] + second_ref[rows, :])
        )
    wide_dot(update_ref[...], xs_ref, y_ref)
    finish_local(
        lambda f: middle_ref[field_rows(f), :],
        star_ref, plus_ref, minus_ref, lift_ref, turn_ref[...], y_ref, g_ref, z_ref, base_ref,
    )


def last_remote_kernel(
    r0, r1, r2, r3, base_ref, traces_ref, slot_flux_ref, scatter_ref, lift_ref, pair_ref, marks_ref,
    out_ref, z_ref,
):
    large = marks_ref[LARGE_ROW : LARGE_ROW + 1, :]
    traces = slot_traces((r0, r1, r2, r3), pair_ref[...], marks_ref)
    for j in range(PAIRS):
        traces[j] = traces[j] + traces_ref[j * NPAD : (j + 1) * NPAD, :] * large

    def emit(f, lifted):
        rows = field_rows(f)
        out_ref[rows, :] = base_ref[rows, :] - lifted

    slot_lift(traces, slot_flux_ref, marks_ref, lift_ref, scatter_ref, z_ref, emit)


STATE = (FIELDS * MODES, LANES)
GATHERED = (FIELDS * NPAD, 4 * LANES)


def call(kernel, inputs, outs, scratch, name, space=pltpu.VMEM, out_space=pltpu.VMEM):
    out_shape = [jax.ShapeDtypeStruct(shape, kind) for shape, kind in outs]
    return pl.pallas_call(
        kernel,
        out_shape=out_shape,
        in_specs=[pl.BlockSpec(memory_space=space)] * len(inputs),
        out_specs=[pl.BlockSpec(memory_space=out_space)] * len(out_shape),
        scratch_shapes=scratch,
        compiler_params=pltpu.CompilerParams(vmem_limit_bytes=24 << 20),
        cost_estimate=pl.CostEstimate(flops=10**9, bytes_accessed=10**6, transcendentals=0),
        name=name,
    )(*inputs)


def scratch_xs():
    return pltpu.VMEM((3 * MPAD, FIELDS * LANES), BF)


def scratch_y(rows):
    return pltpu.VMEM((rows, FIELDS * LANES), F32)


def scratch_slots():
    return pltpu.VMEM((2, 3 * FACES, PAIRS * LANES), BF)


def scratch_z(rows):
    return pltpu.VMEM((2, rows, FIELDS * LANES), BF)


def swap(x, axis, kind):
    count = lax.axis_size(axis)
    pairs = []
    for a in range(kind, count, 2):
        b = (a + 1) % count
        pairs += [(a, b), (b, a)]
    return lax.ppermute(x, axis, pairs)


def trade(sends):
    return [
        swap(send, axis, kind)
        for send, (axis, kind) in zip(sends, (("dom", 1), ("dom", 0), ("near", 1), ("near", 0)))
    ]


def on_device(
    u, star, plus, minus, stiffness, face_lift, face_project,
    cluster, part, slot, face, turn, halo,
):
    width = halo.shape[1]
    u = jnp.transpose(u, (1, 0, 2)).reshape(STATE)
    star, plus, minus = [jnp.transpose(x, (1, 2, 0, 3)) for x in (star, plus, minus)]
    face_lift = jnp.transpose(face_lift, (2, 0, 1))
    face_project = jnp.transpose(face_project, (1, 0, 2))
    state, gathered = (STATE, F32), (GATHERED, F32)
    rims = [((width, 5 * LANES), F32)] * 4
    update_rows = 3 * MODES + FACES
    inputs = (
        u, star, stiffness, halo, plus, minus, face_lift, face_project,
        part, slot, face, turn, cluster.reshape(1, LANES),
    )
    inputs = [pltpu.with_memory_space_constraint(x, pltpu.HBM) for x in inputs]
    *held, first, second, forward, s0, s1, s2, s3 = call(
        first_kernel, inputs,
        [(x.shape, x.dtype) for x in inputs]
        + [state, state, ((3 * MODES, 3 * MPAD), BF)] + rims,
        [
            scratch_xs(), scratch_y(3 * MODES), scratch_y(3 * MODES),
            pltpu.SemaphoreType.DMA((INPUTS,)),
        ], "first",
        pltpu.HBM,
    )
    u, star, stiffness, halo, plus, minus, face_lift, face_project = held[:8]
    part, slot, face, turn, cluster = held[8:]
    sends = s0, s1, s2, s3
    received = trade(sends)
    base, g, marks, update, lift, pair, pack, packed, slot_flux, scatter, pick, turned = call(
        middle_local_kernel,
        (u, first, star, plus, minus, stiffness, face_lift, face_project,
         part, slot, face, turn, cluster, halo),
        [
            state, gathered, ((KINDS, LANES), F32), ((update_rows, 3 * MPAD), BF),
            ((2 * MODES, 4 * FACES), BF), ((2 * FACES, 3 * LANES), BF),
            ((LANES, 2 * LANES), BF), ((PAIRS, 3 * DROWS, LANES), F32),
            ((PAIRS * DROWS, LANES), F32), ((LANES, 2 * LANES), BF), ((4 * LANES, 4 * LANES), BF),
            ((2 * LANES, LANES), BF),
        ],
        [
            scratch_xs(), scratch_y(update_rows), pltpu.VMEM(GATHERED, F32), scratch_z(4 * FACES),
            pltpu.VMEM((4 * FACES, LANES), F32),
        ],
        "middle_local",
    )
    middle, later, traces, *sends = call(
        middle_remote_kernel,
        (
            *received, u, base, second, packed, slot_flux, scatter, forward, lift, pair, marks,
            cluster, halo, pack, turned,
        ),
        [state, state, ((PAIRS * NPAD, LANES), F32)] + rims,
        [
            scratch_xs(), pltpu.VMEM((3 * MPAD, PAIRS * LANES), BF),
            pltpu.VMEM((3 * MODES, PAIRS * LANES), F32),
            pltpu.VMEM((PAIRS * MODES, LANES), F32),
            scratch_slots(),
        ],
        "middle_remote",
    )
    received = trade(sends)
    (base,) = call(
        last_local_kernel,
        (
            u, middle, first, second, later, g, star, plus, minus, update, lift,
            pick, turn, cluster,
        ),
        [state],
        [
            scratch_xs(), scratch_y(update_rows), pltpu.VMEM(GATHERED, F32), scratch_z(4 * FACES),
            pltpu.VMEM(GATHERED, F32),
        ],
        "last_local",
    )
    (out,) = call(
        last_remote_kernel,
        (*received, base, traces, slot_flux, scatter, lift, pair, marks),
        [state],
        [scratch_slots()],
        "last_remote",
    )
    return jnp.transpose(out.reshape(FIELDS, MODES, LANES), (1, 0, 2))


def solution(mesh):
    both = ("dom", "near")
    in_specs = (
        P(None, None, both), P(None, None, None, both), P(None, None, None, both),
        P(None, None, None, both), P(), P(), P(), P(both),
        P(None, both), P(None, both), P(None, both), P(None, both), P(None, both),
    )
    return jax.shard_map(
        on_device, mesh=mesh, in_specs=in_specs, out_specs=P(None, None, both), check_vma=False
    )
```
